128 devices in a mesh: grp: 4 (over z), tok: 32 (over y, x, core).
Axes of the slice: x: 4, y: 4, z: 4, core: 2. Of those that a mesh axis runs over, the one named last changes fastest.
Arguments:
- tokens: bfloat16 [32768, 1408], P(('grp', 'tok')), may hold values from -6 to 6
- seg_ids: int32 [32768], P(('grp', 'tok')), may hold values from 0 to 8191, as said below
- merge_index: int32 [32768], P(('grp', 'tok')), may hold values from 0 to 255, as said below
- owners: int32 [8192, 1], P(('grp', 'tok')), may hold values from 0 to 31; in each aligned block of 64 rows (0 to 63, 64 to 127, ...) at most 4 rows name the same one
- w_qkv: bfloat16 [1408, 2112], replicated, may hold values from -0.15625 to 0.15625
- w_attn_out: bfloat16 [704, 1408], replicated, may hold values from -1.75 to 1.75
- w_in: bfloat16 [6144, 1408], P('grp'), may hold values from -0.15625 to 0.15625
- in_bias: bfloat16 [6144], P('grp'), may hold values from -3 to 3
- w_out: bfloat16 [6144, 1408], P('grp'), may hold values from -0.078125 to 0.078125
- out_bias: float32 [1408], replicated, may hold values from -3 to 3
- merge_gain: float32 [1408], replicated, may hold values from 0.1 to 1.9
- w_merge: bfloat16 [5632, 2048], P(None, 'grp'), may hold values from -0.078125 to 0.078125
- merge_bias: float32 [2048], P('grp'), may hold values from -3 to 3
Outputs:
- embeds: bfloat16 [16384, 2048], P('tok', 'grp')
The draws below stay inside these ranges and needn't reach their ends.
Inputs may be any that keep to these rules, and one draw needn't show every extreme that they name: `seg_ids`: never falling along the tokens; every segment starts at a multiple of 4 tokens, has a multiple of 4 tokens and lies within one aligned block of 8192 tokens. `merge_index`: in each aligned block of 256 entries the values are a permutation of 0 to 255, and each aligned group of 4 entries names rows of a single segment. `owners`: among the 64 merged tokens of one device no owner is named more than 4 times.
All inputs are finite; a program needn't handle non-finite values.
Results may differ from the reference program's by a relative error of at most 0.014.
Values may be sent and summed in bfloat16 or wider, within the bound.
No kernel may reach another device: no remote copies, remote signals or barrier semaphores. Data moves between devices by JAX's collectives and lax.ppermute only.
A program may use at most 320 MiB of HBM per device.

```python
import math
import jax
import jax.numpy as jnp
import numpy as np
from jax import lax

D = 1408
HEADS = 8
HD = 88
FF = 6144
OUT = 2048
TOK_DEV = 256
GROUP_TOK = 8192
TOKENS = 32768
MG = 64
MERGED = 8192
FF_DEV = 1536
CAP = 4
ROWS_OWNER = 512
N_TOK = 32


def segment_units(key):
    unit_count = TOKENS // 4
    group_units = GROUP_TOK // 4
    unit_pos = jnp.arange(unit_count, dtype=jnp.int32)
    cut_flags = jax.random.randint(jax.random.fold_in(key, 7), (unit_count,), 0, group_units) < 2
    group_first = unit_pos % group_units == 0
    boundary = cut_flags | group_first | (unit_pos == 1)
    starts = jnp.where(boundary, unit_pos, unit_count).astype(jnp.int32)
    shifted = jnp.concatenate([starts[1:], jnp.full((1,), unit_count, jnp.int32)])
    next_start = lax.cummin(shifted, axis=0, reverse=True)
    return (next_start - 1).astype(jnp.int32)


def draw_seg_ids(key, part):
    return jnp.repeat(segment_units(key), 4).astype(jnp.int32)


def draw_merge_index(key, part):
    device_count = TOKENS // TOK_DEV
    segments = jnp.repeat(segment_units(key), 4).astype(jnp.int32).reshape(device_count, TOK_DEV)
    local_seg = segments - segments[:, :1]
    jitter = jax.random.randint(jax.random.fold_in(key, 13), (device_count, TOK_DEV), 0, TOK_DEV)
    position = jnp.arange(TOK_DEV, dtype=jnp.int32)[None, :]
    ordering = (local_seg * TOK_DEV + jitter) * TOK_DEV + position
    return jnp.argsort(ordering, axis=1, stable=True).astype(jnp.int32).reshape(TOKENS)


def level_of(key, dims, cuts, smallest, high):
    gain, own = 1.0, jax.random.fold_in(key, 6)
    for dim, shards_of in cuts:
        steps = jnp.exp(jax.random.uniform(jax.random.fold_in(own, dim), (shards_of,), jnp.float32, smallest / len(cuts), high / len(cuts)))
        gain = gain * jnp.repeat(steps, dims[dim] // shards_of).reshape([-1 if axis == dim else 1 for axis in range(len(dims))])
    return gain


def assign_block(own_key, own, number, rows, amount, top, most, slope):
    ranking = jax.random.permutation(own_key, amount)
    packed, ordinary = load_shares(amount, rows * top, most, slope, True), load_shares(amount, rows * top, most, slope, False)
    places = jnp.arange(amount)

    def named(lengths, rotation):
        used = int((lengths > 0).sum())
        fixed = max(1, used // 4)
        moved = fixed + (places - fixed + rotation * (used - fixed)) % max(1, amount - fixed)
        return jnp.zeros((amount,), jnp.int32).at[ranking[jnp.where(places < fixed, places, moved)]].set(jnp.asarray(lengths, jnp.int32))

    lengths = jnp.where(number % 4 == 0, named(packed, number // 4), named(ordinary, number - number // 4 - 1))
    mixed = jax.random.permutation(jax.random.fold_in(own, 3), amount)
    giver, sink = mixed[0:amount // 2 * 2:2], mixed[1:amount // 2 * 2:2]
    slack = jnp.minimum(lengths[giver] - 1, most - lengths[sink]) // 2
    slack = jnp.where((giver == ranking[0]) | (sink == ranking[0]) | (lengths[sink] == 0), 0, jnp.maximum(slack, 0))
    moved = jax.random.randint(jax.random.fold_in(own, 4), (amount // 2,), 0, 1 << 20) % (slack + 1)
    lengths = lengths.at[giver].add(-moved).at[sink].add(moved)
    labels = jnp.searchsorted(jnp.cumsum(lengths), jnp.arange(rows * top), side="right").astype(jnp.int32)
    grid = labels.reshape(top, rows).T
    grid = grid[jax.random.permutation(jax.random.fold_in(own, 1), rows)]
    rotation = jax.random.randint(jax.random.fold_in(own, 2), (rows, 1), 0, top)
    return jnp.take_along_axis(grid, (jnp.arange(top)[None, :] + rotation) % top, axis=1)


def load_shares(count, total, limit, slope, full):
    loads = [(1 << 20) // math.isqrt(standing ** slope) + 1 for standing in range(1, count + 1)]
    largest = limit if full else min(limit, max(-(-total // count), total * loads[0] // sum(loads)))
    least = 1 if total - largest >= count - 1 else 0
    counts, rest = [largest] + [least] * (count - 1), total - largest - least * (count - 1)
    while rest > 0:
        free = [i for i in range(1, count) if counts[i] < largest] or [i for i in range(1, count) if counts[i] < limit]
        pool, left = sum([loads[i] for i in free]), rest
        for i in free:
            more = min(limit - counts[i], max(1, left * loads[i] // pool), rest)
            counts[i] = counts[i] + more
            rest = rest - more
    return np.array(counts)


def bell_draw(key, dims, spread, most, pieces=(), held_as=jnp.bfloat16):
    level = level_of(key, dims, pieces, -0.22, 0.18) if pieces else 1.0
    result = jax.random.normal(key, dims, jnp.float32) * spread * level
    return jnp.minimum(jnp.maximum(result, -most), most).astype(held_as)


def setup_inputs(seed: int = 0) -> dict:
    seeds = jax.random.split(jax.random.key(seed), 14)
    tokens = bell_draw(seeds[0], (TOKENS, D), 1.0, 6.0, ((0, 128),))
    seg_ids = draw_seg_ids(jax.random.fold_in(seeds[13], 71), 0)
    merge_index = draw_merge_index(jax.random.fold_in(seeds[13], 71), 0)
    owners_keys = jax.random.split(jax.random.fold_in(seeds[3], 1), MERGED // MG)
    owners_turns = jax.random.permutation(jax.random.fold_in(seeds[3], 3), MERGED // MG)
    owners = jax.vmap(lambda own, number: assign_block(jax.random.fold_in(seeds[3], 2), own, number, MG, N_TOK, 1, CAP, 1))(owners_keys, owners_turns).reshape((MERGED, 1))
    w_qkv = bell_draw(seeds[4], (D, 3 * HEADS * HD), D ** -0.5, 0.15625)
    w_attn_out = bell_draw(seeds[5], (HEADS * HD, D), 0.3, 1.75)
    w_in = bell_draw(seeds[6], (FF, D), D ** -0.5, 0.15625, ((0, 4),))
    in_bias = bell_draw(seeds[7], (FF,), 0.5, 3.0, ((0, 4),))
    w_out = bell_draw(seeds[8], (FF, D), FF ** -0.5, 0.078125, ((0, 4),))
    out_bias = bell_draw(seeds[9], (D,), 0.5, 3.0, (), jnp.float32)
    merge_gain = jnp.clip(1.0 + 0.18 * jax.random.normal(seeds[10], (D,), jnp.float32), 0.1, 1.9)
    w_merge = bell_draw(seeds[11], (4 * D, OUT), (4 * D) ** -0.5, 0.078125, ((1, 4),))
    merge_bias = bell_draw(seeds[12], (OUT,), 0.5, 3.0, ((0, 4),), jnp.float32)
    return dict(tokens=tokens, seg_ids=seg_ids, merge_index=merge_index, owners=owners, w_qkv=w_qkv, w_attn_out=w_attn_out, w_in=w_in, in_bias=in_bias, w_out=w_out, out_bias=out_bias, merge_gain=merge_gain, w_merge=w_merge, merge_bias=merge_bias)


NORM_EPS = 1e-06

def layer_norm(values):
    centred = values - lax.optimization_barrier(jnp.mean(values, axis=-1, keepdims=True))
    return centred * lax.rsqrt(lax.optimization_barrier(jnp.mean(centred * centred, axis=-1, keepdims=True)) + NORM_EPS)

def head_norm(values):
    return values * lax.rsqrt(lax.optimization_barrier(jnp.mean(values * values, axis=-1, keepdims=True)) + NORM_EPS)

def reference(tokens, seg_ids, merge_index, owners, w_qkv, w_attn_out, w_in, in_bias, w_out, out_bias, merge_gain, w_merge, merge_bias):
    head_width = HEADS * HD
    normed = layer_norm(tokens.astype(jnp.float32)).astype(jnp.bfloat16)
    projected = jnp.dot(normed, w_qkv, preferred_element_type=jnp.float32).astype(jnp.bfloat16)
    queries = head_norm(projected[:, :head_width].astype(jnp.float32).reshape(TOKENS, HEADS, HD)).astype(jnp.bfloat16)
    key_rows = head_norm(projected[:, head_width:2 * head_width].astype(jnp.float32).reshape(TOKENS, HEADS, HD)).astype(jnp.bfloat16)
    value_rows = projected[:, 2 * head_width:].reshape(TOKENS, HEADS, HD)
    block_rows = min(512, GROUP_TOK)
    score_scale = 1.0 / math.sqrt(HD)

    def attend_block(block_id):
        first_row = (block_id * block_rows).astype(jnp.int32)
        group_start = (first_row // GROUP_TOK * GROUP_TOK).astype(jnp.int32)
        block_query = lax.dynamic_slice_in_dim(queries, first_row, block_rows, 0)
        block_seg = lax.dynamic_slice_in_dim(seg_ids, first_row, block_rows, 0)
        group_keys = lax.dynamic_slice_in_dim(key_rows, group_start, GROUP_TOK, 0)
        group_values = lax.dynamic_slice_in_dim(value_rows, group_start, GROUP_TOK, 0)
        group_seg = lax.dynamic_slice_in_dim(seg_ids, group_start, GROUP_TOK, 0)
        scores = jnp.einsum('qhd,khd->hqk', block_query.astype(jnp.float32), group_keys.astype(jnp.float32)) * score_scale
        same_segment = (block_seg[:, None] == group_seg[None, :])[None]
        weights = jnp.where(same_segment, jnp.exp(scores), 0.0)
        denominator = lax.optimization_barrier(jnp.sum(weights, axis=-1))
        rounded = lax.optimization_barrier(weights.astype(jnp.bfloat16)).astype(jnp.float32)
        numerator = jnp.einsum('hqk,khd->qhd', rounded, group_values.astype(jnp.float32))
        return (numerator / jnp.transpose(denominator)[:, :, None]).astype(jnp.bfloat16)
    attended = lax.map(attend_block, jnp.arange(TOKENS // block_rows, dtype=jnp.int32)).reshape(TOKENS, head_width)
    residual = (tokens.astype(jnp.float32) + jnp.dot(attended, w_attn_out, preferred_element_type=jnp.float32)).astype(jnp.bfloat16)
    mlp_in = layer_norm(residual.astype(jnp.float32)).astype(jnp.bfloat16)

    def add_slice(running, shard_id):
        first_unit = (shard_id * FF_DEV).astype(jnp.int32)
        in_rows = lax.dynamic_slice_in_dim(w_in, first_unit, FF_DEV, 0)
        bias_part = lax.dynamic_slice_in_dim(in_bias, first_unit, FF_DEV, 0)
        out_rows = lax.dynamic_slice_in_dim(w_out, first_unit, FF_DEV, 0)
        pre_act = lax.dot_general(mlp_in, in_rows, (((1,), (1,)), ((), ())), preferred_element_type=jnp.float32)
        hidden = jax.nn.gelu(pre_act + bias_part.astype(jnp.float32), approximate=False).astype(jnp.bfloat16)
        partial_sum = jnp.dot(hidden, out_rows, preferred_element_type=jnp.float32)
        rounded = lax.optimization_barrier(partial_sum.astype(jnp.bfloat16)).astype(jnp.float32)
        return (running + rounded, None)
    mlp_sum, unused = lax.scan(add_slice, jnp.zeros((TOKENS, D), jnp.float32), jnp.arange(FF // FF_DEV, dtype=jnp.int32))
    normed_out = (layer_norm(residual.astype(jnp.float32) + mlp_sum + out_bias) * merge_gain).astype(jnp.bfloat16)
    device_first = jnp.arange(TOKENS, dtype=jnp.int32) // TOK_DEV * TOK_DEV
    merged = jnp.take(normed_out, device_first + merge_index, axis=0).reshape(MERGED, 4 * D)
    embedded = (jnp.dot(merged, w_merge, preferred_element_type=jnp.float32) + merge_bias).astype(jnp.bfloat16)
    owner_col = owners[:, 0].reshape(MERGED // MG, MG)
    positions = jnp.arange(MG, dtype=jnp.int32)
    earlier = (owner_col[:, :, None] == owner_col[:, None, :]) & (positions[None, None, :] < positions[None, :, None])
    owner_rank = lax.optimization_barrier(jnp.sum(earlier.astype(jnp.int32), axis=2)).reshape(MERGED)
    device_id = jnp.arange(MERGED, dtype=jnp.int32) // MG
    row_index = owners[:, 0] * ROWS_OWNER + device_id * CAP + owner_rank
    embeds = jnp.zeros((N_TOK * ROWS_OWNER, OUT), jnp.bfloat16).at[row_index].set(embedded)
    return embeds
```

```python
import math

import jax
import jax.numpy as jnp
from jax import lax
from jax.experimental import pallas as pl
from jax.experimental.pallas import tpu as pltpu
from jax.sharding import Mesh
from jax.sharding import PartitionSpec as P

HEADS = 8
HD = 88
EXT = 8
NORM_EPS = 1e-06
LANES = 128
F32 = jnp.float32
BF16 = jnp.bfloat16
VMEM_LIMIT = 60 * 1024 * 1024


def cparams(*semantics):
    return pltpu.CompilerParams(
        dimension_semantics=semantics or None, vmem_limit_bytes=VMEM_LIMIT
    )


def layer_norm(values):
    centred = values - jnp.mean(values, axis=-1, keepdims=True)
    return centred * lax.rsqrt(jnp.mean(centred * centred, axis=-1, keepdims=True) + NORM_EPS)


def dot(a, b, dims=(((1,), (0,)), ((), ()))):
    return lax.dot_general(a, b, dims, preferred_element_type=F32)


NT = (((1,), (1,)), ((), ()))


def qkv_kernel(x_ref, seg_ref, w_hbm, out_ref, w_ref, acc_ref, sems, *, chunks):
    copies = []
    for number, (start, size) in enumerate(chunks):
        copy = pltpu.make_async_copy(
            w_hbm.at[pl.ds(start, size)], w_ref.at[pl.ds(start, size)], sems.at[number]
        )
        copy.start()
        copies.append(copy)
    normed = layer_norm(x_ref[...].astype(F32)).astype(BF16)
    for number, (start, size) in enumerate(chunks):
        copies[number].wait()
        part = dot(normed[:, start : start + size], w_ref[start : start + size, :])
        if number == 0:
            acc_ref[...] = part
        else:
            acc_ref[...] += part
    projected = acc_ref[...].astype(BF16).astype(F32).T
    width = HEADS * HD
    seg = seg_ref[...]
    high = seg // 64
    low = seg - high * 64
    tokens = seg.shape[1]
    row = lax.broadcasted_iota(jnp.int32, (EXT, tokens), 0)
    extra = jnp.where(row == 0, 1, jnp.where(row == 1, high, jnp.where(row == 2, low, 0)))
    extra = extra.astype(F32)
    scale = math.log2(math.e) / math.sqrt(HD)
    for head in range(HEADS):
        at = head * HD
        q = projected[at : at + HD]
        k = projected[width + at : width + at + HD]
        v = projected[2 * width + at : 2 * width + at + HD]
        q = q * (lax.rsqrt(jnp.mean(q * q, axis=0, keepdims=True) + NORM_EPS) * scale)
        k = k * lax.rsqrt(jnp.mean(k * k, axis=0, keepdims=True) + NORM_EPS)
        out_ref[head] = jnp.concatenate([q, k, v, extra], axis=0).astype(BF16)


def qkv(tokens, seg_ids, w_qkv):
    rows, width = tokens.shape
    edges = list(range(0, width, 3 * LANES)) + [width]
    chunks = tuple((a, b - a) for a, b in zip(edges[:-1], edges[1:]))
    return pl.pallas_call(
        lambda *refs: qkv_kernel(*refs, chunks=chunks),
        out_shape=jax.ShapeDtypeStruct((HEADS, 3 * HD + EXT, rows), BF16),
        in_specs=[
            pl.BlockSpec(memory_space=pltpu.VMEM),
            pl.BlockSpec(memory_space=pltpu.VMEM),
            pl.BlockSpec(memory_space=pl.ANY),
        ],
        out_specs=pl.BlockSpec(memory_space=pltpu.VMEM),
        scratch_shapes=[
            pltpu.VMEM(w_qkv.shape, BF16),
            pltpu.VMEM((rows, w_qkv.shape[1]), F32),
            pltpu.SemaphoreType.DMA((len(chunks),)),
        ],
        compiler_params=cparams(),
        name="qkv",
    )(tokens, seg_ids.reshape(1, rows), w_qkv)


def attend_kernel(*refs, first, last, key_block):
    if first:
        q_ref, kv_ref, out_ref, q_sc, segq_sc, k_sc, v_sc, segk_sc = refs
    else:
        q_ref, kv_ref, acc_ref, out_ref, q_sc, segq_sc, k_sc, v_sc, segk_sc = refs
    blocks, _, tokens = kv_ref.shape
    for j in range(blocks):
        at = pl.ds(j * tokens, tokens)
        kv = kv_ref[j].astype(F32)
        k_sc[:, j * tokens : (j + 1) * tokens] = jnp.concatenate(
            [kv[:HD], jnp.zeros((LANES - HD, tokens), F32)], axis=0
        ).astype(BF16)
        wide = jnp.concatenate(
            [kv[HD:], jnp.zeros((LANES - HD - EXT, tokens), F32)], axis=0
        )
        v_sc[at, :] = wide.T.astype(BF16)
        segk_sc[:, j * tokens : (j + 1) * tokens] = (
            kv[2 * HD + 1 : 2 * HD + 2] * 64.0 + kv[2 * HD + 2 : 2 * HD + 3]
        )
        q = q_ref[j].astype(F32)
        q_sc[at, :] = (
            jnp.concatenate([q[:HD], jnp.zeros((LANES - HD, tokens), F32)], axis=0)
            .T.astype(BF16)
        )
        seg = q[3 * HD + 1 : 3 * HD + 2] * 64.0 + q[3 * HD + 2 : 3 * HD + 3]
        segq_sc[at, :] = jnp.broadcast_to(seg, (LANES, tokens)).T

    def tile(step, carry):
        rows = pl.ds(pl.multiple_of(step * tokens, tokens), tokens)
        q = q_sc[rows, :]
        segq = segq_sc[rows, 0:1]
        total = None
        for start in range(0, blocks * tokens, key_block):
            scores = dot(q, k_sc[:, start : start + key_block])
            same = segq == segk_sc[:, start : start + key_block]
            weights = jnp.where(same, jnp.exp2(scores), 0.0).astype(BF16)
            part = dot(weights, v_sc[start : start + key_block, :])
            total = part if total is None else total + part
        if not first:
            total = total + acc_ref[rows, :]
        if last:
            total = total / total[:, HD : HD + 1]
            out_ref[step] = total.T[:HD].astype(BF16)
        else:
            out_ref[rows, :] = total
        return carry

    lax.fori_loop(0, blocks, tile, 0)


def attend(queries, kv, acc=None, last=False, key_block=1024):
    blocks, _, tokens = kv.shape
    total = blocks * tokens
    first = acc is None
    if last:
        shape = jax.ShapeDtypeStruct((blocks, HD, tokens), BF16)
    else:
        shape = jax.ShapeDtypeStruct((total, LANES), F32)
    operands = (queries, kv) if first else (queries, kv, acc)
    return pl.pallas_call(
        lambda *refs: attend_kernel(*refs, first=first, last=last, key_block=key_block),
        out_shape=shape,
        in_specs=[pl.BlockSpec(memory_space=pltpu.VMEM)] * len(operands),
        out_specs=pl.BlockSpec(memory_space=pltpu.VMEM),
        scratch_shapes=[
            pltpu.VMEM((total, LANES), BF16),
            pltpu.VMEM((total, LANES), F32),
            pltpu.VMEM((LANES, total), BF16),
            pltpu.VMEM((total, LANES), BF16),
            pltpu.VMEM((1, total), F32),
        ],
        compiler_params=cparams(),
        name="attend",
    )(*operands)


def project_kernel(att_ref, x_ref, w_ref, res_ref, in_ref):
    heads, _, tokens = att_ref.shape
    att = att_ref[...].astype(F32).reshape(heads * HD, tokens).T.astype(BF16)
    residual = (x_ref[...].astype(F32) + dot(att, w_ref[...])).astype(BF16)
    res_ref[...] = residual
    in_ref[...] = layer_norm(residual.astype(F32)).astype(BF16)


def project(attended, tokens, w_attn_out):
    shape = jax.ShapeDtypeStruct(tokens.shape, BF16)
    return pl.pallas_call(
        project_kernel,
        out_shape=(shape, shape),
        in_specs=[pl.BlockSpec(memory_space=pltpu.VMEM)] * 3,
        out_specs=(pl.BlockSpec(memory_space=pltpu.VMEM),) * 2,
        compiler_params=cparams(),
        name="project",
    )(attended, tokens, w_attn_out)


def mlp_kernel(*refs, pieces):
    x_refs = refs[:pieces]
    w_in_ref, bias_ref, w_out_ref, out_ref, x_sc, acc_ref = refs[pieces:]
    step = pl.program_id(0)

    @pl.when(step == 0)
    def _():
        at = 0
        for x_ref in x_refs:
            x_sc[at : at + x_ref.shape[0], :] = x_ref[...]
            at += x_ref.shape[0]

    pre = dot(x_sc[...], w_in_ref[...], NT) + bias_ref[...].astype(F32)
    hidden = (0.5 * pre * (1.0 + lax.erf(pre * math.sqrt(0.5)))).astype(BF16)
    part = dot(hidden, w_out_ref[...])

    @pl.when(step == 0)
    def _():
        acc_ref[...] = part

    @pl.when(step > 0)
    def _():
        acc_ref[...] += part

    @pl.when(step == pl.num_programs(0) - 1)
    def _():
        out_ref[...] = acc_ref[...].astype(BF16)


def mlp(pieces, w_in, in_bias, w_out, block=256):
    units, width = w_in.shape
    rows = sum(piece.shape[0] for piece in pieces)
    whole = lambda i: (0, 0)
    return pl.pallas_call(
        lambda *refs: mlp_kernel(*refs, pieces=len(pieces)),
        out_shape=jax.ShapeDtypeStruct((rows, width), BF16),
        grid=(units // block,),
        in_specs=[pl.BlockSpec(piece.shape, whole) for piece in pieces]
        + [
            pl.BlockSpec((block, width), lambda i: (i, 0)),
            pl.BlockSpec((1, block), lambda i: (0, i)),
            pl.BlockSpec((block, width), lambda i: (i, 0)),
        ],
        out_specs=pl.BlockSpec((rows, width), whole),
        scratch_shapes=[pltpu.VMEM((rows, width), BF16), pltpu.VMEM((rows, width), F32)],
        compiler_params=cparams("arbitrary"),
        name="mlp",
    )(*pieces, w_in, in_bias.reshape(1, units), w_out)


def merge_kernel(*refs, halves, cap):
    res_ref, bias_ref, gain_ref, index_ref, owner_ref = refs[:5]
    parts = refs[5 : 5 + 3 * halves]
    out_ref, sum_sc = refs[5 + 3 * halves :]
    rows, width = res_ref.shape
    half = rows // halves
    for h in range(halves):
        at = slice(h * half, (h + 1) * half)
        own, left, right = parts[3 * h : 3 * h + 3]
        total = own[...].astype(F32) + left[...].astype(F32) + right[...].astype(F32)
        total = res_ref[at, :].astype(F32) + total + bias_ref[...]
        sum_sc[at, :] = (layer_norm(total) * gain_ref[...]).astype(BF16)
    normed = sum_sc[...]
    count = rows // 4
    lane = lax.broadcasted_iota(jnp.int32, (count, rows), 1)
    for c in range(4):
        pick = (index_ref[:, c : c + 1] == lane).astype(BF16)
        out_ref[:, c * width : (c + 1) * width] = dot(pick, normed).astype(BF16)
    owner = owner_ref[...]
    r = lax.broadcasted_iota(jnp.int32, (count, count), 0)
    s = lax.broadcasted_iota(jnp.int32, (count, count), 1)
    across = jnp.sum(jnp.where(r == s, owner, 0), axis=0, keepdims=True)
    earlier = (across == owner) & (s < r)
    rank = jnp.sum(earlier.astype(jnp.int32), axis=1, keepdims=True)
    slot = (owner * cap + rank).astype(F32).astype(BF16)
    out_ref[:, 4 * width :] = jnp.broadcast_to(slot, (count, LANES))


def merge(residual, out_bias, merge_gain, merge_index, owners, parts, cap):
    rows, width = residual.shape
    operands = (
        residual,
        out_bias.reshape(1, width),
        merge_gain.reshape(1, width),
        merge_index.reshape(rows // 4, 4),
        owners,
        *parts,
    )
    return pl.pallas_call(
        lambda *refs: merge_kernel(*refs, halves=len(parts) // 3, cap=cap),
        out_shape=jax.ShapeDtypeStruct((rows // 4, 4 * width + LANES), BF16),
        in_specs=[pl.BlockSpec(memory_space=pltpu.VMEM)] * len(operands),
        out_specs=pl.BlockSpec(memory_space=pltpu.VMEM),
        scratch_shapes=[pltpu.VMEM((rows, width), BF16)],
        compiler_params=cparams(),
        name="merge",
    )(*operands)


def embed_kernel(group_ref, *refs, pieces, cap, slots):
    x_refs = refs[: len(pieces)]
    w_ref, bias_ref, out_ref, x_sc, acc_ref = refs[len(pieces) :]
    step = pl.program_id(0)
    steps = pl.num_programs(0)
    for (at, _), x_ref in zip(pieces, x_refs):
        x_sc[at : at + x_ref.shape[0], :] = x_ref[...]

    @pl.when(step < steps - 1)
    def _():
        part = dot(x_sc[...], w_ref[...])

        @pl.when(step == 0)
        def _():
            acc_ref[...] = part

        @pl.when(step > 0)
        def _():
            acc_ref[...] += part

    @pl.when(step == steps - 1)
    def _():
        embedded = (acc_ref[...] + bias_ref[...]).astype(BF16)
        total = x_sc.shape[0]
        count = total // 4
        slot = x_sc[:, 0:1].astype(F32).astype(jnp.int32)
        owner = slot // cap
        rank = slot - owner * cap
        shift = lax.broadcasted_iota(jnp.int32, (total, 1), 0) // count
        group = group_ref[0] + shift
        group = jnp.where(group >= 4, group - 4, group)
        target = owner * slots + group * cap + rank
        lane = lax.broadcasted_iota(jnp.int32, (total, out_ref.shape[0]), 1)
        place = (target == lane).astype(F32).T.astype(BF16)
        out_ref[...] = dot(place, embedded).astype(BF16)


def embed(group, pieces, w_merge, merge_bias, cap, slots, owners, block=1408):
    arrays = [array for _, array in pieces]
    rows = sum(array.shape[0] for array in arrays)
    depth, cols = w_merge.shape
    steps = depth // block
    places = tuple((at, array.shape[0]) for at, array in pieces)
    x_block = block

    def x_map(i, _):
        return (0, i)

    spec = lambda array: pl.BlockSpec((array.shape[0], x_block), x_map)
    return pl.pallas_call(
        lambda *refs: embed_kernel(*refs, pieces=places, cap=cap, slots=slots),
        out_shape=jax.ShapeDtypeStruct((owners * slots, cols), BF16),
        grid_spec=pltpu.PrefetchScalarGridSpec(
            num_scalar_prefetch=1,
            grid=(steps + 1,),
            in_specs=[spec(array) for array in arrays]
            + [
                pl.BlockSpec((block, cols), lambda i, _: (jnp.minimum(i, steps - 1), 0)),
                pl.BlockSpec((1, cols), lambda i, _: (0, 0)),
            ],
            out_specs=pl.BlockSpec((owners * slots, cols), lambda i, _: (0, 0)),
            scratch_shapes=[pltpu.VMEM((rows, block), BF16), pltpu.VMEM((rows, cols), F32)],
        ),
        compiler_params=cparams("arbitrary"),
        name="embed",
    )(group, *arrays, w_merge, merge_bias.reshape(1, cols))


def flip(value, axis):
    return lax.ppermute(value, axis, [(0, 1), (1, 0)])


def turn(value, axis, by):
    size = lax.axis_size(axis)
    return lax.ppermute(value, axis, [(i, (i + by) % size) for i in range(size)])


def ring_gather(value, axis):
    before = turn(value, axis, 1)
    after = turn(value, axis, -1)
    half = value.shape[0] // 2
    return before, after, turn(before[:half], axis, 1), turn(after[half:], axis, -1)


def ring_scatter(own, before, after, opposite, axis):
    half = own.shape[0] // 2
    one = turn(opposite[:half], axis, 1)
    two = turn(opposite[half:], axis, -1)
    to_next = jnp.concatenate([(after[:half].astype(F32) + one.astype(F32)).astype(BF16), after[half:]])
    to_last = jnp.concatenate([before[:half], (before[half:].astype(F32) + two.astype(F32)).astype(BF16)])
    return own, turn(to_next, axis, 1), turn(to_last, axis, -1)


HALVES = 2


def local(
    tokens,
    seg_ids,
    merge_index,
    owners,
    w_qkv,
    w_attn_out,
    w_in,
    in_bias,
    w_out,
    out_bias,
    merge_gain,
    w_merge,
    merge_bias,
):
    rows = tokens.shape[0]
    heads = qkv(tokens, seg_ids, w_qkv)
    mine = lax.all_to_all(heads, ("y", "xh"), 0, 0, tiled=True)
    kv = mine[:, HD:]
    kv_c = flip(kv, "c")
    kv_x = flip(kv, "xl")
    kv_xc = flip(kv_x, "c")
    acc = attend(mine, kv)
    acc = attend(mine, kv_c, acc)
    acc = attend(mine, kv_x, acc)
    done = attend(mine, kv_xc, acc, last=True)
    attended = lax.all_to_all(done, ("y", "xh"), 0, 0, tiled=True)
    residual, mlp_in = project(attended, tokens, w_attn_out)
    half = rows // HALVES
    parts = []
    for h in range(HALVES):
        own = mlp_in[h * half : (h + 1) * half]
        before, after, far_a, far_b = ring_gather(own, "grp")
        out = mlp([own, before, after, far_a, far_b], w_in, in_bias, w_out)
        blocks = [out[i * half : (i + 1) * half] for i in range(4)]
        parts.extend(ring_scatter(*blocks, "grp"))
    owner_count = 32
    cap = 4
    merged = merge(residual, out_bias, merge_gain, merge_index, owners, parts, cap)
    count = merged.shape[0]
    before, after, far_a, far_b = ring_gather(merged, "grp")
    pieces = [
        (0, merged),
        (count, after),
        (2 * count, far_a),
        (2 * count + count // 2, far_b),
        (3 * count, before),
    ]
    group = lax.axis_index("grp").reshape(1).astype(jnp.int32)
    slots = 4 * cap
    outgoing = embed(group, pieces, w_merge, merge_bias, cap, slots, owner_count)
    cols = outgoing.shape[1]
    outgoing = outgoing.reshape(owner_count, 4, cap, cols)
    received = lax.all_to_all(
        outgoing, ("y", "xh", "xl", "c"), split_axis=0, concat_axis=2, tiled=True
    )
    return received.reshape(4 * owner_count * cap, cols)


def solution(mesh):
    inner = Mesh(mesh.devices.reshape(4, 4, 2, 2, 2), ("grp", "y", "xh", "xl", "c"))
    every = ("grp", "y", "xh", "xl", "c")
    tok = ("y", "xh", "xl", "c")
    placed = (
        P(every, None),
        P(every),
        P(every),
        P(every, None),
        P(),
        P(),
        P("grp", None),
        P("grp"),
        P("grp", None),
        P(),
        P(),
        P(None, "grp"),
        P("grp"),
    )
    return jax.shard_map(
        local, mesh=inner, in_specs=placed, out_specs=P(tok, "grp"), check_vma=False
    )
```

```python
import math

import jax
import jax.numpy as jnp
from jax import lax
from jax.experimental import pallas as pl
from jax.experimental.pallas import tpu as pltpu
from jax.sharding import Mesh
from jax.sharding import PartitionSpec as P

HEADS = 8
HD = 88
EXT = 8
NORM_EPS = 1e-06
LANES = 128
PAD = 16
F32 = jnp.float32
BF16 = jnp.bfloat16
VMEM_LIMIT = 60 * 1024 * 1024


def cparams(*semantics):
    return pltpu.CompilerParams(
        dimension_semantics=semantics or None, vmem_limit_bytes=VMEM_LIMIT
    )


def layer_norm(values):
    centred = values - jnp.mean(values, axis=-1, keepdims=True)
    return centred * lax.rsqrt(jnp.mean(centred * centred, axis=-1, keepdims=True) + NORM_EPS)


def dot(a, b, dims=(((1,), (0,)), ((), ()))):
    return lax.dot_general(a, b, dims, preferred_element_type=F32)


NT = (((1,), (1,)), ((), ()))


def cost(flops, size, transcendentals=0):
    return pl.CostEstimate(flops=flops, bytes_accessed=size, transcendentals=transcendentals)


def qkv_kernel(x_ref, seg_ref, w_hbm, out_ref, w_ref, sems):
    group = HEADS // 2 * HD
    count = w_ref.shape[0] // group
    copies = []
    for number in range(count):
        at = pl.ds(number * group, group)
        copies.append(pltpu.make_async_copy(w_hbm.at[at], w_ref.at[at], sems.at[number]))
        copies[-1].start()
    normed = layer_norm(x_ref[...].astype(F32)).astype(BF16)
    seg = seg_ref[...]
    high = seg // 64
    low = seg - high * 64
    tokens = seg.shape[1]
    row = lax.broadcasted_iota(jnp.int32, (EXT, tokens), 0)
    extra = jnp.where(row == 0, 1, jnp.where(row == 1, high, jnp.where(row == 2, low, 0)))
    extra = extra.astype(F32)
    scale = math.log2(math.e) / math.sqrt(HD)
    for number in range(count):
        copies[number].wait()
        part = dot(w_ref[number * group : (number + 1) * group, :], normed, NT)
        part = part.astype(BF16).astype(F32)
        kind = number // 2
        for i in range(HEADS // 2):
            head = number % 2 * (HEADS // 2) + i
            rows = part[i * HD : (i + 1) * HD]
            if kind == 2:
                out_ref[head, : HD + EXT] = jnp.concatenate([rows, extra], axis=0).astype(BF16)
                continue
            norm = lax.rsqrt(jnp.mean(rows * rows, axis=0, keepdims=True) + NORM_EPS)
            if kind == 0:
                out_ref[head, 2 * HD + EXT :] = (rows * (norm * scale)).astype(BF16)
            else:
                out_ref[head, HD + EXT : 2 * HD + EXT] = (rows * norm).astype(BF16)


def qkv(tokens, seg_ids, w_qkv):
    rows, width = tokens.shape
    return pl.pallas_call(
        qkv_kernel,
        out_shape=jax.ShapeDtypeStruct((HEADS, 3 * HD + EXT, rows), BF16),
        in_specs=[
            pl.BlockSpec(memory_space=pltpu.VMEM),
            pl.BlockSpec(memory_space=pltpu.VMEM),
            pl.BlockSpec(memory_space=pl.ANY),
        ],
        out_specs=pl.BlockSpec(memory_space=pltpu.VMEM),
        scratch_shapes=[
            pltpu.VMEM((w_qkv.shape[1], width), BF16),
            pltpu.SemaphoreType.DMA((6,)),
        ],
        compiler_params=cparams(),
        cost_estimate=cost(2 * rows * width * w_qkv.shape[1], 8 << 20),
        name="qkv",
    )(tokens, seg_ids.reshape(1, rows), w_qkv.T)


def attend_kernel(*refs, sets, first, last, key_block):
    q_ref = refs[0]
    kv_refs = refs[1 : 1 + sets]
    rest = refs[1 + sets :]
    if not first:
        acc_ref, rest = rest[0], rest[1:]
    out_ref, k_sc, v_sc, seg_sc = rest
    blocks, _, tokens = kv_refs[0].shape
    top = HD + EXT
    width = LANES - HD

    @pl.when(pl.program_id(0) == 0)
    def _():
        for number, kv_ref in enumerate(kv_refs):
            for j in range(blocks):
                start = (number * blocks + j) * tokens
                digits = kv_ref[j, :top].astype(F32)
                seg = digits[HD + 1 : HD + 2] * 64.0 + digits[HD + 2 : HD + 3]
                keys = kv_ref[j, top : top + HD].astype(F32)
                both = jnp.concatenate([keys, jnp.broadcast_to(seg, (width, tokens))], axis=0).T
                v_sc[:, start : start + tokens] = kv_ref[j, :top]
                k_sc[start : start + tokens, :] = both.astype(BF16)
                seg_sc[start : start + tokens, :] = jnp.broadcast_to(
                    both[:, HD : HD + 1], (tokens, LANES)
                )

    mine = q_ref[0].astype(F32)
    q = jnp.concatenate([mine[top + HD :], jnp.zeros((width, tokens), F32)], axis=0)
    q = q.astype(BF16)
    seg = mine[HD + 1 : HD + 2] * 64.0 + mine[HD + 2 : HD + 3]
    total = None if first else acc_ref[...]
    for start in range(0, sets * blocks * tokens, key_block):
        at = slice(start, start + key_block)
        scores = dot(k_sc[at, :], q)
        of_key = seg_sc[at, :]
        of_key = jnp.concatenate([of_key] * (tokens // LANES), axis=1)
        weights = jnp.where(of_key == seg, jnp.exp2(scores), 0.0).astype(BF16)
        part = dot(v_sc[:, at], weights)
        total = part if total is None else total + part
    if last:
        out_ref[0] = (total[:HD] / total[HD : HD + 1]).astype(BF16)
    else:
        out_ref[...] = total


def attend(queries, sets, acc=None, last=False, key_block=512):
    blocks, depth, tokens = queries.shape
    total = blocks * tokens
    keys = total * len(sets)
    first = acc is None
    top = HD + EXT
    block = pl.BlockSpec((top, tokens), lambda i: (0, i))
    if last:
        shape = jax.ShapeDtypeStruct((blocks, HD, tokens), BF16)
        out_spec = pl.BlockSpec((1, HD, tokens), lambda i: (i, 0, 0))
    else:
        shape = jax.ShapeDtypeStruct((top, total), F32)
        out_spec = block
    in_specs = [pl.BlockSpec((1, depth, tokens), lambda i: (i, 0, 0))]
    in_specs += [pl.BlockSpec(kv.shape, lambda i: (0, 0, 0)) for kv in sets]
    operands = [queries, *sets]
    if not first:
        in_specs.append(block)
        operands.append(acc)
    return pl.pallas_call(
        lambda *refs: attend_kernel(
            *refs, sets=len(sets), first=first, last=last, key_block=key_block
        ),
        out_shape=shape,
        grid=(blocks,),
        in_specs=in_specs,
        out_specs=out_spec,
        scratch_shapes=[
            pltpu.VMEM((keys, LANES), BF16),
            pltpu.VMEM((top, keys), BF16),
            pltpu.VMEM((keys, LANES), F32),
        ],
        compiler_params=cparams("arbitrary"),
        cost_estimate=cost(4 * total * keys * LANES, 3 << 20, total * keys),
        name="attend",
    )(*operands)


def project_kernel(att_ref, x_ref, w_ref, res_ref, in_ref):
    heads, _, tokens = att_ref.shape
    att = att_ref[...].astype(F32).reshape(heads * HD, tokens).T.astype(BF16)
    residual = (x_ref[...].astype(F32) + dot(att, w_ref[...])).astype(BF16)
    res_ref[...] = residual
    in_ref[...] = layer_norm(residual.astype(F32)).astype(BF16)


def project(attended, tokens, w_attn_out):
    shape = jax.ShapeDtypeStruct(tokens.shape, BF16)
    return pl.pallas_call(
        project_kernel,
        out_shape=(shape, shape),
        in_specs=[pl.BlockSpec(memory_space=pltpu.VMEM)] * 3,
        out_specs=(pl.BlockSpec(memory_space=pltpu.VMEM),) * 2,
        compiler_params=cparams(),
        cost_estimate=cost(2 * tokens.shape[0] * w_attn_out.shape[0] * w_attn_out.shape[1], 4 << 20),
        name="project",
    )(attended, tokens, w_attn_out)


def mlp_kernel(x_ref, pair_ref, *refs):
    packs = refs[:4]
    own_ref, other_ref, near, far, sems = refs[4:]
    rows = x_ref.shape[0]
    copies = []
    for number in range(3):
        copies.append(pltpu.make_async_copy(packs[number], near.at[number], sems.at[number]))
    copies.append(pltpu.make_async_copy(packs[3], far, sems.at[3]))
    for copy in copies:
        copy.start()
    units = (near.shape[1] - PAD) // 2
    shards = far.shape[0]
    piece = (far.shape[1] - EXT) // 2
    x = x_ref[...], pair_ref[...]
    total = [None, None]
    for number in range(4):
        copies[number].wait()
        if number < 3:
            into = near[number, :units]
            out_of = near[number, units : 2 * units]
            bias = near[number, 2 * units : 2 * units + 1, :units].astype(F32)
        else:
            into = far[:, :piece].reshape(shards * piece, -1)
            out_of = far[:, piece : 2 * piece].reshape(shards * piece, -1)
            bias = jnp.concatenate(
                [far[i, 2 * piece : 2 * piece + 1, :piece].astype(F32) for i in range(shards)],
                axis=1,
            )
        before = [dot(part, into, NT) + bias for part in x]
        for i in range(2):
            pre = before[i]
            hidden = (0.5 * pre * (1.0 + lax.erf(pre * math.sqrt(0.5)))).astype(BF16)
            part = dot(hidden, out_of)
            total[i] = part if total[i] is None else total[i] + part
    own_ref[...] = total[0].astype(BF16)
    other_ref[...] = total[1].astype(BF16)


def mlp(x, pair, packs):
    rows, width = x.shape
    shape = jax.ShapeDtypeStruct((rows, width), BF16)
    vmem = pl.BlockSpec(memory_space=pltpu.VMEM)
    units = (packs[0].shape[0] - PAD) // 2
    return pl.pallas_call(
        mlp_kernel,
        out_shape=(shape, shape),
        in_specs=[vmem, vmem] + [pl.BlockSpec(memory_space=pl.ANY)] * 4,
        out_specs=(vmem, vmem),
        scratch_shapes=[
            pltpu.VMEM((3,) + packs[0].shape, BF16),
            pltpu.VMEM(packs[3].shape, BF16),
            pltpu.SemaphoreType.DMA((4,)),
        ],
        compiler_params=cparams(),
        cost_estimate=cost(2 * rows * 4 * units * width * 4, 20 << 20),
        name="mlp",
    )(x, pair, *packs)


def merge_kernel(res_ref, bias_ref, gain_ref, index_ref, owner_ref, own_ref, other_ref, out_ref, *, cap):
    rows, width = res_ref.shape
    total = own_ref[...].astype(F32) + other_ref[...].astype(F32)
    total = res_ref[...].astype(F32) + total + bias_ref[...]
    normed = (layer_norm(total) * gain_ref[...]).astype(BF16)
    count = rows // 4
    r = lax.broadcasted_iota(jnp.int32, (rows, rows), 0)
    s = lax.broadcasted_iota(jnp.int32, (rows, rows), 1)
    named = (index_ref[...] == r).astype(F32).astype(BF16)
    order = (s == 4 * (r % count) + r // count).astype(F32).astype(BF16)
    pick = dot(order, named, NT).astype(BF16)
    merged = dot(pick, normed).astype(BF16)
    for c in range(4):
        out_ref[:, c * width : (c + 1) * width] = merged[c * count : (c + 1) * count]
    across = owner_ref[...]
    r = lax.broadcasted_iota(jnp.int32, (count, count), 0)
    s = lax.broadcasted_iota(jnp.int32, (count, count), 1)
    owner = jnp.sum(jnp.where(r == s, across, 0), axis=1, keepdims=True)
    earlier = (across == owner) & (s < r)
    rank = jnp.sum(earlier.astype(jnp.int32), axis=1, keepdims=True)
    slot = (owner * cap + rank).astype(F32).astype(BF16)
    out_ref[:, 4 * width :] = jnp.broadcast_to(slot, (count, LANES))


def merge(residual, out_bias, merge_gain, merge_index, owners, own, other, cap):
    rows, width = residual.shape
    operands = (
        residual,
        out_bias.reshape(1, width),
        merge_gain.reshape(1, width),
        merge_index.reshape(1, rows),
        owners.reshape(1, rows // 4),
        own,
        other,
    )
    return pl.pallas_call(
        lambda *refs: merge_kernel(*refs, cap=cap),
        out_shape=jax.ShapeDtypeStruct((rows // 4, 4 * width + LANES), BF16),
        in_specs=[pl.BlockSpec(memory_space=pltpu.VMEM)] * len(operands),
        out_specs=pl.BlockSpec(memory_space=pltpu.VMEM),
        compiler_params=cparams(),
        cost_estimate=cost(2 * rows * rows * width, 4 << 20),
        name="merge",
    )(*operands)


def embed_kernel(group_ref, *refs, pieces, cap, slots):
    x_refs = refs[: len(pieces)]
    w_ref, bias_ref, out_ref, x_sc, acc_ref = refs[len(pieces) :]
    step = pl.program_id(0)
    steps = pl.num_programs(0)
    for (at, _), x_ref in zip(pieces, x_refs):
        x_sc[at : at + x_ref.shape[0], :] = x_ref[...]

    @pl.when(step < steps - 1)
    def _():
        part = dot(x_sc[...], w_ref[...])

        @pl.when(step == 0)
        def _():
            acc_ref[...] = part

        @pl.when(step > 0)
        def _():
            acc_ref[...] += part

    @pl.when(step == steps - 1)
    def _():
        embedded = (acc_ref[...] + bias_ref[...]).astype(BF16)
        total = x_sc.shape[0]
        count = total // 4
        slot = x_sc[:, 0:1].astype(F32).astype(jnp.int32)
        owner = slot // cap
        rank = slot - owner * cap
        shift = lax.broadcasted_iota(jnp.int32, (total, 1), 0) // count
        group = group_ref[0] + shift
        group = jnp.where(group >= 4, group - 4, group)
        target = owner * slots + group * cap + rank
        lane = lax.broadcasted_iota(jnp.int32, (total, out_ref.shape[0]), 1)
        place = (target == lane).astype(F32).T.astype(BF16)
        out_ref[...] = dot(place, embedded).astype(BF16)


def embed(group, pieces, w_merge, merge_bias, cap, slots, owners, block=1408):
    arrays = [array for _, array in pieces]
    rows = sum(array.shape[0] for array in arrays)
    depth, cols = w_merge.shape
    steps = depth // block
    places = tuple((at, array.shape[0]) for at, array in pieces)
    x_block = block

    def x_map(i, _):
        return (0, i)

    spec = lambda array: pl.BlockSpec((array.shape[0], x_block), x_map)
    return pl.pallas_call(
        lambda *refs: embed_kernel(*refs, pieces=places, cap=cap, slots=slots),
        out_shape=jax.ShapeDtypeStruct((owners * slots, cols), BF16),
        grid_spec=pltpu.PrefetchScalarGridSpec(
            num_scalar_prefetch=1,
            grid=(steps + 1,),
            in_specs=[spec(array) for array in arrays]
            + [
                pl.BlockSpec((block, cols), lambda i, _: (jnp.minimum(i, steps - 1), 0)),
                pl.BlockSpec((1, cols), lambda i, _: (0, 0)),
            ],
            out_specs=pl.BlockSpec((owners * slots, cols), lambda i, _: (0, 0)),
            scratch_shapes=[pltpu.VMEM((rows, block), BF16), pltpu.VMEM((rows, cols), F32)],
        ),
        compiler_params=cparams("arbitrary"),
        cost_estimate=cost(2 * rows * depth * cols, 10 << 20),
        name="embed",
    )(group, *arrays, w_merge, merge_bias.reshape(1, cols))


def flip(value, axis):
    return lax.ppermute(value, axis, [(0, 1), (1, 0)])


def turn(value, axis, by):
    size = lax.axis_size(axis)
    return lax.ppermute(value, axis, [(i, (i + by) % size) for i in range(size)])


def ring_gather(value, axis):
    before = turn(value, axis, 1)
    after = turn(value, axis, -1)
    half = value.shape[0] // 2
    return before, after, turn(before[:half], axis, 1), turn(after[half:], axis, -1)


def pack(w_in, in_bias, w_out, start, count, extra):
    width = w_in.shape[1]
    bias = lax.dynamic_slice_in_dim(in_bias, start, count)
    bias = jnp.pad(bias.reshape(1, count), ((0, extra - 1), (0, width - count)))
    return jnp.concatenate(
        [
            lax.dynamic_slice_in_dim(w_in, start, count),
            lax.dynamic_slice_in_dim(w_out, start, count),
            bias,
        ]
    )


def spread_weights(w_in, in_bias, w_out):
    half = w_in.shape[0] // 2
    core = lax.axis_index("c") * half
    chips = ("y", "xh", "xl")
    share = half // lax.axis_size(chips)
    start = core + lax.axis_index(chips) * share
    far = turn(pack(w_in, in_bias, w_out, start, share, EXT), "grp", 2)
    own = pack(w_in, in_bias, w_out, core, half, PAD)
    far = lax.all_gather(far, chips)
    return own, turn(own, "grp", 1), turn(own, "grp", -1), far


def local(
    tokens,
    seg_ids,
    merge_index,
    owners,
    w_qkv,
    w_attn_out,
    w_in,
    in_bias,
    w_out,
    out_bias,
    merge_gain,
    w_merge,
    merge_bias,
):
    packs = spread_weights(w_in, in_bias, w_out)
    heads = qkv(tokens, seg_ids, w_qkv)
    mine = lax.all_to_all(heads, ("y", "xh"), 0, 0, tiled=True)
    kv = mine[:, : 2 * HD + EXT]
    kv_x = flip(kv, "xl")
    kv_c = flip(kv, "c")
    kv_xc = flip(kv_x, "c")
    acc = attend(mine, [kv])
    acc = attend(mine, [kv_c], acc)
    done = attend(mine, [kv_x, kv_xc], acc, last=True)
    attended = lax.all_to_all(done, ("y", "xh"), 0, 0, tiled=True)
    residual, mlp_in = project(attended, tokens, w_attn_out)
    own, other = mlp(mlp_in, flip(mlp_in, "c"), packs)
    owner_count = lax.axis_size(("y", "xh", "xl", "c"))
    cap = 4
    merged = merge(
        residual, out_bias, merge_gain, merge_index, owners, own, flip(other, "c"), cap
    )
    count = merged.shape[0]
    before, after, far_a, far_b = ring_gather(merged, "grp")
    pieces = [
        (0, merged),
        (count, after),
        (2 * count, far_a),
        (2 * count + count // 2, far_b),
        (3 * count, before),
    ]
    group = lax.axis_index("grp").reshape(1).astype(jnp.int32)
    slots = 4 * cap
    outgoing = embed(group, pieces, w_merge, merge_bias, cap, slots, owner_count)
    cols = outgoing.shape[1]
    outgoing = outgoing.reshape(owner_count, 4, cap, cols)
    received = lax.all_to_all(
        outgoing, ("y", "xh", "xl", "c"), split_axis=0, concat_axis=2, tiled=True
    )
    return received.reshape(4 * owner_count * cap, cols)


def solution(mesh):
    inner = Mesh(mesh.devices.reshape(4, 4, 2, 2, 2), ("grp", "y", "xh", "xl", "c"))
    every = ("grp", "y", "xh", "xl", "c")
    tok = ("y", "xh", "xl", "c")
    placed = (
        P(every, None),
        P(every),
        P(every),
        P(every, None),
        P(),
        P(),
        P("grp", None),
        P("grp"),
        P("grp", None),
        P(),
        P(),
        P(None, "grp"),
        P("grp"),
    )
    return jax.shard_map(
        local, mesh=inner, in_specs=placed, out_specs=P(tok, "grp"), check_vma=False
    )
```

```python
import math

import jax
import jax.numpy as jnp
from jax import lax
from jax.experimental import pallas as pl
from jax.experimental.pallas import tpu as pltpu
from jax.sharding import Mesh
from jax.sharding import PartitionSpec as P

HEADS = 8
HD = 88
EXT = 8
NORM_EPS = 1e-06
LANES = 128
PAD = 16
F32 = jnp.float32
BF16 = jnp.bfloat16
VMEM_LIMIT = 60 * 1024 * 1024


def cparams(*semantics):
    return pltpu.CompilerParams(
        dimension_semantics=semantics or None, vmem_limit_bytes=VMEM_LIMIT
    )


def layer_norm(values):
    centred = values - jnp.mean(values, axis=-1, keepdims=True)
    return centred * lax.rsqrt(jnp.mean(centred * centred, axis=-1, keepdims=True) + NORM_EPS)


def dot(a, b, dims=(((1,), (0,)), ((), ()))):
    return lax.dot_general(a, b, dims, preferred_element_type=F32)


NT = (((1,), (1,)), ((), ()))


def cost(flops, size, transcendentals=0):
    return pl.CostEstimate(flops=flops, bytes_accessed=size, transcendentals=transcendentals)


def qkv_kernel(x_ref, seg_ref, w_hbm, out_ref, w_ref, sems):
    group = HEADS // 2 * HD
    count = w_ref.shape[0] // group
    copies = []
    for number in range(count):
        at = pl.ds(number * group, group)
        copies.append(pltpu.make_async_copy(w_hbm.at[at], w_ref.at[at], sems.at[number]))
        copies[-1].start()
    normed = layer_norm(x_ref[...].astype(F32)).astype(BF16)
    seg = seg_ref[...]
    high = seg // 64
    low = seg - high * 64
    tokens = seg.shape[1]
    row = lax.broadcasted_iota(jnp.int32, (EXT, tokens), 0)
    extra = jnp.where(row == 0, 1, jnp.where(row == 1, high, jnp.where(row == 2, low, 0)))
    extra = extra.astype(F32)
    scale = math.log2(math.e) / math.sqrt(HD)
    for number in range(count):
        copies[number].wait()
        part = dot(w_ref[number * group : (number + 1) * group, :], normed, NT)
        part = part.astype(BF16).astype(F32)
        kind = number // 2
        for i in range(HEADS // 2):
            head = number % 2 * (HEADS // 2) + i
            rows = part[i * HD : (i + 1) * HD]
            if kind == 2:
                out_ref[head, : HD + EXT] = jnp.concatenate([rows, extra], axis=0).astype(BF16)
                continue
            norm = lax.rsqrt(jnp.mean(rows * rows, axis=0, keepdims=True) + NORM_EPS)
            if kind == 0:
                out_ref[head, 2 * HD + EXT :] = (rows * (norm * scale)).astype(BF16)
            else:
                out_ref[head, HD + EXT : 2 * HD + EXT] = (rows * norm).astype(BF16)


def qkv(tokens, seg_ids, w_qkv):
    rows, width = tokens.shape
    return pl.pallas_call(
        qkv_kernel,
        out_shape=jax.ShapeDtypeStruct((HEADS, 3 * HD + EXT, rows), BF16),
        in_specs=[
            pl.BlockSpec(memory_space=pltpu.VMEM),
            pl.BlockSpec(memory_space=pltpu.VMEM),
            pl.BlockSpec(memory_space=pl.ANY),
        ],
        out_specs=pl.BlockSpec(memory_space=pltpu.VMEM),
        scratch_shapes=[
            pltpu.VMEM((w_qkv.shape[1], width), BF16),
            pltpu.SemaphoreType.DMA((6,)),
        ],
        compiler_params=cparams(),
        cost_estimate=cost(2 * rows * width * w_qkv.shape[1], 8 << 20),
        name="qkv",
    )(tokens, seg_ids.reshape(1, rows), w_qkv.T)


def attend_kernel(*refs, sets, first, last, key_block, unroll):
    q_ref = refs[0]
    kv_refs = refs[1 : 1 + sets]
    rest = refs[1 + sets :]
    if not first:
        acc_ref, rest = rest[0], rest[1:]
    out_ref, k_sc, v_sc, seg_sc = rest
    blocks, _, tokens = q_ref.shape
    top = HD + EXT
    width = LANES - HD
    for number, kv_ref in enumerate(kv_refs):
        for j in range(blocks):
            start = (number * blocks + j) * tokens
            digits = kv_ref[j, :top].astype(F32)
            seg = digits[HD + 1 : HD + 2] * 64.0 + digits[HD + 2 : HD + 3]
            keys = kv_ref[j, top : top + HD].astype(F32)
            both = jnp.concatenate([keys, jnp.broadcast_to(seg, (width, tokens))], axis=0).T
            v_sc[:, start : start + tokens] = kv_ref[j, :top]
            k_sc[start : start + tokens, :] = both.astype(BF16)
            seg_sc[start : start + tokens, :] = jnp.broadcast_to(
                both[:, HD : HD + 1], (tokens, LANES)
            )
    def tile(i):
        at_q = pl.ds(pl.multiple_of(i * tokens, tokens), tokens)
        mine = q_ref[i].astype(F32)
        q = jnp.concatenate([mine[top + HD :], jnp.zeros((width, tokens), F32)], axis=0)
        q = q.astype(BF16)
        seg = mine[HD + 1 : HD + 2] * 64.0 + mine[HD + 2 : HD + 3]
        total = None
        for start in range(0, sets * blocks * tokens, key_block):
            at = slice(start, start + key_block)
            scores = dot(k_sc[at, :], q)
            of_key = seg_sc[at, :]
            of_key = jnp.concatenate([of_key] * (tokens // LANES), axis=1)
            weights = jnp.where(of_key == seg, jnp.exp2(scores), 0.0).astype(BF16)
            part = dot(v_sc[:, at], weights)
            total = part if total is None else total + part
        if not first:
            total = total + acc_ref[:, at_q]
        if last:
            out_ref[i] = (total[:HD] / total[HD : HD + 1]).astype(BF16)
        else:
            out_ref[:, at_q] = total

    def step(i, carry):
        for j in range(unroll):
            tile(i * unroll + j)
        return carry

    lax.fori_loop(0, blocks // unroll, step, 0)


def attend(queries, sets, acc=None, last=False, key_block=512, unroll=4):
    blocks, depth, tokens = queries.shape
    total = blocks * tokens
    keys = total * len(sets)
    first = acc is None
    top = HD + EXT
    if last:
        shape = jax.ShapeDtypeStruct((blocks, HD, tokens), BF16)
    else:
        shape = jax.ShapeDtypeStruct((top, total), F32)
    operands = [queries, *sets]
    if not first:
        operands.append(acc)
    return pl.pallas_call(
        lambda *refs: attend_kernel(
            *refs, sets=len(sets), first=first, last=last, key_block=key_block, unroll=unroll
        ),
        out_shape=shape,
        in_specs=[pl.BlockSpec(memory_space=pltpu.VMEM)] * len(operands),
        out_specs=pl.BlockSpec(memory_space=pltpu.VMEM),
        scratch_shapes=[
            pltpu.VMEM((keys, LANES), BF16),
            pltpu.VMEM((top, keys), BF16),
            pltpu.VMEM((keys, LANES), F32),
        ],
        compiler_params=cparams(),
        cost_estimate=cost(4 * total * keys * LANES, 3 << 20, total * keys),
        name="attend",
    )(*operands)


def project_kernel(att_ref, x_ref, w_ref, res_ref, in_ref):
    heads, _, tokens = att_ref.shape
    att = att_ref[...].astype(F32).reshape(heads * HD, tokens).T.astype(BF16)
    residual = (x_ref[...].astype(F32) + dot(att, w_ref[...])).astype(BF16)
    res_ref[...] = residual
    in_ref[...] = layer_norm(residual.astype(F32)).astype(BF16)


def project(attended, tokens, w_attn_out):
    shape = jax.ShapeDtypeStruct(tokens.shape, BF16)
    return pl.pallas_call(
        project_kernel,
        out_shape=(shape, shape),
        in_specs=[pl.BlockSpec(memory_space=pltpu.VMEM)] * 3,
        out_specs=(pl.BlockSpec(memory_space=pltpu.VMEM),) * 2,
        compiler_params=cparams(),
        cost_estimate=cost(2 * tokens.shape[0] * w_attn_out.shape[0] * w_attn_out.shape[1], 4 << 20),
        name="project",
    )(attended, tokens, w_attn_out)


def mlp_kernel(x_ref, pair_ref, *refs):
    packs = refs[:4]
    own_ref, other_ref, near, far, sems = refs[4:]
    rows = x_ref.shape[0]
    copies = []
    for number in range(3):
        copies.append(pltpu.make_async_copy(packs[number], near.at[number], sems.at[number]))
    copies.append(pltpu.make_async_copy(packs[3], far, sems.at[3]))
    for copy in copies:
        copy.start()
    units = (near.shape[1] - PAD) // 2
    shards = far.shape[0]
    piece = (far.shape[1] - EXT) // 2
    x = x_ref[...], pair_ref[...]
    total = [None, None]
    for number in range(4):
        copies[number].wait()
        if number < 3:
            into = near[number, :units]
            out_of = near[number, units : 2 * units]
            bias = near[number, 2 * units : 2 * units + 1, :units].astype(F32)
        else:
            into = far[:, :piece].reshape(shards * piece, -1)
            out_of = far[:, piece : 2 * piece].reshape(shards * piece, -1)
            bias = far[0, 2 * piece : 2 * piece + 1, :units].astype(F32)
        before = [dot(part, into, NT) + bias for part in x]
        for i in range(2):
            pre = before[i]
            hidden = (0.5 * pre * (1.0 + lax.erf(pre * math.sqrt(0.5)))).astype(BF16)
            part = dot(hidden, out_of)
            total[i] = part if total[i] is None else total[i] + part
    own_ref[...] = total[0].astype(BF16)
    other_ref[...] = total[1].astype(BF16)


def mlp(x, pair, packs):
    rows, width = x.shape
    shape = jax.ShapeDtypeStruct((rows, width), BF16)
    vmem = pl.BlockSpec(memory_space=pltpu.VMEM)
    units = (packs[0].shape[0] - PAD) // 2
    return pl.pallas_call(
        mlp_kernel,
        out_shape=(shape, shape),
        in_specs=[vmem, vmem] + [pl.BlockSpec(memory_space=pl.ANY)] * 4,
        out_specs=(vmem, vmem),
        scratch_shapes=[
            pltpu.VMEM((3,) + packs[0].shape, BF16),
            pltpu.VMEM(packs[3].shape, BF16),
            pltpu.SemaphoreType.DMA((4,)),
        ],
        compiler_params=cparams(),
        cost_estimate=cost(2 * rows * 4 * units * width * 4, 20 << 20),
        name="mlp",
    )(x, pair, *packs)


def merge_kernel(res_ref, bias_ref, gain_ref, index_ref, owner_ref, own_ref, other_ref, out_ref, *, cap):
    rows, width = res_ref.shape
    total = own_ref[...].astype(F32) + other_ref[...].astype(F32)
    total = res_ref[...].astype(F32) + total + bias_ref[...]
    normed = (layer_norm(total) * gain_ref[...]).astype(BF16)
    count = rows // 4
    r = lax.broadcasted_iota(jnp.int32, (rows, rows), 0)
    s = lax.broadcasted_iota(jnp.int32, (rows, rows), 1)
    named = (index_ref[...] == r).astype(F32).astype(BF16)
    order = (s == 4 * (r % count) + r // count).astype(F32).astype(BF16)
    pick = dot(order, named, NT).astype(BF16)
    merged = dot(pick, normed).astype(BF16)
    for c in range(4):
        out_ref[:, c * width : (c + 1) * width] = merged[c * count : (c + 1) * count]
    across = owner_ref[...]
    r = lax.broadcasted_iota(jnp.int32, (count, count), 0)
    s = lax.broadcasted_iota(jnp.int32, (count, count), 1)
    owner = jnp.sum(jnp.where(r == s, across, 0), axis=1, keepdims=True)
    earlier = (across == owner) & (s < r)
    rank = jnp.sum(earlier.astype(jnp.int32), axis=1, keepdims=True)
    slot = (owner * cap + rank).astype(F32).astype(BF16)
    out_ref[:, 4 * width :] = jnp.broadcast_to(slot, (count, LANES))


def merge(residual, out_bias, merge_gain, merge_index, owners, own, other, cap):
    rows, width = residual.shape
    operands = (
        residual,
        out_bias.reshape(1, width),
        merge_gain.reshape(1, width),
        merge_index.reshape(1, rows),
        owners.reshape(1, rows // 4),
        own,
        other,
    )
    return pl.pallas_call(
        lambda *refs: merge_kernel(*refs, cap=cap),
        out_shape=jax.ShapeDtypeStruct((rows // 4, 4 * width + LANES), BF16),
        in_specs=[pl.BlockSpec(memory_space=pltpu.VMEM)] * len(operands),
        out_specs=pl.BlockSpec(memory_space=pltpu.VMEM),
        compiler_params=cparams(),
        cost_estimate=cost(2 * rows * rows * width, 4 << 20),
        name="merge",
    )(*operands)


def embed_kernel(group_ref, *refs, pieces, cap, slots):
    x_refs = refs[: len(pieces)]
    w_ref, bias_ref, out_ref, x_sc, acc_ref = refs[len(pieces) :]
    step = pl.program_id(0)
    steps = pl.num_programs(0)
    for (at, _), x_ref in zip(pieces, x_refs):
        x_sc[at : at + x_ref.shape[0], :] = x_ref[...]

    @pl.when(step < steps - 1)
    def _():
        part = dot(x_sc[...], w_ref[...])

        @pl.when(step == 0)
        def _():
            acc_ref[...] = part

        @pl.when(step > 0)
        def _():
            acc_ref[...] += part

    @pl.when(step == steps - 1)
    def _():
        embedded = (acc_ref[...] + bias_ref[...]).astype(BF16)
        total = x_sc.shape[0]
        count = total // 4
        slot = x_sc[:, 0:1].astype(F32).astype(jnp.int32)
        owner = slot // cap
        rank = slot - owner * cap
        shift = lax.broadcasted_iota(jnp.int32, (total, 1), 0) // count
        group = group_ref[0] + shift
        group = jnp.where(group >= 4, group - 4, group)
        target = owner * slots + group * cap + rank
        lane = lax.broadcasted_iota(jnp.int32, (total, out_ref.shape[0]), 1)
        place = (target == lane).astype(F32).T.astype(BF16)
        out_ref[...] = dot(place, embedded).astype(BF16)


def embed(group, pieces, w_merge, merge_bias, cap, slots, owners, block=1408):
    arrays = [array for _, array in pieces]
    rows = sum(array.shape[0] for array in arrays)
    depth, cols = w_merge.shape
    steps = depth // block
    places = tuple((at, array.shape[0]) for at, array in pieces)
    x_block = block

    def x_map(i, _):
        return (0, i)

    spec = lambda array: pl.BlockSpec((array.shape[0], x_block), x_map)
    return pl.pallas_call(
        lambda *refs: embed_kernel(*refs, pieces=places, cap=cap, slots=slots),
        out_shape=jax.ShapeDtypeStruct((owners * slots, cols), BF16),
        grid_spec=pltpu.PrefetchScalarGridSpec(
            num_scalar_prefetch=1,
            grid=(steps + 1,),
            in_specs=[spec(array) for array in arrays]
            + [
                pl.BlockSpec((block, cols), lambda i, _: (jnp.minimum(i, steps - 1), 0)),
                pl.BlockSpec((1, cols), lambda i, _: (0, 0)),
            ],
            out_specs=pl.BlockSpec((owners * slots, cols), lambda i, _: (0, 0)),
            scratch_shapes=[pltpu.VMEM((rows, block), BF16), pltpu.VMEM((rows, cols), F32)],
        ),
        compiler_params=cparams("arbitrary"),
        cost_estimate=cost(2 * rows * depth * cols, 10 << 20),
        name="embed",
    )(group, *arrays, w_merge, merge_bias.reshape(1, cols))


def flip(value, axis):
    return lax.ppermute(value, axis, [(0, 1), (1, 0)])


def turn(value, axis, by):
    size = lax.axis_size(axis)
    return lax.ppermute(value, axis, [(i, (i + by) % size) for i in range(size)])


def ring_gather(value, axis):
    before = turn(value, axis, 1)
    after = turn(value, axis, -1)
    half = value.shape[0] // 2
    return before, after, turn(before[:half], axis, 1), turn(after[half:], axis, -1)


def pack_kernel(place_ref, in_ref, bias_ref, out_ref, near_ref, far_ref, row_sc, sems):
    half = (near_ref.shape[0] - PAD) // 2
    share = (far_ref.shape[0] - EXT) // 2
    core = place_ref[0]
    first = pl.multiple_of(core * half, half)
    at = pl.multiple_of(first + place_ref[1] * share, 16)
    width = in_ref.shape[1]
    bias = bias_ref[...].astype(F32)
    bias = jnp.where(core == 0, bias[:, :half], bias[:, half:])
    bias = jnp.concatenate([bias, jnp.zeros((1, width - half), F32)], axis=1)
    row_sc[...] = jnp.broadcast_to(bias, row_sc.shape).astype(BF16)
    moves = [
        (in_ref.at[pl.ds(first, half)], near_ref.at[pl.ds(0, half)]),
        (out_ref.at[pl.ds(first, half)], near_ref.at[pl.ds(half, half)]),
        (in_ref.at[pl.ds(at, share)], far_ref.at[pl.ds(0, share)]),
        (out_ref.at[pl.ds(at, share)], far_ref.at[pl.ds(share, share)]),
        (row_sc, near_ref.at[pl.ds(2 * half, PAD)]),
        (row_sc.at[pl.ds(0, EXT)], far_ref.at[pl.ds(2 * share, EXT)]),
    ]
    copies = [
        pltpu.make_async_copy(source, target, sems.at[i])
        for i, (source, target) in enumerate(moves)
    ]
    for copy in copies:
        copy.start()
    for copy in copies:
        copy.wait()


def pack(place, w_in, in_bias, w_out, shares):
    units, width = w_in.shape
    half = units // 2
    any_space = pl.BlockSpec(memory_space=pl.ANY)
    return pl.pallas_call(
        pack_kernel,
        out_shape=(
            jax.ShapeDtypeStruct((2 * half + PAD, width), BF16),
            jax.ShapeDtypeStruct((2 * half // shares + EXT, width), BF16),
        ),
        in_specs=[
            pl.BlockSpec(memory_space=pltpu.SMEM),
            any_space,
            pl.BlockSpec(memory_space=pltpu.VMEM),
            any_space,
        ],
        out_specs=(any_space, any_space),
        scratch_shapes=[pltpu.VMEM((PAD, width), BF16), pltpu.SemaphoreType.DMA((6,))],
        compiler_params=cparams(),
        cost_estimate=cost(0, 9 << 20),
        name="pack",
    )(place, w_in, in_bias.reshape(1, units), w_out)


def local(
    tokens,
    seg_ids,
    merge_index,
    owners,
    w_qkv,
    w_attn_out,
    w_in,
    in_bias,
    w_out,
    out_bias,
    merge_gain,
    w_merge,
    merge_bias,
):
    chips = ("y", "xh", "xl")
    place = jnp.stack([lax.axis_index("c"), lax.axis_index(chips)]).astype(jnp.int32)
    near, far = pack(place, w_in, in_bias, w_out, lax.axis_size(chips))
    far = turn(far, "grp", 2)
    one, two = turn(near, "grp", 1), turn(near, "grp", -1)
    heads = qkv(tokens, seg_ids, w_qkv)
    far, heads = lax.optimization_barrier((far, heads))
    far = lax.all_gather(far, chips)
    mine = lax.all_to_all(heads, ("y", "xh"), 0, 0, tiled=True)
    kv = mine[:, : 2 * HD + EXT]
    kv_x = flip(kv, "xl")
    kv_c = flip(kv, "c")
    acc = attend(mine, [mine])
    kv_c, acc = lax.optimization_barrier((kv_c, acc))
    acc = attend(mine, [kv_c], acc)
    kv_x, acc = lax.optimization_barrier((kv_x, acc))
    kv_xc = flip(kv_x, "c")
    acc = attend(mine, [kv_x], acc)
    done = attend(mine, [kv_xc], acc, last=True)
    attended = lax.all_to_all(done, ("y", "xh"), 0, 0, tiled=True)
    residual, mlp_in = project(attended, tokens, w_attn_out)
    own, other = mlp(mlp_in, flip(mlp_in, "c"), (near, one, two, far))
    owner_count = lax.axis_size(("y", "xh", "xl", "c"))
    cap = 4
    merged = merge(
        residual, out_bias, merge_gain, merge_index, owners, own, flip(other, "c"), cap
    )
    count = merged.shape[0]
    before, after, far_a, far_b = ring_gather(merged, "grp")
    pieces = [
        (0, merged),
        (count, after),
        (2 * count, far_a),
        (2 * count + count // 2, far_b),
        (3 * count, before),
    ]
    group = lax.axis_index("grp").reshape(1).astype(jnp.int32)
    slots = 4 * cap
    outgoing = embed(group, pieces, w_merge, merge_bias, cap, slots, owner_count)
    cols = outgoing.shape[1]
    outgoing = outgoing.reshape(owner_count, 4, cap, cols)
    received = lax.all_to_all(
        outgoing, ("y", "xh", "xl", "c"), split_axis=0, concat_axis=2, tiled=True
    )
    return received.reshape(4 * owner_count * cap, cols)


def solution(mesh):
    inner = Mesh(mesh.devices.reshape(4, 4, 2, 2, 2), ("grp", "y", "xh", "xl", "c"))
    every = ("grp", "y", "xh", "xl", "c")
    tok = ("y", "xh", "xl", "c")
    placed = (
        P(every, None),
        P(every),
        P(every),
        P(every, None),
        P(),
        P(),
        P("grp", None),
        P("grp"),
        P("grp", None),
        P(),
        P(),
        P(None, "grp"),
        P("grp"),
    )
    return jax.shard_map(
        local, mesh=inner, in_specs=placed, out_specs=P(tok, "grp"), check_vma=False
    )
```

```python
import math

import jax
import jax.numpy as jnp
from jax import lax
from jax.experimental import pallas as pl
from jax.experimental.pallas import tpu as pltpu
from jax.sharding import Mesh
from jax.sharding import PartitionSpec as P

HEADS = 8
HD = 88
EXT = 8
NORM_EPS = 1e-06
LANES = 128
PAD = 16
F32 = jnp.float32
BF16 = jnp.bfloat16
VMEM_LIMIT = 60 * 1024 * 1024


def cparams(*semantics):
    return pltpu.CompilerParams(
        dimension_semantics=semantics or None, vmem_limit_bytes=VMEM_LIMIT
    )


def layer_norm(values):
    centred = values - jnp.mean(values, axis=-1, keepdims=True)
    return centred * lax.rsqrt(jnp.mean(centred * centred, axis=-1, keepdims=True) + NORM_EPS)


def dot(a, b, dims=(((1,), (0,)), ((), ()))):
    return lax.dot_general(a, b, dims, preferred_element_type=F32)


NT = (((1,), (1,)), ((), ()))


def cost(flops, size, transcendentals=0):
    return pl.CostEstimate(flops=flops, bytes_accessed=size, transcendentals=transcendentals)


def qkv_kernel(x_ref, seg_ref, w_hbm, out_ref, w_ref, sems):
    group = HEADS // 2 * HD
    count = w_ref.shape[0] // group
    copies = []
    for number in range(count):
        at = pl.ds(number * group, group)
        copies.append(pltpu.make_async_copy(w_hbm.at[at], w_ref.at[at], sems.at[number]))
        copies[-1].start()
    normed = layer_norm(x_ref[...].astype(F32)).astype(BF16)
    seg = seg_ref[...]
    high = seg // 64
    low = seg - high * 64
    tokens = seg.shape[1]
    row = lax.broadcasted_iota(jnp.int32, (EXT, tokens), 0)
    extra = jnp.where(row == 0, 1, jnp.where(row == 1, high, jnp.where(row == 2, low, 0)))
    extra = extra.astype(F32)
    scale = math.log2(math.e) / math.sqrt(HD)
    for number in range(count):
        copies[number].wait()
        part = dot(w_ref[number * group : (number + 1) * group, :], normed, NT)
        part = part.astype(BF16).astype(F32)
        kind = number // 2
        for i in range(HEADS // 2):
            head = number % 2 * (HEADS // 2) + i
            rows = part[i * HD : (i + 1) * HD]
            if kind == 2:
                out_ref[head, HD : 2 * HD + EXT] = jnp.concatenate([extra, rows], axis=0).astype(
                    BF16
                )
                continue
            norm = lax.rsqrt(jnp.mean(rows * rows, axis=0, keepdims=True) + NORM_EPS)
            if kind == 0:
                out_ref[head, :HD] = (rows * (norm * scale)).astype(BF16)
            else:
                out_ref[head, 2 * HD + EXT :] = (rows * norm).astype(BF16)


def qkv(tokens, seg_ids, w_qkv):
    rows, width = tokens.shape
    return pl.pallas_call(
        qkv_kernel,
        out_shape=jax.ShapeDtypeStruct((HEADS, 3 * HD + EXT, rows), BF16),
        in_specs=[
            pl.BlockSpec(memory_space=pltpu.VMEM),
            pl.BlockSpec(memory_space=pltpu.VMEM),
            pl.BlockSpec(memory_space=pl.ANY),
        ],
        out_specs=pl.BlockSpec(memory_space=pltpu.VMEM),
        scratch_shapes=[
            pltpu.VMEM((w_qkv.shape[1], width), BF16),
            pltpu.SemaphoreType.DMA((6,)),
        ],
        compiler_params=cparams(),
        cost_estimate=cost(2 * rows * width * w_qkv.shape[1], 8 << 20),
        name="qkv",
    )(tokens, seg_ids.reshape(1, rows), w_qkv.T)


def attend_kernel(*refs, sets, first, send, key_block, unroll):
    q_ref = refs[0]
    kv_refs = refs[1 : 1 + sets]
    rest = refs[1 + sets :]
    if not first:
        acc_ref, rest = rest[0], rest[1:]
    out_ref, k_sc, v_sc, seg_sc = rest
    blocks, top, tokens = q_ref.shape
    width = LANES - HD
    for number, kv_ref in enumerate(kv_refs):
        for j in range(blocks):
            start = (number * blocks + j) * tokens
            digits = kv_ref[j, : 2 * EXT].astype(F32)
            seg = digits[1:2] * 64.0 + digits[2:3]
            keys = kv_ref[j, top:].astype(F32)
            both = jnp.concatenate([keys, jnp.broadcast_to(seg, (width, tokens))], axis=0).T
            v_sc[:, start : start + tokens] = kv_ref[j, :top]
            k_sc[start : start + tokens, :] = both.astype(BF16)
            seg_sc[start : start + tokens, :] = jnp.broadcast_to(
                both[:, HD : HD + 1], (tokens, LANES)
            )

    def tile(i):
        at_q = pl.ds(pl.multiple_of(i * tokens, tokens), tokens)
        mine = q_ref[i].astype(F32)
        q = jnp.concatenate([mine[:HD], jnp.zeros((width, tokens), F32)], axis=0).astype(BF16)
        seg = mine[HD + 1 : HD + 2] * 64.0 + mine[HD + 2 : HD + 3]
        total = None
        for start in range(0, sets * blocks * tokens, key_block):
            at = slice(start, start + key_block)
            scores = dot(k_sc[at, :], q)
            of_key = seg_sc[at, :]
            of_key = jnp.concatenate([of_key] * (tokens // LANES), axis=1)
            weights = jnp.where(of_key == seg, jnp.exp2(scores), 0.0).astype(BF16)
            part = dot(v_sc[:, at], weights)
            total = part if total is None else total + part
        if not first:
            total = total + acc_ref[:, at_q]
        if send:
            near = total[:1].astype(BF16).astype(F32)
            rows = [near, total[:1] - near, jnp.zeros((EXT - 2, tokens), F32), total[EXT:]]
            out_ref[i] = jnp.concatenate(rows, axis=0).astype(BF16)
        else:
            out_ref[:, at_q] = total

    def step(i, carry):
        for j in range(unroll):
            tile(i * unroll + j)
        return carry

    lax.fori_loop(0, blocks // unroll, step, 0)


def attend(queries, sets, acc=None, send=False, key_block=512, unroll=4):
    blocks, top, tokens = queries.shape
    total = blocks * tokens
    keys = total * len(sets)
    first = acc is None
    if send:
        shape = jax.ShapeDtypeStruct(queries.shape, BF16)
    else:
        shape = jax.ShapeDtypeStruct((top, total), F32)
    operands = [queries, *sets]
    if not first:
        operands.append(acc)
    return pl.pallas_call(
        lambda *refs: attend_kernel(
            *refs, sets=len(sets), first=first, send=send, key_block=key_block, unroll=unroll
        ),
        out_shape=shape,
        in_specs=[pl.BlockSpec(memory_space=pltpu.VMEM)] * len(operands),
        out_specs=pl.BlockSpec(memory_space=pltpu.VMEM),
        scratch_shapes=[
            pltpu.VMEM((keys, LANES), BF16),
            pltpu.VMEM((top, keys), BF16),
            pltpu.VMEM((keys, LANES), F32),
        ],
        compiler_params=cparams(),
        cost_estimate=cost(4 * total * keys * LANES, 3 << 20, total * keys),
        name="attend",
    )(*operands)


def combine_kernel(acc_ref, sent_ref, out_ref):
    blocks, _, tokens = sent_ref.shape
    for i in range(blocks):
        acc = acc_ref[:, i * tokens : (i + 1) * tokens]
        sent = sent_ref[i].astype(F32)
        weight = acc[:1] + (sent[:1] + sent[1:2])
        out_ref[i] = ((acc[EXT:] + sent[EXT:]) / weight).astype(BF16)


def combine(acc, sent):
    blocks, top, tokens = sent.shape
    return pl.pallas_call(
        combine_kernel,
        out_shape=jax.ShapeDtypeStruct((blocks, top - EXT, tokens), BF16),
        in_specs=[pl.BlockSpec(memory_space=pltpu.VMEM)] * 2,
        out_specs=pl.BlockSpec(memory_space=pltpu.VMEM),
        compiler_params=cparams(),
        cost_estimate=cost(0, 2 << 20),
        name="combine",
    )(acc, sent)


def project_kernel(att_ref, x_ref, w_ref, res_ref, in_ref):
    heads, _, tokens = att_ref.shape
    att = att_ref[...].astype(F32).reshape(heads * HD, tokens).T.astype(BF16)
    residual = (x_ref[...].astype(F32) + dot(att, w_ref[...])).astype(BF16)
    res_ref[...] = residual
    in_ref[...] = layer_norm(residual.astype(F32)).astype(BF16)


def project(attended, tokens, w_attn_out):
    shape = jax.ShapeDtypeStruct(tokens.shape, BF16)
    return pl.pallas_call(
        project_kernel,
        out_shape=(shape, shape),
        in_specs=[pl.BlockSpec(memory_space=pltpu.VMEM)] * 3,
        out_specs=(pl.BlockSpec(memory_space=pltpu.VMEM),) * 2,
        compiler_params=cparams(),
        cost_estimate=cost(2 * tokens.shape[0] * w_attn_out.shape[0] * w_attn_out.shape[1], 4 << 20),
        name="project",
    )(attended, tokens, w_attn_out)


def mlp_kernel(x_ref, pair_ref, *refs):
    packs = refs[:4]
    own_ref, other_ref, near, far, sems = refs[4:]
    rows = x_ref.shape[0]
    copies = []
    for number in range(3):
        copies.append(pltpu.make_async_copy(packs[number], near.at[number], sems.at[number]))
    copies.append(pltpu.make_async_copy(packs[3], far, sems.at[3]))
    for copy in copies:
        copy.start()
    units = (near.shape[1] - PAD) // 2
    shards = far.shape[0]
    piece = (far.shape[1] - EXT) // 2
    x = x_ref[...], pair_ref[...]
    total = [None, None]
    for number in range(4):
        copies[number].wait()
        if number < 3:
            into = near[number, :units]
            out_of = near[number, units : 2 * units]
            bias = near[number, 2 * units : 2 * units + 1, :units].astype(F32)
        else:
            into = far[:, :piece].reshape(shards * piece, -1)
            out_of = far[:, piece : 2 * piece].reshape(shards * piece, -1)
            bias = far[0, 2 * piece : 2 * piece + 1, :units].astype(F32)
        before = [dot(part, into, NT) + bias for part in x]
        for i in range(2):
            pre = before[i]
            hidden = (0.5 * pre * (1.0 + lax.erf(pre * math.sqrt(0.5)))).astype(BF16)
            part = dot(hidden, out_of)
            total[i] = part if total[i] is None else total[i] + part
    own_ref[...] = total[0].astype(BF16)
    other_ref[...] = total[1].astype(BF16)


def mlp(x, pair, packs):
    rows, width = x.shape
    shape = jax.ShapeDtypeStruct((rows, width), BF16)
    vmem = pl.BlockSpec(memory_space=pltpu.VMEM)
    units = (packs[0].shape[0] - PAD) // 2
    return pl.pallas_call(
        mlp_kernel,
        out_shape=(shape, shape),
        in_specs=[vmem, vmem] + [pl.BlockSpec(memory_space=pl.ANY)] * 4,
        out_specs=(vmem, vmem),
        scratch_shapes=[
            pltpu.VMEM((3,) + packs[0].shape, BF16),
            pltpu.VMEM(packs[3].shape, BF16),
            pltpu.SemaphoreType.DMA((4,)),
        ],
        compiler_params=cparams(),
        cost_estimate=cost(2 * rows * 4 * units * width * 4, 20 << 20),
        name="mlp",
    )(x, pair, *packs)


def merge_kernel(res_ref, bias_ref, gain_ref, index_ref, owner_ref, own_ref, other_ref, out_ref, *, cap):
    rows, width = res_ref.shape
    total = own_ref[...].astype(F32) + other_ref[...].astype(F32)
    total = res_ref[...].astype(F32) + total + bias_ref[...]
    normed = (layer_norm(total) * gain_ref[...]).astype(BF16)
    count = rows // 4
    r = lax.broadcasted_iota(jnp.int32, (rows, rows), 0)
    s = lax.broadcasted_iota(jnp.int32, (rows, rows), 1)
    named = (index_ref[...] == r).astype(F32).astype(BF16)
    order = (s == 4 * (r % count) + r // count).astype(F32).astype(BF16)
    pick = dot(order, named, NT).astype(BF16)
    merged = dot(pick, normed).astype(BF16)
    for c in range(4):
        out_ref[:, c * width : (c + 1) * width] = merged[c * count : (c + 1) * count]
    across = owner_ref[...]
    r = lax.broadcasted_iota(jnp.int32, (count, count), 0)
    s = lax.broadcasted_iota(jnp.int32, (count, count), 1)
    owner = jnp.sum(jnp.where(r == s, across, 0), axis=1, keepdims=True)
    earlier = (across == owner) & (s < r)
    rank = jnp.sum(earlier.astype(jnp.int32), axis=1, keepdims=True)
    slot = (owner * cap + rank).astype(F32).astype(BF16)
    out_ref[:, 4 * width :] = jnp.broadcast_to(slot, (count, LANES))


def merge(residual, out_bias, merge_gain, merge_index, owners, own, other, cap):
    rows, width = residual.shape
    operands = (
        residual,
        out_bias.reshape(1, width),
        merge_gain.reshape(1, width),
        merge_index.reshape(1, rows),
        owners.reshape(1, rows // 4),
        own,
        other,
    )
    return pl.pallas_call(
        lambda *refs: merge_kernel(*refs, cap=cap),
        out_shape=jax.ShapeDtypeStruct((rows // 4, 4 * width + LANES), BF16),
        in_specs=[pl.BlockSpec(memory_space=pltpu.VMEM)] * len(operands),
        out_specs=pl.BlockSpec(memory_space=pltpu.VMEM),
        compiler_params=cparams(),
        cost_estimate=cost(2 * rows * rows * width, 4 << 20),
        name="merge",
    )(*operands)


def embed_kernel(group_ref, *refs, pieces, cap, slots):
    x_refs = refs[: len(pieces)]
    w_ref, bias_ref, out_ref, x_sc, acc_ref = refs[len(pieces) :]
    step = pl.program_id(0)
    steps = pl.num_programs(0)
    for (at, _), x_ref in zip(pieces, x_refs):
        x_sc[at : at + x_ref.shape[0], :] = x_ref[...]

    @pl.when(step < steps - 1)
    def _():
        part = dot(x_sc[...], w_ref[...])

        @pl.when(step == 0)
        def _():
            acc_ref[...] = part

        @pl.when(step > 0)
        def _():
            acc_ref[...] += part

    @pl.when(step == steps - 1)
    def _():
        embedded = (acc_ref[...] + bias_ref[...]).astype(BF16)
        total = x_sc.shape[0]
        count = total // 4
        slot = x_sc[:, 0:1].astype(F32).astype(jnp.int32)
        owner = slot // cap
        rank = slot - owner * cap
        shift = lax.broadcasted_iota(jnp.int32, (total, 1), 0) // count
        group = group_ref[0] + shift
        group = jnp.where(group >= 4, group - 4, group)
        target = owner * slots + group * cap + rank
        lane = lax.broadcasted_iota(jnp.int32, (total, out_ref.shape[0]), 1)
        place = (target == lane).astype(F32).T.astype(BF16)
        out_ref[...] = dot(place, embedded).astype(BF16)


def embed(group, pieces, w_merge, merge_bias, cap, slots, owners, block=1408):
    arrays = [array for _, array in pieces]
    rows = sum(array.shape[0] for array in arrays)
    depth, cols = w_merge.shape
    steps = depth // block
    places = tuple((at, array.shape[0]) for at, array in pieces)
    x_block = block

    def x_map(i, _):
        return (0, i)

    spec = lambda array: pl.BlockSpec((array.shape[0], x_block), x_map)
    return pl.pallas_call(
        lambda *refs: embed_kernel(*refs, pieces=places, cap=cap, slots=slots),
        out_shape=jax.ShapeDtypeStruct((owners * slots, cols), BF16),
        grid_spec=pltpu.PrefetchScalarGridSpec(
            num_scalar_prefetch=1,
            grid=(steps + 1,),
            in_specs=[spec(array) for array in arrays]
            + [
                pl.BlockSpec((block, cols), lambda i, _: (jnp.minimum(i, steps - 1), 0)),
                pl.BlockSpec((1, cols), lambda i, _: (0, 0)),
            ],
            out_specs=pl.BlockSpec((owners * slots, cols), lambda i, _: (0, 0)),
            scratch_shapes=[pltpu.VMEM((rows, block), BF16), pltpu.VMEM((rows, cols), F32)],
        ),
        compiler_params=cparams("arbitrary"),
        cost_estimate=cost(2 * rows * depth * cols, 10 << 20),
        name="embed",
    )(group, *arrays, w_merge, merge_bias.reshape(1, cols))


def flip(value, axis):
    return lax.ppermute(value, axis, [(0, 1), (1, 0)])


def turn(value, axis, by):
    size = lax.axis_size(axis)
    return lax.ppermute(value, axis, [(i, (i + by) % size) for i in range(size)])


def ring_gather(value, axis):
    before = turn(value, axis, 1)
    after = turn(value, axis, -1)
    half = value.shape[0] // 2
    return before, after, turn(before[:half], axis, 1), turn(after[half:], axis, -1)


def pack_kernel(place_ref, in_ref, bias_ref, out_ref, near_ref, far_ref, row_sc, near_sc, far_sc, sems):
    half = (near_ref.shape[0] - PAD) // 2
    share = (far_ref.shape[0] - EXT) // 2
    core = place_ref[0]
    first = pl.multiple_of(core * half, half)
    at = pl.multiple_of(first + place_ref[1] * share, 16)
    width = in_ref.shape[1]
    bias = bias_ref[...].astype(F32)
    bias = jnp.where(core == 0, bias[:, :half], bias[:, half:])
    bias = jnp.concatenate([bias, jnp.zeros((1, width - half), F32)], axis=1)
    row_sc[...] = jnp.broadcast_to(bias, row_sc.shape).astype(BF16)
    pieces = [
        (in_ref, first, 0, half, near_ref, near_sc),
        (out_ref, first, half, half, near_ref, near_sc),
        (in_ref, at, 0, share, far_ref, far_sc),
        (out_ref, at, share, share, far_ref, far_sc),
    ]
    inward = []
    for i, (source, begin, to, size, _, buffer) in enumerate(pieces):
        copy = pltpu.make_async_copy(
            source.at[pl.ds(begin, size)], buffer.at[pl.ds(to, size)], sems.at[i]
        )
        copy.start()
        inward.append(copy)
    outward = [
        pltpu.make_async_copy(row_sc, near_ref.at[pl.ds(2 * half, PAD)], sems.at[8]),
        pltpu.make_async_copy(
            row_sc.at[pl.ds(0, EXT)], far_ref.at[pl.ds(2 * share, EXT)], sems.at[9]
        ),
    ]
    outward[0].start()
    outward[1].start()
    for i in (2, 3, 0, 1):
        _, _, to, size, target, buffer = pieces[i]
        inward[i].wait()
        copy = pltpu.make_async_copy(
            buffer.at[pl.ds(to, size)], target.at[pl.ds(to, size)], sems.at[4 + i]
        )
        copy.start()
        outward.append(copy)
    for copy in outward:
        copy.wait()


def pack(place, w_in, in_bias, w_out, shares):
    units, width = w_in.shape
    half = units // 2
    any_space = pl.BlockSpec(memory_space=pl.ANY)
    return pl.pallas_call(
        pack_kernel,
        out_shape=(
            jax.ShapeDtypeStruct((2 * half + PAD, width), BF16),
            jax.ShapeDtypeStruct((2 * half // shares + EXT, width), BF16),
        ),
        in_specs=[
            pl.BlockSpec(memory_space=pltpu.SMEM),
            any_space,
            pl.BlockSpec(memory_space=pltpu.VMEM),
            any_space,
        ],
        out_specs=(any_space, any_space),
        scratch_shapes=[
            pltpu.VMEM((PAD, width), BF16),
            pltpu.VMEM((2 * half, width), BF16),
            pltpu.VMEM((2 * half // shares, width), BF16),
            pltpu.SemaphoreType.DMA((10,)),
        ],
        compiler_params=cparams(),
        cost_estimate=cost(0, 9 << 20),
        name="pack",
    )(place, w_in, in_bias.reshape(1, units), w_out)


def local(
    tokens,
    seg_ids,
    merge_index,
    owners,
    w_qkv,
    w_attn_out,
    w_in,
    in_bias,
    w_out,
    out_bias,
    merge_gain,
    w_merge,
    merge_bias,
):
    chips = ("y", "xh", "xl")
    place = jnp.stack([lax.axis_index("c"), lax.axis_index(chips)]).astype(jnp.int32)
    near, far = pack(place, w_in, in_bias, w_out, lax.axis_size(chips))
    far = turn(far, "grp", 2)
    one, two = turn(near, "grp", 1), turn(near, "grp", -1)
    heads = qkv(tokens, seg_ids, w_qkv)
    far, heads = lax.optimization_barrier((far, heads))
    far = lax.all_gather(far, chips)
    mine = lax.all_to_all(heads, ("y", "xh"), 0, 0, tiled=True)
    queries, kv = mine[:, : HD + EXT], mine[:, HD:]
    away = flip(queries, "xl")
    kv_c = flip(kv, "c")
    acc = attend(queries, [kv])
    away, kv_c, acc = lax.optimization_barrier((away, kv_c, acc))
    sent = flip(attend(away, [kv, kv_c], send=True), "xl")
    acc = attend(queries, [kv_c], acc)
    sent, acc = lax.optimization_barrier((sent, acc))
    done = combine(acc, sent)
    attended = lax.all_to_all(done, ("y", "xh"), 0, 0, tiled=True)
    residual, mlp_in = project(attended, tokens, w_attn_out)
    own, other = mlp(mlp_in, flip(mlp_in, "c"), (near, one, two, far))
    owner_count = lax.axis_size(("y", "xh", "xl", "c"))
    cap = 4
    merged = merge(
        residual, out_bias, merge_gain, merge_index, owners, own, flip(other, "c"), cap
    )
    count = merged.shape[0]
    before, after, far_a, far_b = ring_gather(merged, "grp")
    pieces = [
        (0, merged),
        (count, after),
        (2 * count, far_a),
        (2 * count + count // 2, far_b),
        (3 * count, before),
    ]
    group = lax.axis_index("grp").reshape(1).astype(jnp.int32)
    slots = 4 * cap
    outgoing = embed(group, pieces, w_merge, merge_bias, cap, slots, owner_count)
    cols = outgoing.shape[1]
    outgoing = outgoing.reshape(owner_count, 4, cap, cols)
    received = lax.all_to_all(
        outgoing, ("y", "xh", "xl", "c"), split_axis=0, concat_axis=2, tiled=True
    )
    return received.reshape(4 * owner_count * cap, cols)


def solution(mesh):
    inner = Mesh(mesh.devices.reshape(4, 4, 2, 2, 2), ("grp", "y", "xh", "xl", "c"))
    every = ("grp", "y", "xh", "xl", "c")
    tok = ("y", "xh", "xl", "c")
    placed = (
        P(every, None),
        P(every),
        P(every),
        P(every, None),
        P(),
        P(),
        P("grp", None),
        P("grp"),
        P("grp", None),
        P(),
        P(),
        P(None, "grp"),
        P("grp"),
    )
    return jax.shard_map(
        local, mesh=inner, in_specs=placed, out_specs=P(tok, "grp"), check_vma=False
    )
```

```python
import math

import jax
import jax.numpy as jnp
from jax import lax
from jax.experimental import pallas as pl
from jax.experimental.pallas import tpu as pltpu
from jax.sharding import Mesh
from jax.sharding import PartitionSpec as P

HEADS = 8
HD = 88
EXT = 8
NORM_EPS = 1e-06
LANES = 128
PAD = 16
CHIPS = ("y", "xh", "xl")
F32 = jnp.float32
BF16 = jnp.bfloat16
VMEM_LIMIT = 60 * 1024 * 1024


def cparams(*semantics):
    return pltpu.CompilerParams(
        dimension_semantics=semantics or None, vmem_limit_bytes=VMEM_LIMIT
    )


def layer_norm(values):
    centred = values - jnp.mean(values, axis=-1, keepdims=True)
    return centred * lax.rsqrt(jnp.mean(centred * centred, axis=-1, keepdims=True) + NORM_EPS)


def dot(a, b, dims=(((1,), (0,)), ((), ()))):
    return lax.dot_general(a, b, dims, preferred_element_type=F32)


NT = (((1,), (1,)), ((), ()))


def cost(flops, size, transcendentals=0):
    return pl.CostEstimate(flops=flops, bytes_accessed=size, transcendentals=transcendentals)


def qkv_kernel(x_ref, seg_ref, w_hbm, out_ref, w_ref, sems):
    group = HEADS // 2 * HD
    count = w_ref.shape[0] // group
    copies = []
    for number in range(count):
        at = pl.ds(number * group, group)
        copies.append(pltpu.make_async_copy(w_hbm.at[at], w_ref.at[at], sems.at[number]))
        copies[-1].start()
    normed = layer_norm(x_ref[...].astype(F32)).astype(BF16)
    seg = seg_ref[...]
    high = seg // 64
    low = seg - high * 64
    tokens = seg.shape[1]
    row = lax.broadcasted_iota(jnp.int32, (EXT, tokens), 0)
    extra = jnp.where(row == 0, 1, jnp.where(row == 1, high, jnp.where(row == 2, low, 0)))
    extra = extra.astype(F32)
    scale = math.log2(math.e) / math.sqrt(HD)
    for number in range(count):
        copies[number].wait()
        part = dot(w_ref[number * group : (number + 1) * group, :], normed, NT)
        part = part.astype(BF16).astype(F32)
        kind = number // 2
        for i in range(HEADS // 2):
            head = number % 2 * (HEADS // 2) + i
            rows = part[i * HD : (i + 1) * HD]
            if kind == 2:
                out_ref[head, HD : 2 * HD + EXT] = jnp.concatenate([extra, rows], axis=0).astype(
                    BF16
                )
                continue
            norm = lax.rsqrt(jnp.mean(rows * rows, axis=0, keepdims=True) + NORM_EPS)
            if kind == 0:
                out_ref[head, :HD] = (rows * (norm * scale)).astype(BF16)
            else:
                out_ref[head, 2 * HD + EXT :] = (rows * norm).astype(BF16)


def qkv(tokens, seg_ids, w_qkv):
    rows, width = tokens.shape
    return pl.pallas_call(
        qkv_kernel,
        out_shape=jax.ShapeDtypeStruct((HEADS, 3 * HD + EXT, rows), BF16),
        in_specs=[
            pl.BlockSpec(memory_space=pltpu.VMEM),
            pl.BlockSpec(memory_space=pltpu.VMEM),
            pl.BlockSpec(memory_space=pl.ANY),
        ],
        out_specs=pl.BlockSpec(memory_space=pltpu.VMEM),
        scratch_shapes=[
            pltpu.VMEM((w_qkv.shape[1], width), BF16),
            pltpu.SemaphoreType.DMA((6,)),
        ],
        compiler_params=cparams(),
        cost_estimate=cost(2 * rows * width * w_qkv.shape[1], 8 << 20),
        name="qkv",
    )(tokens, seg_ids.reshape(1, rows), w_qkv.T)


def attend_kernel(*refs, sets, first, send, key_block, unroll):
    q_ref = refs[0]
    kv_refs = refs[1 : 1 + sets]
    rest = refs[1 + sets :]
    if not first:
        acc_ref, rest = rest[0], rest[1:]
    out_ref, k_sc, v_sc, seg_sc = rest
    blocks, top, tokens = q_ref.shape
    width = LANES - HD
    for number, kv_ref in enumerate(kv_refs):
        for j in range(blocks):
            start = (number * blocks + j) * tokens
            digits = kv_ref[j, : 2 * EXT].astype(F32)
            seg = digits[1:2] * 64.0 + digits[2:3]
            keys = kv_ref[j, top:].astype(F32)
            both = jnp.concatenate([keys, jnp.broadcast_to(seg, (width, tokens))], axis=0).T
            v_sc[:, start : start + tokens] = kv_ref[j, :top]
            k_sc[start : start + tokens, :] = both.astype(BF16)
            seg_sc[start : start + tokens, :] = jnp.broadcast_to(
                both[:, HD : HD + 1], (tokens, LANES)
            )

    def tile(i):
        at_q = pl.ds(pl.multiple_of(i * tokens, tokens), tokens)
        mine = q_ref[i].astype(F32)
        q = jnp.concatenate([mine[:HD], jnp.zeros((width, tokens), F32)], axis=0).astype(BF16)
        seg = mine[HD + 1 : HD + 2] * 64.0 + mine[HD + 2 : HD + 3]
        total = None
        for start in range(0, sets * blocks * tokens, key_block):
            at = slice(start, start + key_block)
            scores = dot(k_sc[at, :], q)
            of_key = seg_sc[at, :]
            of_key = jnp.concatenate([of_key] * (tokens // LANES), axis=1)
            weights = jnp.where(of_key == seg, jnp.exp2(scores), 0.0).astype(BF16)
            part = dot(v_sc[:, at], weights)
            total = part if total is None else total + part
        if not first:
            total = total + acc_ref[:, at_q]
        if send:
            near = total[:1].astype(BF16).astype(F32)
            rows = [near, total[:1] - near, jnp.zeros((EXT - 2, tokens), F32), total[EXT:]]
            out_ref[i] = jnp.concatenate(rows, axis=0).astype(BF16)
        else:
            out_ref[:, at_q] = total

    def step(i, carry):
        for j in range(unroll):
            tile(i * unroll + j)
        return carry

    lax.fori_loop(0, blocks // unroll, step, 0)


def attend(queries, sets, acc=None, send=False, key_block=512, unroll=4):
    blocks, top, tokens = queries.shape
    total = blocks * tokens
    keys = total * len(sets)
    first = acc is None
    if send:
        shape = jax.ShapeDtypeStruct(queries.shape, BF16)
    else:
        shape = jax.ShapeDtypeStruct((top, total), F32)
    operands = [queries, *sets]
    if not first:
        operands.append(acc)
    return pl.pallas_call(
        lambda *refs: attend_kernel(
            *refs, sets=len(sets), first=first, send=send, key_block=key_block, unroll=unroll
        ),
        out_shape=shape,
        in_specs=[pl.BlockSpec(memory_space=pltpu.VMEM)] * len(operands),
        out_specs=pl.BlockSpec(memory_space=pltpu.VMEM),
        scratch_shapes=[
            pltpu.VMEM((keys, LANES), BF16),
            pltpu.VMEM((top, keys), BF16),
            pltpu.VMEM((keys, LANES), F32),
        ],
        compiler_params=cparams(),
        cost_estimate=cost(4 * total * keys * LANES, 3 << 20, total * keys),
        name="attend",
    )(*operands)


def combine_kernel(acc_ref, sent_ref, out_ref):
    blocks, _, tokens = sent_ref.shape
    for i in range(blocks):
        acc = acc_ref[:, i * tokens : (i + 1) * tokens]
        sent = sent_ref[i].astype(F32)
        weight = acc[:1] + (sent[:1] + sent[1:2])
        out_ref[i] = ((acc[EXT:] + sent[EXT:]) / weight).astype(BF16)


def combine(acc, sent):
    blocks, top, tokens = sent.shape
    return pl.pallas_call(
        combine_kernel,
        out_shape=jax.ShapeDtypeStruct((blocks, top - EXT, tokens), BF16),
        in_specs=[pl.BlockSpec(memory_space=pltpu.VMEM)] * 2,
        out_specs=pl.BlockSpec(memory_space=pltpu.VMEM),
        compiler_params=cparams(),
        cost_estimate=cost(0, 2 << 20),
        name="combine",
    )(acc, sent)


def project_kernel(att_ref, x_ref, w_ref, res_ref, in_ref):
    heads, _, tokens = att_ref.shape
    att = att_ref[...].astype(F32).reshape(heads * HD, tokens).T.astype(BF16)
    residual = (x_ref[...].astype(F32) + dot(att, w_ref[...])).astype(BF16)
    res_ref[...] = residual
    in_ref[...] = layer_norm(residual.astype(F32)).astype(BF16)


def project(attended, tokens, w_attn_out):
    shape = jax.ShapeDtypeStruct(tokens.shape, BF16)
    return pl.pallas_call(
        project_kernel,
        out_shape=(shape, shape),
        in_specs=[pl.BlockSpec(memory_space=pltpu.VMEM)] * 3,
        out_specs=(pl.BlockSpec(memory_space=pltpu.VMEM),) * 2,
        compiler_params=cparams(),
        cost_estimate=cost(2 * tokens.shape[0] * w_attn_out.shape[0] * w_attn_out.shape[1], 4 << 20),
        name="project",
    )(attended, tokens, w_attn_out)


def mlp_kernel(x_ref, pair_ref, *refs, near_count, far_count):
    near_refs, far_refs = refs[:near_count], refs[near_count : near_count + far_count]
    rest = refs[near_count + far_count :]
    own_ref, other_ref, near = rest[:3]
    far, sems = (rest[3], rest[4]) if far_count else (None, rest[3])
    copies = []
    for number, ref in enumerate(near_refs):
        copies.append(pltpu.make_async_copy(ref, near.at[number], sems.at[number]))
    at = 0
    for number, ref in enumerate(far_refs):
        target = far.at[pl.ds(at, ref.shape[0])]
        copies.append(pltpu.make_async_copy(ref, target, sems.at[near_count + number]))
        at += ref.shape[0]
    for copy in copies:
        copy.start()
    units = (near.shape[1] - PAD) // 2
    x = x_ref[...], pair_ref[...]
    total = [None, None]
    for number in range(near_count + (1 if far_count else 0)):
        if number < near_count:
            copies[number].wait()
            into = near[number, :units]
            out_of = near[number, units : 2 * units]
            bias = near[number, 2 * units : 2 * units + 1, :units].astype(F32)
        else:
            for copy in copies[near_count:]:
                copy.wait()
            shards = far.shape[0]
            piece = (far.shape[1] - EXT) // 2
            into = far[:, :piece].reshape(shards * piece, -1)
            out_of = far[:, piece : 2 * piece].reshape(shards * piece, -1)
            bias = jnp.concatenate(
                [far[i, 2 * piece : 2 * piece + 1, :piece].astype(F32) for i in range(shards)],
                axis=1,
            )
        before = [dot(part, into, NT) + bias for part in x]
        for i in range(2):
            pre = before[i]
            hidden = (0.5 * pre * (1.0 + lax.erf(pre * math.sqrt(0.5)))).astype(BF16)
            part = dot(hidden, out_of)
            total[i] = part if total[i] is None else total[i] + part
    own_ref[...] = total[0].astype(BF16)
    other_ref[...] = total[1].astype(BF16)


def mlp(x, pair, near, far=()):
    rows, width = x.shape
    shape = jax.ShapeDtypeStruct((rows, width), BF16)
    vmem = pl.BlockSpec(memory_space=pltpu.VMEM)
    units = (near[0].shape[0] - PAD) // 2
    groups = len(near) + (1 if far else 0)
    scratch = [pltpu.VMEM((len(near),) + near[0].shape, BF16)]
    if far:
        shards = sum(array.shape[0] for array in far)
        scratch.append(pltpu.VMEM((shards,) + far[0].shape[1:], BF16))
    scratch.append(pltpu.SemaphoreType.DMA((len(near) + len(far),)))
    return pl.pallas_call(
        lambda *refs: mlp_kernel(*refs, near_count=len(near), far_count=len(far)),
        out_shape=(shape, shape),
        in_specs=[vmem, vmem] + [pl.BlockSpec(memory_space=pl.ANY)] * (len(near) + len(far)),
        out_specs=(vmem, vmem),
        scratch_shapes=scratch,
        compiler_params=cparams(),
        cost_estimate=cost(8 * rows * groups * units * width, groups * (5 << 20)),
        name="mlp",
    )(x, pair, *near, *far)


def merge_kernel(res_ref, bias_ref, gain_ref, index_ref, owner_ref, *refs, cap):
    parts, out_ref = refs[:-1], refs[-1]
    rows, width = res_ref.shape
    total = res_ref[...].astype(F32) + bias_ref[...].reshape(1, width)
    for part in parts:
        total = total + part[...].astype(F32)
    normed = (layer_norm(total) * gain_ref[...].reshape(1, width)).astype(BF16)
    count = rows // 4
    r = lax.broadcasted_iota(jnp.int32, (rows, rows), 0)
    s = lax.broadcasted_iota(jnp.int32, (rows, rows), 1)
    named = (index_ref[...] == r).astype(F32).astype(BF16)
    order = (s == 4 * (r % count) + r // count).astype(F32).astype(BF16)
    pick = dot(order, named, NT).astype(BF16)
    merged = dot(pick, normed).astype(BF16)
    for c in range(4):
        out_ref[:, c * width : (c + 1) * width] = merged[c * count : (c + 1) * count]
    across = owner_ref[...]
    r = lax.broadcasted_iota(jnp.int32, (count, count), 0)
    s = lax.broadcasted_iota(jnp.int32, (count, count), 1)
    owner = jnp.sum(jnp.where(r == s, across, 0), axis=1, keepdims=True)
    earlier = (across == owner) & (s < r)
    rank = jnp.sum(earlier.astype(jnp.int32), axis=1, keepdims=True)
    slot = (owner * cap + rank).astype(F32).astype(BF16)
    out_ref[:, 4 * width :] = jnp.broadcast_to(slot, (count, LANES))


def merge(residual, out_bias, merge_gain, merge_index, owners, parts, cap):
    rows, width = residual.shape
    operands = (
        residual,
        out_bias,
        merge_gain,
        merge_index.reshape(1, rows),
        owners.reshape(1, rows // 4),
        *parts,
    )
    return pl.pallas_call(
        lambda *refs: merge_kernel(*refs, cap=cap),
        out_shape=jax.ShapeDtypeStruct((rows // 4, 4 * width + LANES), BF16),
        in_specs=[pl.BlockSpec(memory_space=pltpu.VMEM)] * len(operands),
        out_specs=pl.BlockSpec(memory_space=pltpu.VMEM),
        compiler_params=cparams(),
        cost_estimate=cost(2 * rows * rows * width, 4 << 20),
        name="merge",
    )(*operands)


def embed_kernel(group_ref, *refs, pieces, cap, slots):
    x_refs = refs[: len(pieces)]
    w_ref, bias_ref, out_ref, x_sc, acc_ref = refs[len(pieces) :]
    step = pl.program_id(0)
    steps = pl.num_programs(0)
    for (at, _), x_ref in zip(pieces, x_refs):
        x_sc[at : at + x_ref.shape[0], :] = x_ref[...]

    @pl.when(step < steps - 1)
    def _():
        part = dot(x_sc[...], w_ref[...])

        @pl.when(step == 0)
        def _():
            acc_ref[...] = part

        @pl.when(step > 0)
        def _():
            acc_ref[...] += part

    @pl.when(step == steps - 1)
    def _():
        embedded = (acc_ref[...] + bias_ref[...]).astype(BF16)
        total = x_sc.shape[0]
        count = total // 4
        slot = x_sc[:, 0:1].astype(F32).astype(jnp.int32)
        owner = slot // cap
        rank = slot - owner * cap
        shift = lax.broadcasted_iota(jnp.int32, (total, 1), 0) // count
        group = group_ref[0] + shift
        group = jnp.where(group >= 4, group - 4, group)
        target = owner * slots + group * cap + rank
        lane = lax.broadcasted_iota(jnp.int32, (total, out_ref.shape[0]), 1)
        place = (target == lane).astype(F32).T.astype(BF16)
        out_ref[...] = dot(place, embedded).astype(BF16)


def embed(group, pieces, w_merge, merge_bias, cap, slots, owners, block=1408):
    arrays = [array for _, array in pieces]
    rows = sum(array.shape[0] for array in arrays)
    depth, cols = w_merge.shape
    steps = depth // block
    places = tuple((at, array.shape[0]) for at, array in pieces)
    x_block = block

    def x_map(i, _):
        return (0, i)

    spec = lambda array: pl.BlockSpec((array.shape[0], x_block), x_map)
    return pl.pallas_call(
        lambda *refs: embed_kernel(*refs, pieces=places, cap=cap, slots=slots),
        out_shape=jax.ShapeDtypeStruct((owners * slots, cols), BF16),
        grid_spec=pltpu.PrefetchScalarGridSpec(
            num_scalar_prefetch=1,
            grid=(steps + 1,),
            in_specs=[spec(array) for array in arrays]
            + [
                pl.BlockSpec((block, cols), lambda i, _: (jnp.minimum(i, steps - 1), 0)),
                pl.BlockSpec((1, cols), lambda i, _: (0, 0)),
            ],
            out_specs=pl.BlockSpec((owners * slots, cols), lambda i, _: (0, 0)),
            scratch_shapes=[pltpu.VMEM((rows, block), BF16), pltpu.VMEM((rows, cols), F32)],
        ),
        compiler_params=cparams("arbitrary"),
        cost_estimate=cost(2 * rows * depth * cols, 10 << 20),
        name="embed",
    )(group, *arrays, w_merge, merge_bias.reshape(1, cols))


def flip(value, axis):
    return lax.ppermute(value, axis, [(0, 1), (1, 0)])


def turn(value, axis, by):
    size = lax.axis_size(axis)
    return lax.ppermute(value, axis, [(i, (i + by) % size) for i in range(size)])


def ring_gather(value, axis):
    before = turn(value, axis, 1)
    after = turn(value, axis, -1)
    half = value.shape[0] // 2
    return before, after, turn(before[:half], axis, 1), turn(after[half:], axis, -1)


def pack_kernel(in_ref, bias_ref, out_ref, near_ref, far_ref, row_sc, near_sc, far_sc, sems):
    half = (near_ref.shape[0] - PAD) // 2
    share = (far_ref.shape[0] - EXT) // 2
    core = lax.axis_index("c")
    first = pl.multiple_of(core * half, half)
    chip = lax.axis_index(CHIPS)
    at = pl.multiple_of(first + chip * share, 16)
    width = in_ref.shape[1]
    bias = bias_ref[...].astype(F32).reshape(1, 2 * half)
    bias = jnp.where(core == 0, bias[:, :half], bias[:, half:])
    rest = jnp.zeros((PAD, width - half), F32)
    bias = jnp.broadcast_to(bias, (PAD, half))
    row_sc[0] = jnp.concatenate([bias, rest], axis=1).astype(BF16)
    bias = pltpu.roll(bias, jnp.where(chip == 0, 0, half - chip * share), 1)
    row_sc[1] = jnp.concatenate([bias, rest], axis=1).astype(BF16)
    pieces = [
        (in_ref, first, 0, half, near_ref, near_sc),
        (out_ref, first, half, half, near_ref, near_sc),
        (in_ref, at, 0, share, far_ref, far_sc),
        (out_ref, at, share, share, far_ref, far_sc),
    ]
    inward = []
    for i, (source, begin, to, size, _, buffer) in enumerate(pieces):
        copy = pltpu.make_async_copy(
            source.at[pl.ds(begin, size)], buffer.at[pl.ds(to, size)], sems.at[i]
        )
        copy.start()
        inward.append(copy)
    outward = [
        pltpu.make_async_copy(row_sc.at[0], near_ref.at[pl.ds(2 * half, PAD)], sems.at[8]),
        pltpu.make_async_copy(
            row_sc.at[1, pl.ds(0, EXT)], far_ref.at[pl.ds(2 * share, EXT)], sems.at[9]
        ),
    ]
    outward[0].start()
    outward[1].start()
    for i in (2, 3, 0, 1):
        _, _, to, size, target, buffer = pieces[i]
        inward[i].wait()
        copy = pltpu.make_async_copy(
            buffer.at[pl.ds(to, size)], target.at[pl.ds(to, size)], sems.at[4 + i]
        )
        copy.start()
        outward.append(copy)
    for copy in outward:
        copy.wait()


def pack(w_in, in_bias, w_out, shares):
    units, width = w_in.shape
    half = units // 2
    any_space = pl.BlockSpec(memory_space=pl.ANY)
    return pl.pallas_call(
        pack_kernel,
        out_shape=(
            jax.ShapeDtypeStruct((2 * half + PAD, width), BF16),
            jax.ShapeDtypeStruct((2 * half // shares + EXT, width), BF16),
        ),
        in_specs=[
            any_space,
            pl.BlockSpec(memory_space=pltpu.VMEM),
            any_space,
        ],
        out_specs=(any_space, any_space),
        scratch_shapes=[
            pltpu.VMEM((2, PAD, width), BF16),
            pltpu.VMEM((2 * half, width), BF16),
            pltpu.VMEM((2 * half // shares, width), BF16),
            pltpu.SemaphoreType.DMA((10,)),
        ],
        compiler_params=cparams(),
        cost_estimate=cost(0, 9 << 20),
        name="pack",
    )(w_in, in_bias, w_out)


def local(
    tokens,
    seg_ids,
    merge_index,
    owners,
    w_qkv,
    w_attn_out,
    w_in,
    in_bias,
    w_out,
    out_bias,
    merge_gain,
    w_merge,
    merge_bias,
):
    near, far = pack(w_in, in_bias, w_out, lax.axis_size(CHIPS))
    far = turn(far, "grp", 2)
    one, two = turn(near, "grp", 1), turn(near, "grp", -1)
    heads = qkv(tokens, seg_ids, w_qkv)
    far, heads = lax.optimization_barrier((far, heads))
    row = [far] + [turn(far, ("xh", "xl"), by) for by in (1, 2, 3)]
    mine = lax.all_to_all(heads, ("y", "xh"), 0, 0, tiled=True)
    row, mine = lax.optimization_barrier((row, mine))
    row = jnp.stack(row)
    below, above = turn(row, "y", 1), turn(row, "y", -1)
    queries, kv = mine[:, : HD + EXT], mine[:, HD:]
    away = flip(queries, "xl")
    kv_c = flip(kv, "c")
    acc = attend(queries, [kv])
    away, kv_c, acc = lax.optimization_barrier((away, kv_c, acc))
    sent = attend(away, [kv, kv_c], send=True)
    below, above, sent = lax.optimization_barrier((below, above, sent))
    sent = flip(sent, "xl")
    far_a, far_b = turn(below[:2], "y", 1), turn(above[2:], "y", -1)
    acc = attend(queries, [kv_c], acc)
    sent, acc = lax.optimization_barrier((sent, acc))
    done = combine(acc, sent)
    attended = lax.all_to_all(done, ("y", "xh"), 0, 0, tiled=True)
    far_a, far_b, attended = lax.optimization_barrier((far_a, far_b, attended))
    far = [row, below, above, far_a, far_b]
    residual, mlp_in = project(attended, tokens, w_attn_out)
    pair = flip(mlp_in, "c")
    own, other = mlp(mlp_in, pair, [near], far)
    other = flip(other, "c")
    one, two, own = lax.optimization_barrier((one, two, own))
    own_b, other_b = mlp(mlp_in, pair, [one, two])
    parts = [own, other, own_b, flip(other_b, "c")]
    owner_count = lax.axis_size(("y", "xh", "xl", "c"))
    cap = 4
    merged = merge(residual, out_bias, merge_gain, merge_index, owners, parts, cap)
    count = merged.shape[0]
    before, after, far_a, far_b = ring_gather(merged, "grp")
    pieces = [
        (0, merged),
        (count, after),
        (2 * count, far_a),
        (2 * count + count // 2, far_b),
        (3 * count, before),
    ]
    group = lax.axis_index("grp").reshape(1).astype(jnp.int32)
    slots = 4 * cap
    outgoing = embed(group, pieces, w_merge, merge_bias, cap, slots, owner_count)
    cols = outgoing.shape[1]
    received = lax.all_to_all(outgoing, ("y", "xh", "xl", "c"), 0, 0, tiled=True)
    received = received.reshape(owner_count, 4, cap, cols)
    return received.transpose(1, 0, 2, 3).reshape(4 * owner_count * cap, cols)


def solution(mesh):
    inner = Mesh(mesh.devices.reshape(4, 4, 2, 2, 2), ("grp", "y", "xh", "xl", "c"))
    every = ("grp", "y", "xh", "xl", "c")
    tok = ("y", "xh", "xl", "c")
    placed = (
        P(every, None),
        P(every),
        P(every),
        P(every, None),
        P(),
        P(),
        P("grp", None),
        P("grp"),
        P("grp", None),
        P(),
        P(),
        P(None, "grp"),
        P("grp"),
    )
    return jax.shard_map(
        local, mesh=inner, in_specs=placed, out_specs=P(tok, "grp"), check_vma=False
    )
```

```python
import math

import jax
import jax.numpy as jnp
from jax import lax
from jax.experimental import pallas as pl
from jax.experimental.pallas import tpu as pltpu
from jax.sharding import Mesh
from jax.sharding import PartitionSpec as P

HEADS = 8
HD = 88
EXT = 8
NORM_EPS = 1e-06
LANES = 128
PAD = 16
CHIPS = ("y", "xh", "xl")
F32 = jnp.float32
BF16 = jnp.bfloat16
VMEM_LIMIT = 60 * 1024 * 1024


def cparams(*semantics):
    return pltpu.CompilerParams(
        dimension_semantics=semantics or None, vmem_limit_bytes=VMEM_LIMIT
    )


def in_vmem(value):
    return pltpu.with_memory_space_constraint(value, pltpu.VMEM)


def layer_norm(values):
    centred = values - jnp.mean(values, axis=-1, keepdims=True)
    return centred * lax.rsqrt(jnp.mean(centred * centred, axis=-1, keepdims=True) + NORM_EPS)


def dot(a, b, dims=(((1,), (0,)), ((), ()))):
    return lax.dot_general(a, b, dims, preferred_element_type=F32)


NT = (((1,), (1,)), ((), ()))


def cost(flops, size, transcendentals=0):
    return pl.CostEstimate(flops=flops, bytes_accessed=size, transcendentals=transcendentals)


def qkv_kernel(x_ref, seg_ref, w_hbm, out_ref, w_ref, sems):
    group = HEADS // 2 * HD
    count = w_ref.shape[0] // group
    copies = []
    for number in range(count):
        at = pl.ds(number * group, group)
        copies.append(pltpu.make_async_copy(w_hbm.at[at], w_ref.at[at], sems.at[number]))
        copies[-1].start()
    normed = layer_norm(x_ref[...].astype(F32)).astype(BF16)
    seg = seg_ref[...]
    high = seg // 64
    low = seg - high * 64
    tokens = seg.shape[1]
    row = lax.broadcasted_iota(jnp.int32, (EXT, tokens), 0)
    extra = jnp.where(row == 0, 1, jnp.where(row == 1, high, jnp.where(row == 2, low, 0)))
    extra = extra.astype(F32)
    scale = math.log2(math.e) / math.sqrt(HD)
    for number in range(count):
        copies[number].wait()
        part = dot(w_ref[number * group : (number + 1) * group, :], normed, NT)
        part = part.astype(BF16).astype(F32)
        kind = number // 2
        for i in range(HEADS // 2):
            head = number % 2 * (HEADS // 2) + i
            rows = part[i * HD : (i + 1) * HD]
            if kind == 2:
                out_ref[head, HD : 2 * HD + EXT] = jnp.concatenate([extra, rows], axis=0).astype(
                    BF16
                )
                continue
            norm = lax.rsqrt(jnp.mean(rows * rows, axis=0, keepdims=True) + NORM_EPS)
            if kind == 0:
                out_ref[head, :HD] = (rows * (norm * scale)).astype(BF16)
            else:
                out_ref[head, 2 * HD + EXT :] = (rows * norm).astype(BF16)


def qkv(tokens, seg_ids, w_qkv):
    rows, width = tokens.shape
    return pl.pallas_call(
        qkv_kernel,
        out_shape=jax.ShapeDtypeStruct((HEADS, 3 * HD + EXT, rows), BF16),
        in_specs=[
            pl.BlockSpec(memory_space=pltpu.VMEM),
            pl.BlockSpec(memory_space=pltpu.VMEM),
            pl.BlockSpec(memory_space=pl.ANY),
        ],
        out_specs=pl.BlockSpec(memory_space=pltpu.VMEM),
        scratch_shapes=[
            pltpu.VMEM((w_qkv.shape[1], width), BF16),
            pltpu.SemaphoreType.DMA((6,)),
        ],
        compiler_params=cparams(),
        cost_estimate=cost(2 * rows * width * w_qkv.shape[1], 8 << 20),
        name="qkv",
    )(tokens, seg_ids.reshape(1, rows), w_qkv.T)


def attend_kernel(*refs, sets, first, send, key_block, unroll):
    q_ref = refs[0]
    kv_refs = refs[1 : 1 + sets]
    rest = refs[1 + sets :]
    if not first:
        acc_ref, rest = rest[0], rest[1:]
    out_ref, k_sc, v_sc, seg_sc = rest
    blocks, top, tokens = q_ref.shape
    width = LANES - HD
    for number, kv_ref in enumerate(kv_refs):
        for j in range(blocks):
            start = (number * blocks + j) * tokens
            digits = kv_ref[j, : 2 * EXT].astype(F32)
            seg = digits[1:2] * 64.0 + digits[2:3]
            keys = kv_ref[j, top:].astype(F32)
            both = jnp.concatenate([keys, jnp.broadcast_to(seg, (width, tokens))], axis=0).T
            v_sc[:, start : start + tokens] = kv_ref[j, :top]
            k_sc[start : start + tokens, :] = both.astype(BF16)
            seg_sc[start : start + tokens, :] = jnp.broadcast_to(
                both[:, HD : HD + 1], (tokens, LANES)
            )

    def tile(i):
        at_q = pl.ds(pl.multiple_of(i * tokens, tokens), tokens)
        mine = q_ref[i].astype(F32)
        q = jnp.concatenate([mine[:HD], jnp.zeros((width, tokens), F32)], axis=0).astype(BF16)
        seg = mine[HD + 1 : HD + 2] * 64.0 + mine[HD + 2 : HD + 3]
        total = None
        for start in range(0, sets * blocks * tokens, key_block):
            at = slice(start, start + key_block)
            scores = dot(k_sc[at, :], q)
            of_key = seg_sc[at, :]
            of_key = jnp.concatenate([of_key] * (tokens // LANES), axis=1)
            weights = jnp.where(of_key == seg, jnp.exp2(scores), 0.0).astype(BF16)
            part = dot(v_sc[:, at], weights)
            total = part if total is None else total + part
        if not first:
            total = total + acc_ref[:, at_q]
        if send:
            near = total[:1].astype(BF16).astype(F32)
            rows = [near, total[:1] - near, jnp.zeros((EXT - 2, tokens), F32), total[EXT:]]
            out_ref[i] = jnp.concatenate(rows, axis=0).astype(BF16)
        else:
            out_ref[:, at_q] = total

    def step(i, carry):
        for j in range(unroll):
            tile(i * unroll + j)
        return carry

    lax.fori_loop(0, blocks // unroll, step, 0)


def attend(queries, sets, acc=None, send=False, key_block=512, unroll=4):
    blocks, top, tokens = queries.shape
    total = blocks * tokens
    keys = total * len(sets)
    first = acc is None
    if send:
        shape = jax.ShapeDtypeStruct(queries.shape, BF16)
    else:
        shape = jax.ShapeDtypeStruct((top, total), F32)
    operands = [in_vmem(queries), *map(in_vmem, sets)]
    if not first:
        operands.append(in_vmem(acc))
    return pl.pallas_call(
        lambda *refs: attend_kernel(
            *refs, sets=len(sets), first=first, send=send, key_block=key_block, unroll=unroll
        ),
        out_shape=shape,
        in_specs=[pl.BlockSpec(memory_space=pltpu.VMEM)] * len(operands),
        out_specs=pl.BlockSpec(memory_space=pltpu.VMEM),
        scratch_shapes=[
            pltpu.VMEM((keys, LANES), BF16),
            pltpu.VMEM((top, keys), BF16),
            pltpu.VMEM((keys, LANES), F32),
        ],
        compiler_params=cparams(),
        cost_estimate=cost(4 * total * keys * LANES, 3 << 20, total * keys),
        name="attend",
    )(*operands)


def combine_kernel(acc_ref, sent_ref, out_ref):
    blocks, _, tokens = sent_ref.shape
    for i in range(blocks):
        acc = acc_ref[:, i * tokens : (i + 1) * tokens]
        sent = sent_ref[i].astype(F32)
        weight = acc[:1] + (sent[:1] + sent[1:2])
        out_ref[i] = ((acc[EXT:] + sent[EXT:]) / weight).astype(BF16)


def combine(acc, sent):
    blocks, top, tokens = sent.shape
    return pl.pallas_call(
        combine_kernel,
        out_shape=jax.ShapeDtypeStruct((blocks, top - EXT, tokens), BF16),
        in_specs=[pl.BlockSpec(memory_space=pltpu.VMEM)] * 2,
        out_specs=pl.BlockSpec(memory_space=pltpu.VMEM),
        compiler_params=cparams(),
        cost_estimate=cost(0, 2 << 20),
        name="combine",
    )(in_vmem(acc), in_vmem(sent))


def project_kernel(att_ref, x_ref, w_ref, res_ref, in_ref):
    heads, _, tokens = att_ref.shape
    att = att_ref[...].astype(F32).reshape(heads * HD, tokens).T.astype(BF16)
    residual = (x_ref[...].astype(F32) + dot(att, w_ref[...])).astype(BF16)
    res_ref[...] = residual
    in_ref[...] = layer_norm(residual.astype(F32)).astype(BF16)


def project(attended, tokens, w_attn_out):
    shape = jax.ShapeDtypeStruct(tokens.shape, BF16)
    return pl.pallas_call(
        project_kernel,
        out_shape=(shape, shape),
        in_specs=[pl.BlockSpec(memory_space=pltpu.VMEM)] * 3,
        out_specs=(pl.BlockSpec(memory_space=pltpu.VMEM),) * 2,
        compiler_params=cparams(),
        cost_estimate=cost(2 * tokens.shape[0] * w_attn_out.shape[0] * w_attn_out.shape[1], 4 << 20),
        name="project",
    )(in_vmem(attended), tokens, w_attn_out)


def mlp_kernel(x_ref, pair_ref, *refs, near_count, far_count):
    near_refs, far_refs = refs[:near_count], refs[near_count : near_count + far_count]
    rest = refs[near_count + far_count :]
    own_ref, other_ref, near = rest[:3]
    far, sems = (rest[3], rest[4]) if far_count else (None, rest[3])
    copies = []
    for number, ref in enumerate(near_refs):
        copies.append(pltpu.make_async_copy(ref, near.at[number], sems.at[number]))
    at = 0
    for number, ref in enumerate(far_refs):
        target = far.at[pl.ds(at, ref.shape[0])]
        copies.append(pltpu.make_async_copy(ref, target, sems.at[near_count + number]))
        at += ref.shape[0]
    for copy in copies:
        copy.start()
    units = (near.shape[1] - PAD) // 2
    x = x_ref[...], pair_ref[...]
    total = [None, None]
    for number in range(near_count + (1 if far_count else 0)):
        if number < near_count:
            copies[number].wait()
            into = near[number, :units]
            out_of = near[number, units : 2 * units]
            bias = near[number, 2 * units : 2 * units + 1, :units].astype(F32)
        else:
            for copy in copies[near_count:]:
                copy.wait()
            shards = far.shape[0]
            piece = (far.shape[1] - EXT) // 2
            into = far[:, :piece].reshape(shards * piece, -1)
            out_of = far[:, piece : 2 * piece].reshape(shards * piece, -1)
            bias = jnp.concatenate(
                [far[i, 2 * piece : 2 * piece + 1, :piece].astype(F32) for i in range(shards)],
                axis=1,
            )
        before = [dot(part, into, NT) + bias for part in x]
        for i in range(2):
            pre = before[i]
            hidden = (0.5 * pre * (1.0 + lax.erf(pre * math.sqrt(0.5)))).astype(BF16)
            part = dot(hidden, out_of)
            total[i] = part if total[i] is None else total[i] + part
    own_ref[...] = total[0].astype(BF16)
    other_ref[...] = total[1].astype(BF16)


def mlp(x, pair, near, far=()):
    rows, width = x.shape
    shape = jax.ShapeDtypeStruct((rows, width), BF16)
    vmem = pl.BlockSpec(memory_space=pltpu.VMEM)
    units = (near[0].shape[0] - PAD) // 2
    groups = len(near) + (1 if far else 0)
    scratch = [pltpu.VMEM((len(near),) + near[0].shape, BF16)]
    if far:
        shards = sum(array.shape[0] for array in far)
        scratch.append(pltpu.VMEM((shards,) + far[0].shape[1:], BF16))
    scratch.append(pltpu.SemaphoreType.DMA((len(near) + len(far),)))
    return pl.pallas_call(
        lambda *refs: mlp_kernel(*refs, near_count=len(near), far_count=len(far)),
        out_shape=(shape, shape),
        in_specs=[vmem, vmem] + [pl.BlockSpec(memory_space=pl.ANY)] * (len(near) + len(far)),
        out_specs=(vmem, vmem),
        scratch_shapes=scratch,
        compiler_params=cparams(),
        cost_estimate=cost(8 * rows * groups * units * width, groups * (5 << 20)),
        name="mlp",
    )(x, in_vmem(pair), *near, *far)


def merge_kernel(res_ref, bias_ref, gain_ref, index_ref, owner_ref, *refs, cap):
    parts, out_ref = refs[:-1], refs[-1]
    rows, width = res_ref.shape
    total = res_ref[...].astype(F32) + bias_ref[...].reshape(1, width)
    for part in parts:
        total = total + part[...].astype(F32)
    normed = (layer_norm(total) * gain_ref[...].reshape(1, width)).astype(BF16)
    count = rows // 4
    r = lax.broadcasted_iota(jnp.int32, (rows, rows), 0)
    s = lax.broadcasted_iota(jnp.int32, (rows, rows), 1)
    named = (index_ref[...] == r).astype(F32).astype(BF16)
    order = (s == 4 * (r % count) + r // count).astype(F32).astype(BF16)
    pick = dot(order, named, NT).astype(BF16)
    merged = dot(pick, normed).astype(BF16)
    for c in range(4):
        out_ref[:, c * width : (c + 1) * width] = merged[c * count : (c + 1) * count]
    across = owner_ref[...]
    r = lax.broadcasted_iota(jnp.int32, (count, count), 0)
    s = lax.broadcasted_iota(jnp.int32, (count, count), 1)
    owner = jnp.sum(jnp.where(r == s, across, 0), axis=1, keepdims=True)
    earlier = (across == owner) & (s < r)
    rank = jnp.sum(earlier.astype(jnp.int32), axis=1, keepdims=True)
    slot = (owner * cap + rank).astype(F32).astype(BF16)
    out_ref[:, 4 * width :] = jnp.broadcast_to(slot, (count, LANES))


def merge(residual, out_bias, merge_gain, merge_index, owners, parts, cap):
    rows, width = residual.shape
    operands = (
        residual,
        out_bias,
        merge_gain,
        merge_index.reshape(1, rows),
        owners.reshape(1, rows // 4),
        parts[0],
        *map(in_vmem, parts[1:]),
    )
    return pl.pallas_call(
        lambda *refs: merge_kernel(*refs, cap=cap),
        out_shape=jax.ShapeDtypeStruct((rows // 4, 4 * width + LANES), BF16),
        in_specs=[pl.BlockSpec(memory_space=pltpu.VMEM)] * len(operands),
        out_specs=pl.BlockSpec(memory_space=pltpu.VMEM),
        compiler_params=cparams(),
        cost_estimate=cost(2 * rows * rows * width, 4 << 20),
        name="merge",
    )(*operands)


def embed_kernel(*refs, pieces, cap, slots):
    x_refs = refs[: len(pieces)]
    w_hbm, bias_ref, out_ref, x_sc, w_sc, sems = refs[len(pieces) :]
    depth, cols = w_hbm.shape
    block = depth // 4
    copies = []
    for i in range(4):
        at = pl.ds(i * block, block)
        copies.append(pltpu.make_async_copy(w_hbm.at[at], w_sc.at[at], sems.at[i]))
        copies[-1].start()
    for at, x_ref in zip(pieces, x_refs):
        x_sc[at : at + x_ref.shape[0], :] = x_ref[...]
    embedded = jnp.broadcast_to(bias_ref[...].reshape(1, cols), (x_sc.shape[0], cols))
    for i in range(4):
        copies[i].wait()
        at = slice(i * block, (i + 1) * block)
        embedded = embedded + dot(x_sc[:, at], w_sc[at, :])
    embedded = embedded.astype(BF16)
    total = x_sc.shape[0]
    count = total // 4
    slot = x_sc[:, depth : depth + 1].astype(F32).astype(jnp.int32)
    owner = slot // cap
    rank = slot - owner * cap
    group = lax.axis_index("grp") + lax.broadcasted_iota(jnp.int32, (total, 1), 0) // count
    group = jnp.where(group >= 4, group - 4, group)
    target = owner * slots + group * cap + rank
    lane = lax.broadcasted_iota(jnp.int32, (total, out_ref.shape[0]), 1)
    place = (target == lane).astype(F32).T.astype(BF16)
    out_ref[...] = dot(place, embedded).astype(BF16)


def embed(pieces, w_merge, merge_bias, cap, slots, owners):
    arrays = [in_vmem(array) for _, array in pieces]
    rows = sum(array.shape[0] for array in arrays)
    depth, cols = w_merge.shape
    places = tuple(at for at, _ in pieces)
    return pl.pallas_call(
        lambda *refs: embed_kernel(*refs, pieces=places, cap=cap, slots=slots),
        out_shape=jax.ShapeDtypeStruct((owners * slots, cols), BF16),
        in_specs=[pl.BlockSpec(memory_space=pltpu.VMEM)] * len(arrays)
        + [pl.BlockSpec(memory_space=pl.ANY), pl.BlockSpec(memory_space=pltpu.VMEM)],
        out_specs=pl.BlockSpec(memory_space=pltpu.VMEM),
        scratch_shapes=[
            pltpu.VMEM((rows, arrays[0].shape[1]), BF16),
            pltpu.VMEM((depth, cols), BF16),
            pltpu.SemaphoreType.DMA((4,)),
        ],
        compiler_params=cparams(),
        cost_estimate=cost(2 * rows * depth * cols, 10 << 20),
        name="embed",
    )(*arrays, w_merge, merge_bias)


def flip(value, axis):
    return lax.ppermute(value, axis, [(0, 1), (1, 0)])


def turn(value, axis, by):
    size = lax.axis_size(axis)
    return lax.ppermute(value, axis, [(i, (i + by) % size) for i in range(size)])


def ring_gather(value, axis):
    before = turn(value, axis, 1)
    after = turn(value, axis, -1)
    half = value.shape[0] // 2
    return before, after, turn(before[:half], axis, 1), turn(after[half:], axis, -1)


def pack_kernel(in_ref, bias_ref, out_ref, pack_ref, row_sc, sc, sems, *, shares):
    size = sc.shape[0] // 2
    half = size * shares
    tail = row_sc.shape[0]
    core = lax.axis_index("c")
    first = pl.multiple_of(core * half, half)
    if shares > 1:
        chip = lax.axis_index(CHIPS)
        first = pl.multiple_of(first + chip * size, 16)
    copies = []
    for i, ref in enumerate((in_ref, out_ref)):
        source = ref.at[pl.ds(first, size)]
        copies.append(pltpu.make_async_copy(source, sc.at[pl.ds(i * size, size)], sems.at[i]))
        copies[-1].start()
    width = in_ref.shape[1]
    bias = bias_ref[...].astype(F32).reshape(1, 2 * half)
    bias = jnp.where(core == 0, bias[:, :half], bias[:, half:])
    bias = jnp.broadcast_to(bias, (tail, half))
    if shares > 1:
        bias = pltpu.roll(bias, jnp.where(chip == 0, 0, half - chip * size), 1)
    rest = jnp.zeros((tail, width - half), F32)
    row_sc[...] = jnp.concatenate([bias, rest], axis=1).astype(BF16)
    copies.append(
        pltpu.make_async_copy(row_sc, pack_ref.at[pl.ds(2 * size, tail)], sems.at[2])
    )
    copies[-1].start()
    for i in range(2):
        at = pl.ds(i * size, size)
        copies[i].wait()
        copies.append(pltpu.make_async_copy(sc.at[at], pack_ref.at[at], sems.at[3 + i]))
        copies[-1].start()
    for copy in copies[2:]:
        copy.wait()


def pack(w_in, in_bias, w_out, shares, tail):
    units, width = w_in.shape
    size = units // 2 // shares
    any_space = pl.BlockSpec(memory_space=pl.ANY)
    return pl.pallas_call(
        lambda *refs: pack_kernel(*refs, shares=shares),
        out_shape=jax.ShapeDtypeStruct((2 * size + tail, width), BF16),
        in_specs=[any_space, pl.BlockSpec(memory_space=pltpu.VMEM), any_space],
        out_specs=any_space,
        scratch_shapes=[
            pltpu.VMEM((tail, width), BF16),
            pltpu.VMEM((2 * size, width), BF16),
            pltpu.SemaphoreType.DMA((5,)),
        ],
        compiler_params=cparams(),
        cost_estimate=cost(0, 8 * size * width),
        name="pack",
    )(w_in, in_bias, w_out)


def local(
    tokens,
    seg_ids,
    merge_index,
    owners,
    w_qkv,
    w_attn_out,
    w_in,
    in_bias,
    w_out,
    out_bias,
    merge_gain,
    w_merge,
    merge_bias,
):
    far = turn(pack(w_in, in_bias, w_out, lax.axis_size(CHIPS), EXT), "grp", 2)
    near = pack(w_in, in_bias, w_out, 1, PAD)
    far, near = lax.optimization_barrier((far, near))
    row = [far] + [turn(far, ("xh", "xl"), by) for by in (1, 2, 3)]
    one, two = turn(near, "grp", 1), turn(near, "grp", -1)
    heads = qkv(tokens, seg_ids, w_qkv)
    row, heads = lax.optimization_barrier((row, heads))
    mine = lax.all_to_all(heads, ("y", "xh"), 0, 0, tiled=True)
    row, mine = lax.optimization_barrier((jnp.stack(row), mine))
    below, above = turn(row, "y", 1), turn(row, "y", -1)
    queries, kv = mine[:, : HD + EXT], mine[:, HD:]
    kv_c = flip(kv, "c")
    queries, kv_c = lax.optimization_barrier((queries, kv_c))
    away = flip(queries, "xl")
    acc = attend(queries, [kv])
    away, acc = lax.optimization_barrier((away, acc))
    sent = flip(attend(away, [kv, kv_c], send=True), "xl")
    acc = attend(queries, [kv_c], acc)
    below, above, acc = lax.optimization_barrier((below, above, acc))
    far_a, far_b = turn(below[:2], "y", 1), turn(above[2:], "y", -1)
    sent, acc = lax.optimization_barrier((sent, acc))
    done = combine(acc, sent)
    attended = lax.all_to_all(done, ("y", "xh"), 0, 0, tiled=True)
    far_a, far_b, attended = lax.optimization_barrier((far_a, far_b, attended))
    far = [row, below, above, far_a, far_b]
    residual, mlp_in = project(attended, tokens, w_attn_out)
    pair = flip(mlp_in, "c")
    own, other = mlp(mlp_in, pair, [near, one, two], far)
    parts = [own, flip(other, "c")]
    owner_count = lax.axis_size(("y", "xh", "xl", "c"))
    cap = 4
    merged = merge(residual, out_bias, merge_gain, merge_index, owners, parts, cap)
    count = merged.shape[0]
    before, after, far_a, far_b = ring_gather(merged, "grp")
    pieces = [
        (0, merged),
        (count, after),
        (2 * count, far_a),
        (2 * count + count // 2, far_b),
        (3 * count, before),
    ]
    slots = 4 * cap
    outgoing = embed(pieces, w_merge, merge_bias, cap, slots, owner_count)
    cols = outgoing.shape[1]
    received = lax.all_to_all(outgoing, ("y", "xh", "xl", "c"), 0, 0, tiled=True)
    received = received.reshape(owner_count, 4, cap, cols)
    return received.transpose(1, 0, 2, 3).reshape(4 * owner_count * cap, cols)


def solution(mesh):
    inner = Mesh(mesh.devices.reshape(4, 4, 2, 2, 2), ("grp", "y", "xh", "xl", "c"))
    every = ("grp", "y", "xh", "xl", "c")
    tok = ("y", "xh", "xl", "c")
    placed = (
        P(every, None),
        P(every),
        P(every),
        P(every, None),
        P(),
        P(),
        P("grp", None),
        P("grp"),
        P("grp", None),
        P(),
        P(),
        P(None, "grp"),
        P("grp"),
    )
    return jax.shard_map(
        local, mesh=inner, in_specs=placed, out_specs=P(tok, "grp"), check_vma=False
    )
```

```python
import math

import jax
import jax.numpy as jnp
from jax import lax
from jax.experimental import pallas as pl
from jax.experimental.pallas import tpu as pltpu
from jax.sharding import Mesh
from jax.sharding import PartitionSpec as P

HEADS = 8
HD = 88
EXT = 8
NORM_EPS = 1e-06
LANES = 128
PAD = 16
RINGS = 2
CHIPS = ("y", "xh", "xl")
F32 = jnp.float32
BF16 = jnp.bfloat16
VMEM_LIMIT = 60 * 1024 * 1024


def cparams(*semantics):
    return pltpu.CompilerParams(
        dimension_semantics=semantics or None, vmem_limit_bytes=VMEM_LIMIT
    )


def in_vmem(value):
    return pltpu.with_memory_space_constraint(value, pltpu.VMEM)


def layer_norm(values):
    centred = values - jnp.mean(values, axis=-1, keepdims=True)
    return centred * lax.rsqrt(jnp.mean(centred * centred, axis=-1, keepdims=True) + NORM_EPS)


def dot(a, b, dims=(((1,), (0,)), ((), ()))):
    return lax.dot_general(a, b, dims, preferred_element_type=F32)


NT = (((1,), (1,)), ((), ()))


def cost(flops, size, transcendentals=0):
    return pl.CostEstimate(flops=flops, bytes_accessed=size, transcendentals=transcendentals)


def qkv_kernel(x_ref, seg_ref, w_hbm, out_ref, w_ref, sems):
    group = HEADS // 2 * HD
    count = w_ref.shape[0] // group
    copies = []
    for number in range(count):
        at = pl.ds(number * group, group)
        copies.append(pltpu.make_async_copy(w_hbm.at[at], w_ref.at[at], sems.at[number]))
        copies[-1].start()
    normed = layer_norm(x_ref[...].astype(F32)).astype(BF16)
    seg = seg_ref[...]
    high = seg // 64
    low = seg - high * 64
    tokens = seg.shape[1]
    row = lax.broadcasted_iota(jnp.int32, (EXT, tokens), 0)
    extra = jnp.where(row == 0, 1, jnp.where(row == 1, high, jnp.where(row == 2, low, 0)))
    extra = extra.astype(F32)
    scale = math.log2(math.e) / math.sqrt(HD)
    for number in range(count):
        copies[number].wait()
        part = dot(w_ref[number * group : (number + 1) * group, :], normed, NT)
        part = part.astype(BF16).astype(F32)
        kind = number // 2
        for i in range(HEADS // 2):
            head = number % 2 * (HEADS // 2) + i
            rows = part[i * HD : (i + 1) * HD]
            if kind == 2:
                out_ref[head, HD : 2 * HD + EXT] = jnp.concatenate([extra, rows], axis=0).astype(
                    BF16
                )
                continue
            norm = lax.rsqrt(jnp.mean(rows * rows, axis=0, keepdims=True) + NORM_EPS)
            if kind == 0:
                out_ref[head, :HD] = (rows * (norm * scale)).astype(BF16)
            else:
                out_ref[head, 2 * HD + EXT :] = (rows * norm).astype(BF16)


def qkv(tokens, seg_ids, w_qkv):
    rows, width = tokens.shape
    return pl.pallas_call(
        qkv_kernel,
        out_shape=jax.ShapeDtypeStruct((HEADS, 3 * HD + EXT, rows), BF16),
        in_specs=[
            pl.BlockSpec(memory_space=pltpu.VMEM),
            pl.BlockSpec(memory_space=pltpu.VMEM),
            pl.BlockSpec(memory_space=pl.ANY),
        ],
        out_specs=pl.BlockSpec(memory_space=pltpu.VMEM),
        scratch_shapes=[
            pltpu.VMEM((w_qkv.shape[1], width), BF16),
            pltpu.SemaphoreType.DMA((6,)),
        ],
        compiler_params=cparams(),
        cost_estimate=cost(2 * rows * width * w_qkv.shape[1], 8 << 20),
        name="qkv",
    )(tokens, seg_ids.reshape(1, rows), w_qkv.T)


def attend_kernel(*refs, sets, first, send, key_block, unroll):
    q_ref = refs[0]
    kv_refs = refs[1 : 1 + sets]
    rest = refs[1 + sets :]
    if not first:
        acc_ref, rest = rest[0], rest[1:]
    out_ref, k_sc, v_sc, seg_sc = rest
    blocks, top, tokens = q_ref.shape
    width = LANES - HD
    for number, kv_ref in enumerate(kv_refs):
        for j in range(blocks):
            start = (number * blocks + j) * tokens
            digits = kv_ref[j, : 2 * EXT].astype(F32)
            seg = digits[1:2] * 64.0 + digits[2:3]
            keys = kv_ref[j, top:].astype(F32)
            both = jnp.concatenate([keys, jnp.broadcast_to(seg, (width, tokens))], axis=0).T
            v_sc[:, start : start + tokens] = kv_ref[j, :top]
            k_sc[start : start + tokens, :] = both.astype(BF16)
            seg_sc[start : start + tokens, :] = jnp.broadcast_to(
                both[:, HD : HD + 1], (tokens, LANES)
            )

    def tile(i):
        at_q = pl.ds(pl.multiple_of(i * tokens, tokens), tokens)
        mine = q_ref[i].astype(F32)
        q = jnp.concatenate([mine[:HD], jnp.zeros((width, tokens), F32)], axis=0).astype(BF16)
        seg = mine[HD + 1 : HD + 2] * 64.0 + mine[HD + 2 : HD + 3]
        total = None
        for start in range(0, sets * blocks * tokens, key_block):
            at = slice(start, start + key_block)
            scores = dot(k_sc[at, :], q)
            of_key = seg_sc[at, :]
            of_key = jnp.concatenate([of_key] * (tokens // LANES), axis=1)
            weights = jnp.where(of_key == seg, jnp.exp2(scores), 0.0).astype(BF16)
            part = dot(v_sc[:, at], weights)
            total = part if total is None else total + part
        if not first:
            total = total + acc_ref[:, at_q]
        if send:
            near = total[:1].astype(BF16).astype(F32)
            rows = [near, total[:1] - near, jnp.zeros((EXT - 2, tokens), F32), total[EXT:]]
            out_ref[i] = jnp.concatenate(rows, axis=0).astype(BF16)
        else:
            out_ref[:, at_q] = total

    def step(i, carry):
        for j in range(unroll):
            tile(i * unroll + j)
        return carry

    lax.fori_loop(0, blocks // unroll, step, 0)


def attend(queries, sets, acc=None, send=False, key_block=512, unroll=4):
    blocks, top, tokens = queries.shape
    total = blocks * tokens
    keys = total * len(sets)
    first = acc is None
    if send:
        shape = jax.ShapeDtypeStruct(queries.shape, BF16)
    else:
        shape = jax.ShapeDtypeStruct((top, total), F32)
    operands = [in_vmem(queries), *map(in_vmem, sets)]
    if not first:
        operands.append(in_vmem(acc))
    return pl.pallas_call(
        lambda *refs: attend_kernel(
            *refs, sets=len(sets), first=first, send=send, key_block=key_block, unroll=unroll
        ),
        out_shape=shape,
        in_specs=[pl.BlockSpec(memory_space=pltpu.VMEM)] * len(operands),
        out_specs=pl.BlockSpec(memory_space=pltpu.VMEM),
        scratch_shapes=[
            pltpu.VMEM((keys, LANES), BF16),
            pltpu.VMEM((top, keys), BF16),
            pltpu.VMEM((keys, LANES), F32),
        ],
        compiler_params=cparams(),
        cost_estimate=cost(4 * total * keys * LANES, 3 << 20, total * keys),
        name="attend",
    )(*operands)


def combine_kernel(acc_ref, sent_ref, out_ref):
    blocks, _, tokens = sent_ref.shape
    for i in range(blocks):
        acc = acc_ref[:, i * tokens : (i + 1) * tokens]
        sent = sent_ref[i].astype(F32)
        weight = acc[:1] + (sent[:1] + sent[1:2])
        out_ref[i] = ((acc[EXT:] + sent[EXT:]) / weight).astype(BF16)


def combine(acc, sent):
    blocks, top, tokens = sent.shape
    return pl.pallas_call(
        combine_kernel,
        out_shape=jax.ShapeDtypeStruct((blocks, top - EXT, tokens), BF16),
        in_specs=[pl.BlockSpec(memory_space=pltpu.VMEM)] * 2,
        out_specs=pl.BlockSpec(memory_space=pltpu.VMEM),
        compiler_params=cparams(),
        cost_estimate=cost(0, 2 << 20),
        name="combine",
    )(in_vmem(acc), in_vmem(sent))


def project_kernel(att_ref, x_ref, w_ref, res_ref, in_ref):
    heads, _, tokens = att_ref.shape
    att = att_ref[...].astype(F32).reshape(heads * HD, tokens).T.astype(BF16)
    residual = (x_ref[...].astype(F32) + dot(att, w_ref[...])).astype(BF16)
    res_ref[...] = residual
    in_ref[...] = layer_norm(residual.astype(F32)).astype(BF16)


def project(attended, tokens, w_attn_out):
    shape = jax.ShapeDtypeStruct(tokens.shape, BF16)
    return pl.pallas_call(
        project_kernel,
        out_shape=(shape, shape),
        in_specs=[pl.BlockSpec(memory_space=pltpu.VMEM)] * 3,
        out_specs=(pl.BlockSpec(memory_space=pltpu.VMEM),) * 2,
        compiler_params=cparams(),
        cost_estimate=cost(2 * tokens.shape[0] * w_attn_out.shape[0] * w_attn_out.shape[1], 4 << 20),
        name="project",
    )(in_vmem(attended), tokens, w_attn_out)


def mlp_kernel(x_ref, pair_ref, *refs, near_count, far_count):
    near_refs, far_refs = refs[:near_count], refs[near_count : near_count + far_count]
    rest = refs[near_count + far_count :]
    own_ref, other_ref, near = rest[:3]
    far, sems = (rest[3], rest[4]) if far_count else (None, rest[3])
    copies = []
    for number, ref in enumerate(near_refs):
        copies.append(pltpu.make_async_copy(ref, near.at[number], sems.at[number]))
    at = 0
    for number, ref in enumerate(far_refs):
        target = far.at[pl.ds(at, ref.shape[0])]
        copies.append(pltpu.make_async_copy(ref, target, sems.at[near_count + number]))
        at += ref.shape[0]
    for copy in copies:
        copy.start()
    units = (near.shape[1] - PAD) // 2
    x = x_ref[...], pair_ref[...]
    total = [None, None]
    for number in range(near_count + (1 if far_count else 0)):
        if number < near_count:
            copies[number].wait()
            into = near[number, :units]
            out_of = near[number, units : 2 * units]
            bias = near[number, 2 * units : 2 * units + 1, :units].astype(F32)
        else:
            for copy in copies[near_count:]:
                copy.wait()
            shards = far.shape[0]
            piece = (far.shape[1] - EXT) // 2
            into = far[:, :piece].reshape(shards * piece, -1)
            out_of = far[:, piece : 2 * piece].reshape(shards * piece, -1)
            bias = jnp.concatenate(
                [far[i, 2 * piece : 2 * piece + 1, :piece].astype(F32) for i in range(shards)],
                axis=1,
            )
        before = [dot(part, into, NT) + bias for part in x]
        for i in range(2):
            pre = before[i]
            hidden = (0.5 * pre * (1.0 + lax.erf(pre * math.sqrt(0.5)))).astype(BF16)
            part = dot(hidden, out_of)
            total[i] = part if total[i] is None else total[i] + part
    own_ref[...] = total[0].astype(BF16)
    other_ref[...] = total[1].astype(BF16)


def mlp(x, pair, near, far=()):
    rows, width = x.shape
    shape = jax.ShapeDtypeStruct((rows, width), BF16)
    vmem = pl.BlockSpec(memory_space=pltpu.VMEM)
    units = (near[0].shape[0] - PAD) // 2
    groups = len(near) + (1 if far else 0)
    scratch = [pltpu.VMEM((len(near),) + near[0].shape, BF16)]
    if far:
        shards = sum(array.shape[0] for array in far)
        scratch.append(pltpu.VMEM((shards,) + far[0].shape[1:], BF16))
    scratch.append(pltpu.SemaphoreType.DMA((len(near) + len(far),)))
    return pl.pallas_call(
        lambda *refs: mlp_kernel(*refs, near_count=len(near), far_count=len(far)),
        out_shape=(shape, shape),
        in_specs=[vmem, vmem] + [pl.BlockSpec(memory_space=pl.ANY)] * (len(near) + len(far)),
        out_specs=(vmem, vmem),
        scratch_shapes=scratch,
        compiler_params=cparams(),
        cost_estimate=cost(8 * rows * groups * units * width, groups * (5 << 20)),
        name="mlp",
    )(x, in_vmem(pair), *near, *far)


def merge_kernel(res_ref, bias_ref, gain_ref, index_ref, owner_ref, *refs, cap):
    parts, out_refs = refs[:-RINGS], refs[-RINGS:]
    rows, width = res_ref.shape
    total = res_ref[...].astype(F32) + bias_ref[...].reshape(1, width)
    for part in parts:
        total = total + part[...].astype(F32)
    normed = (layer_norm(total) * gain_ref[...].reshape(1, width)).astype(BF16)
    count = rows // 4
    r = lax.broadcasted_iota(jnp.int32, (rows, rows), 0)
    s = lax.broadcasted_iota(jnp.int32, (rows, rows), 1)
    named = (index_ref[...] == r).astype(F32).astype(BF16)
    order = (s == 4 * (r % count) + r // count).astype(F32).astype(BF16)
    pick = dot(order, named, NT).astype(BF16)
    merged = dot(pick, normed).astype(BF16)
    size = count // RINGS
    for c in range(4):
        for i, out_ref in enumerate(out_refs):
            at = c * count + i * size
            out_ref[:, c * width : (c + 1) * width] = merged[at : at + size]
    across = owner_ref[...]
    r = lax.broadcasted_iota(jnp.int32, (count, count), 0)
    s = lax.broadcasted_iota(jnp.int32, (count, count), 1)
    owner = jnp.sum(jnp.where(r == s, across, 0), axis=1, keepdims=True)
    earlier = (across == owner) & (s < r)
    rank = jnp.sum(earlier.astype(jnp.int32), axis=1, keepdims=True)
    slot = (owner * cap + rank).astype(F32).astype(BF16)
    for i, out_ref in enumerate(out_refs):
        out_ref[:, 4 * width :] = jnp.broadcast_to(
            slot[i * size : (i + 1) * size], (size, LANES)
        )


def merge(residual, out_bias, merge_gain, merge_index, owners, parts, cap):
    rows, width = residual.shape
    operands = (
        residual,
        out_bias,
        merge_gain,
        merge_index.reshape(1, rows),
        owners.reshape(1, rows // 4),
        parts[0],
        *map(in_vmem, parts[1:]),
    )
    return pl.pallas_call(
        lambda *refs: merge_kernel(*refs, cap=cap),
        out_shape=(jax.ShapeDtypeStruct((rows // 4 // RINGS, 4 * width + LANES), BF16),) * RINGS,
        in_specs=[pl.BlockSpec(memory_space=pltpu.VMEM)] * len(operands),
        out_specs=(pl.BlockSpec(memory_space=pltpu.VMEM),) * RINGS,
        compiler_params=cparams(),
        cost_estimate=cost(2 * rows * rows * width, 4 << 20),
        name="merge",
    )(*operands)


def embed_kernel(*refs, pieces, cap, slots):
    x_refs = refs[: len(pieces)]
    w_hbm, bias_ref, out_ref, x_sc, w_sc, sems = refs[len(pieces) :]
    depth, cols = w_hbm.shape
    block = depth // 4
    copies = []
    for i in range(4):
        at = pl.ds(i * block, block)
        copies.append(pltpu.make_async_copy(w_hbm.at[at], w_sc.at[at], sems.at[i]))
        copies[-1].start()
    for at, x_ref in zip(pieces, x_refs):
        x_sc[at : at + x_ref.shape[0], :] = x_ref[...]
    embedded = jnp.broadcast_to(bias_ref[...].reshape(1, cols), (x_sc.shape[0], cols))
    for i in range(4):
        copies[i].wait()
        at = slice(i * block, (i + 1) * block)
        embedded = embedded + dot(x_sc[:, at], w_sc[at, :])
    embedded = embedded.astype(BF16)
    total = x_sc.shape[0]
    count = total // 4
    slot = x_sc[:, depth : depth + 1].astype(F32).astype(jnp.int32)
    owner = slot // cap
    rank = slot - owner * cap
    group = lax.axis_index("grp") + lax.broadcasted_iota(jnp.int32, (total, 1), 0) // count
    group = jnp.where(group >= 4, group - 4, group)
    target = owner * slots + group * cap + rank
    lane = lax.broadcasted_iota(jnp.int32, (total, out_ref.shape[0]), 1)
    place = (target == lane).astype(F32).T.astype(BF16)
    out_ref[...] = dot(place, embedded).astype(BF16)


def embed(pieces, w_merge, merge_bias, cap, slots, owners):
    arrays = [in_vmem(array) for _, array in pieces]
    rows = sum(array.shape[0] for array in arrays)
    depth, cols = w_merge.shape
    places = tuple(at for at, _ in pieces)
    return pl.pallas_call(
        lambda *refs: embed_kernel(*refs, pieces=places, cap=cap, slots=slots),
        out_shape=jax.ShapeDtypeStruct((owners * slots, cols), BF16),
        in_specs=[pl.BlockSpec(memory_space=pltpu.VMEM)] * len(arrays)
        + [pl.BlockSpec(memory_space=pl.ANY), pl.BlockSpec(memory_space=pltpu.VMEM)],
        out_specs=pl.BlockSpec(memory_space=pltpu.VMEM),
        scratch_shapes=[
            pltpu.VMEM((rows, arrays[0].shape[1]), BF16),
            pltpu.VMEM((depth, cols), BF16),
            pltpu.SemaphoreType.DMA((4,)),
        ],
        compiler_params=cparams(),
        cost_estimate=cost(2 * rows * depth * cols, 10 << 20),
        name="embed",
    )(*arrays, w_merge, merge_bias)


def flip(value, axis):
    return lax.ppermute(value, axis, [(0, 1), (1, 0)])


def turn(value, axis, by):
    size = lax.axis_size(axis)
    return lax.ppermute(value, axis, [(i, (i + by) % size) for i in range(size)])


def ring_gather(value, axis):
    before = turn(value, axis, 1)
    after = turn(value, axis, -1)
    half = value.shape[0] // 2
    return before, after, turn(before[:half], axis, 1), turn(after[half:], axis, -1)


def pack_kernel(in_ref, bias_ref, out_ref, pack_ref, row_sc, sc, sems, *, shares):
    size = sc.shape[0] // 2
    half = size * shares
    tail = row_sc.shape[0]
    core = lax.axis_index("c")
    first = pl.multiple_of(core * half, half)
    if shares > 1:
        chip = lax.axis_index(CHIPS)
        first = pl.multiple_of(first + chip * size, 16)
    copies = []
    for i, ref in enumerate((in_ref, out_ref)):
        source = ref.at[pl.ds(first, size)]
        copies.append(pltpu.make_async_copy(source, sc.at[pl.ds(i * size, size)], sems.at[i]))
        copies[-1].start()
    width = in_ref.shape[1]
    bias = bias_ref[...].astype(F32).reshape(1, 2 * half)
    bias = jnp.where(core == 0, bias[:, :half], bias[:, half:])
    bias = jnp.broadcast_to(bias, (tail, half))
    if shares > 1:
        bias = pltpu.roll(bias, jnp.where(chip == 0, 0, half - chip * size), 1)
    rest = jnp.zeros((tail, width - half), F32)
    row_sc[...] = jnp.concatenate([bias, rest], axis=1).astype(BF16)
    copies.append(
        pltpu.make_async_copy(row_sc, pack_ref.at[pl.ds(2 * size, tail)], sems.at[2])
    )
    copies[-1].start()
    for i in range(2):
        at = pl.ds(i * size, size)
        copies[i].wait()
        copies.append(pltpu.make_async_copy(sc.at[at], pack_ref.at[at], sems.at[3 + i]))
        copies[-1].start()
    for copy in copies[2:]:
        copy.wait()


def pack(w_in, in_bias, w_out, shares, tail):
    units, width = w_in.shape
    size = units // 2 // shares
    any_space = pl.BlockSpec(memory_space=pl.ANY)
    return pl.pallas_call(
        lambda *refs: pack_kernel(*refs, shares=shares),
        out_shape=jax.ShapeDtypeStruct((2 * size + tail, width), BF16),
        in_specs=[any_space, pl.BlockSpec(memory_space=pltpu.VMEM), any_space],
        out_specs=any_space,
        scratch_shapes=[
            pltpu.VMEM((tail, width), BF16),
            pltpu.VMEM((2 * size, width), BF16),
            pltpu.SemaphoreType.DMA((5,)),
        ],
        compiler_params=cparams(),
        cost_estimate=cost(0, 8 * size * width),
        name="pack",
    )(w_in, in_bias, w_out)


def local(
    tokens,
    seg_ids,
    merge_index,
    owners,
    w_qkv,
    w_attn_out,
    w_in,
    in_bias,
    w_out,
    out_bias,
    merge_gain,
    w_merge,
    merge_bias,
):
    far = turn(pack(w_in, in_bias, w_out, lax.axis_size(CHIPS), EXT), "grp", 2)
    near = pack(w_in, in_bias, w_out, 1, PAD)
    far, near = lax.optimization_barrier((far, near))
    row = [far] + [turn(far, ("xh", "xl"), by) for by in (1, 2, 3)]
    one, two = turn(near, "grp", 1), turn(near, "grp", -1)
    heads = qkv(tokens, seg_ids, w_qkv)
    row, heads = lax.optimization_barrier((row, heads))
    mine = lax.all_to_all(heads, ("y", "xh"), 0, 0, tiled=True)
    row, mine = lax.optimization_barrier((jnp.stack(row), mine))
    below, above = turn(row, "y", 1), turn(row, "y", -1)
    queries, kv = mine[:, : HD + EXT], mine[:, HD:]
    kv_c = flip(kv, "c")
    queries, kv_c = lax.optimization_barrier((queries, kv_c))
    away = flip(queries, "xl")
    acc = attend(queries, [kv])
    away, acc = lax.optimization_barrier((away, acc))
    sent = flip(attend(away, [kv, kv_c], send=True), "xl")
    acc = attend(queries, [kv_c], acc)
    below, above, acc = lax.optimization_barrier((below, above, acc))
    far_a, far_b = turn(below[:2], "y", 1), turn(above[2:], "y", -1)
    sent, acc = lax.optimization_barrier((sent, acc))
    done = combine(acc, sent)
    attended = lax.all_to_all(done, ("y", "xh"), 0, 0, tiled=True)
    far_a, far_b, attended = lax.optimization_barrier((far_a, far_b, attended))
    far = [row, below, above, far_a, far_b]
    residual, mlp_in = project(attended, tokens, w_attn_out)
    pair = flip(mlp_in, "c")
    own, other = mlp(mlp_in, pair, [near, one, two], far)
    parts = [own, flip(other, "c")]
    owner_count = lax.axis_size(("y", "xh", "xl", "c"))
    cap = 4
    merged = merge(residual, out_bias, merge_gain, merge_index, owners, parts, cap)
    size = merged[0].shape[0]
    count = size * RINGS
    pieces = []
    for i, part in enumerate(merged):
        before, after, far_a, far_b = ring_gather(part, "grp")
        at = i * size
        pieces += [
            (at, part),
            (count + at, after),
            (2 * count + at, far_a),
            (2 * count + at + size // 2, far_b),
            (3 * count + at, before),
        ]
    slots = 4 * cap
    outgoing = embed(pieces, w_merge, merge_bias, cap, slots, owner_count)
    cols = outgoing.shape[1]
    received = lax.all_to_all(outgoing, ("y", "xh", "xl", "c"), 0, 0, tiled=True)
    received = received.reshape(owner_count, 4, cap, cols)
    return received.transpose(1, 0, 2, 3).reshape(4 * owner_count * cap, cols)


def solution(mesh):
    inner = Mesh(mesh.devices.reshape(4, 4, 2, 2, 2), ("grp", "y", "xh", "xl", "c"))
    every = ("grp", "y", "xh", "xl", "c")
    tok = ("y", "xh", "xl", "c")
    placed = (
        P(every, None),
        P(every),
        P(every),
        P(every, None),
        P(),
        P(),
        P("grp", None),
        P("grp"),
        P("grp", None),
        P(),
        P(),
        P(None, "grp"),
        P("grp"),
    )
    return jax.shard_map(
        local, mesh=inner, in_specs=placed, out_specs=P(tok, "grp"), check_vma=False
    )
```

```python
import math

import jax
import jax.numpy as jnp
from jax import lax
from jax.experimental import pallas as pl
from jax.experimental.pallas import tpu as pltpu
from jax.sharding import Mesh
from jax.sharding import PartitionSpec as P

HEADS = 8
HD = 88
EXT = 8
NORM_EPS = 1e-06
LANES = 128
PAD = 16
RINGS = 2
CHIPS = ("y", "xh", "xl")
F32 = jnp.float32
BF16 = jnp.bfloat16
VMEM_LIMIT = 60 * 1024 * 1024


def cparams(*semantics):
    return pltpu.CompilerParams(
        dimension_semantics=semantics or None, vmem_limit_bytes=VMEM_LIMIT
    )


def in_vmem(value):
    return pltpu.with_memory_space_constraint(value, pltpu.VMEM)


def layer_norm(values):
    centred = values - jnp.mean(values, axis=-1, keepdims=True)
    return centred * lax.rsqrt(jnp.mean(centred * centred, axis=-1, keepdims=True) + NORM_EPS)


def dot(a, b, dims=(((1,), (0,)), ((), ()))):
    return lax.dot_general(a, b, dims, preferred_element_type=F32)


NT = (((1,), (1,)), ((), ()))


def cost(flops, size, transcendentals=0):
    return pl.CostEstimate(flops=flops, bytes_accessed=size, transcendentals=transcendentals)


def qkv_kernel(x_ref, seg_ref, w_hbm, out_ref, w_ref, sems):
    group = HEADS * HD
    count = w_ref.shape[0] // group
    copies = []
    for number in range(count):
        at = pl.ds(number * group, group)
        copies.append(pltpu.make_async_copy(w_hbm.at[at], w_ref.at[at], sems.at[number]))
        copies[-1].start()
    normed = layer_norm(x_ref[...].astype(F32)).astype(BF16)
    seg = seg_ref[...]
    high = seg // 64
    low = seg - high * 64
    tokens = seg.shape[1]
    row = lax.broadcasted_iota(jnp.int32, (EXT, tokens), 0)
    extra = jnp.where(row == 0, 1, jnp.where(row == 1, high, jnp.where(row == 2, low, 0)))
    extra = extra.astype(F32)
    scale = math.log2(math.e) / math.sqrt(HD)
    for number in range(count):
        copies[number].wait()
        part = dot(w_ref[number * group : (number + 1) * group, :], normed, NT)
        part = part.astype(BF16).astype(F32)
        for head in range(HEADS):
            rows = part[head * HD : (head + 1) * HD]
            if number == 2:
                out_ref[head, HD : 2 * HD + EXT] = jnp.concatenate([extra, rows], axis=0).astype(
                    BF16
                )
                continue
            norm = lax.rsqrt(jnp.mean(rows * rows, axis=0, keepdims=True) + NORM_EPS)
            if number == 0:
                out_ref[head, :HD] = (rows * (norm * scale)).astype(BF16)
            else:
                out_ref[head, 2 * HD + EXT :] = (rows * norm).astype(BF16)


def qkv(tokens, seg_ids, w_qkv):
    rows, width = tokens.shape
    return pl.pallas_call(
        qkv_kernel,
        out_shape=jax.ShapeDtypeStruct((HEADS, 3 * HD + EXT, rows), BF16),
        in_specs=[
            pl.BlockSpec(memory_space=pltpu.VMEM),
            pl.BlockSpec(memory_space=pltpu.VMEM),
            pl.BlockSpec(memory_space=pl.ANY),
        ],
        out_specs=pl.BlockSpec(memory_space=pltpu.VMEM),
        scratch_shapes=[
            pltpu.VMEM((w_qkv.shape[1], width), BF16),
            pltpu.SemaphoreType.DMA((3,)),
        ],
        compiler_params=cparams(),
        cost_estimate=cost(2 * rows * width * w_qkv.shape[1], 8 << 20),
        name="qkv",
    )(tokens, seg_ids.reshape(1, rows), w_qkv.T)


def attend_kernel(*refs, sets, first, send, key_block, unroll):
    q_ref = refs[0]
    kv_refs = refs[1 : 1 + sets]
    rest = refs[1 + sets :]
    if not first:
        acc_ref, rest = rest[0], rest[1:]
    out_ref, k_sc, v_sc, seg_sc = rest
    blocks, top, tokens = q_ref.shape
    width = LANES - HD
    for number, kv_ref in enumerate(kv_refs):
        for j in range(blocks):
            start = (number * blocks + j) * tokens
            digits = kv_ref[j, : 2 * EXT].astype(F32)
            seg = digits[1:2] * 64.0 + digits[2:3]
            keys = kv_ref[j, top:].astype(F32)
            both = jnp.concatenate([keys, jnp.broadcast_to(seg, (width, tokens))], axis=0).T
            v_sc[:, start : start + tokens] = kv_ref[j, :top]
            k_sc[start : start + tokens, :] = both.astype(BF16)
            seg_sc[start : start + tokens, :] = jnp.broadcast_to(
                both[:, HD : HD + 1], (tokens, LANES)
            )

    def tile(i):
        at_q = pl.ds(pl.multiple_of(i * tokens, tokens), tokens)
        mine = q_ref[i].astype(F32)
        q = jnp.concatenate([mine[:HD], jnp.zeros((width, tokens), F32)], axis=0).astype(BF16)
        seg = mine[HD + 1 : HD + 2] * 64.0 + mine[HD + 2 : HD + 3]
        total = None
        for start in range(0, sets * blocks * tokens, key_block):
            at = slice(start, start + key_block)
            scores = dot(k_sc[at, :], q)
            of_key = seg_sc[at, :]
            of_key = jnp.concatenate([of_key] * (tokens // LANES), axis=1)
            weights = jnp.where(of_key == seg, jnp.exp2(scores), 0.0).astype(BF16)
            part = dot(v_sc[:, at], weights)
            total = part if total is None else total + part
        if not first:
            total = total + acc_ref[:, at_q]
        if send:
            near = total[:1].astype(BF16).astype(F32)
            rows = [near, total[:1] - near, jnp.zeros((EXT - 2, tokens), F32), total[EXT:]]
            out_ref[i] = jnp.concatenate(rows, axis=0).astype(BF16)
        else:
            out_ref[:, at_q] = total

    def step(i, carry):
        for j in range(unroll):
            tile(i * unroll + j)
        return carry

    lax.fori_loop(0, blocks // unroll, step, 0)


def attend(queries, sets, acc=None, send=False, key_block=512, unroll=4):
    blocks, top, tokens = queries.shape
    total = blocks * tokens
    keys = total * len(sets)
    first = acc is None
    if send:
        shape = jax.ShapeDtypeStruct(queries.shape, BF16)
    else:
        shape = jax.ShapeDtypeStruct((top, total), F32)
    operands = [in_vmem(queries), *map(in_vmem, sets)]
    if not first:
        operands.append(in_vmem(acc))
    return pl.pallas_call(
        lambda *refs: attend_kernel(
            *refs, sets=len(sets), first=first, send=send, key_block=key_block, unroll=unroll
        ),
        out_shape=shape,
        in_specs=[pl.BlockSpec(memory_space=pltpu.VMEM)] * len(operands),
        out_specs=pl.BlockSpec(memory_space=pltpu.VMEM),
        scratch_shapes=[
            pltpu.VMEM((keys, LANES), BF16),
            pltpu.VMEM((top, keys), BF16),
            pltpu.VMEM((keys, LANES), F32),
        ],
        compiler_params=cparams(),
        cost_estimate=cost(4 * total * keys * LANES, 3 << 20, total * keys),
        name="attend",
    )(*operands)


def combine_kernel(acc_ref, sent_ref, out_ref):
    blocks, _, tokens = sent_ref.shape
    for i in range(blocks):
        acc = acc_ref[:, i * tokens : (i + 1) * tokens]
        sent = sent_ref[i].astype(F32)
        weight = acc[:1] + (sent[:1] + sent[1:2])
        out_ref[i] = ((acc[EXT:] + sent[EXT:]) / weight).astype(BF16)


def combine(acc, sent):
    blocks, top, tokens = sent.shape
    return pl.pallas_call(
        combine_kernel,
        out_shape=jax.ShapeDtypeStruct((blocks, top - EXT, tokens), BF16),
        in_specs=[pl.BlockSpec(memory_space=pltpu.VMEM)] * 2,
        out_specs=pl.BlockSpec(memory_space=pltpu.VMEM),
        compiler_params=cparams(),
        cost_estimate=cost(0, 2 << 20),
        name="combine",
    )(in_vmem(acc), in_vmem(sent))


def project_kernel(att_ref, x_ref, w_ref, res_ref, in_ref):
    heads, _, tokens = att_ref.shape
    att = att_ref[...].astype(F32).reshape(heads * HD, tokens).T.astype(BF16)
    residual = (x_ref[...].astype(F32) + dot(att, w_ref[...])).astype(BF16)
    res_ref[...] = residual
    in_ref[...] = layer_norm(residual.astype(F32)).astype(BF16)


def project(attended, tokens, w_attn_out):
    shape = jax.ShapeDtypeStruct(tokens.shape, BF16)
    return pl.pallas_call(
        project_kernel,
        out_shape=(shape, shape),
        in_specs=[pl.BlockSpec(memory_space=pltpu.VMEM)] * 3,
        out_specs=(pl.BlockSpec(memory_space=pltpu.VMEM),) * 2,
        compiler_params=cparams(),
        cost_estimate=cost(2 * tokens.shape[0] * w_attn_out.shape[0] * w_attn_out.shape[1], 4 << 20),
        name="project",
    )(in_vmem(attended), tokens, w_attn_out)


def mlp_kernel(x_ref, pair_ref, *refs, near_count, far_count):
    near_refs, far_refs = refs[:near_count], refs[near_count : near_count + far_count]
    rest = refs[near_count + far_count :]
    own_ref, other_ref, near = rest[:3]
    far, sems = (rest[3], rest[4]) if far_count else (None, rest[3])
    copies = []
    for number, ref in enumerate(near_refs):
        copies.append(pltpu.make_async_copy(ref, near.at[number], sems.at[number]))
    at = 0
    for number, ref in enumerate(far_refs):
        target = far.at[pl.ds(at, ref.shape[0])]
        copies.append(pltpu.make_async_copy(ref, target, sems.at[near_count + number]))
        at += ref.shape[0]
    for copy in copies:
        copy.start()
    units = (near.shape[1] - PAD) // 2
    x = x_ref[...], pair_ref[...]
    total = [None, None]
    for number in range(near_count + (1 if far_count else 0)):
        if number < near_count:
            copies[number].wait()
            into = near[number, :units]
            out_of = near[number, units : 2 * units]
            bias = near[number, 2 * units : 2 * units + 1, :units].astype(F32)
        else:
            for copy in copies[near_count:]:
                copy.wait()
            shards = far.shape[0]
            piece = (far.shape[1] - EXT) // 2
            into = far[:, :piece].reshape(shards * piece, -1)
            out_of = far[:, piece : 2 * piece].reshape(shards * piece, -1)
            bias = jnp.concatenate(
                [far[i, 2 * piece : 2 * piece + 1, :piece].astype(F32) for i in range(shards)],
                axis=1,
            )
        before = [dot(part, into, NT) + bias for part in x]
        for i in range(2):
            pre = before[i]
            hidden = (0.5 * pre * (1.0 + lax.erf(pre * math.sqrt(0.5)))).astype(BF16)
            part = dot(hidden, out_of)
            total[i] = part if total[i] is None else total[i] + part
    own_ref[...] = total[0].astype(BF16)
    other_ref[...] = total[1].astype(BF16)


def mlp(x, pair, near, far=()):
    rows, width = x.shape
    shape = jax.ShapeDtypeStruct((rows, width), BF16)
    vmem = pl.BlockSpec(memory_space=pltpu.VMEM)
    units = (near[0].shape[0] - PAD) // 2
    groups = len(near) + (1 if far else 0)
    scratch = [pltpu.VMEM((len(near),) + near[0].shape, BF16)]
    if far:
        shards = sum(array.shape[0] for array in far)
        scratch.append(pltpu.VMEM((shards,) + far[0].shape[1:], BF16))
    scratch.append(pltpu.SemaphoreType.DMA((len(near) + len(far),)))
    return pl.pallas_call(
        lambda *refs: mlp_kernel(*refs, near_count=len(near), far_count=len(far)),
        out_shape=(shape, shape),
        in_specs=[vmem, vmem] + [pl.BlockSpec(memory_space=pl.ANY)] * (len(near) + len(far)),
        out_specs=(vmem, vmem),
        scratch_shapes=scratch,
        compiler_params=cparams(),
        cost_estimate=cost(8 * rows * groups * units * width, groups * (5 << 20)),
        name="mlp",
    )(x, in_vmem(pair), *near, *far)


def merge_kernel(res_ref, bias_ref, gain_ref, index_ref, owner_ref, *refs, cap):
    parts, out_refs = refs[:-RINGS], refs[-RINGS:]
    rows, width = res_ref.shape
    total = res_ref[...].astype(F32) + bias_ref[...].reshape(1, width)
    for part in parts:
        total = total + part[...].astype(F32)
    normed = (layer_norm(total) * gain_ref[...].reshape(1, width)).astype(BF16)
    count = rows // 4
    r = lax.broadcasted_iota(jnp.int32, (rows, rows), 0)
    s = lax.broadcasted_iota(jnp.int32, (rows, rows), 1)
    named = (index_ref[...] == r).astype(F32).astype(BF16)
    order = (s == 4 * (r % count) + r // count).astype(F32).astype(BF16)
    pick = dot(order, named, NT).astype(BF16)
    merged = dot(pick, normed).astype(BF16)
    size = count // RINGS
    for c in range(4):
        for i, out_ref in enumerate(out_refs):
            at = c * count + i * size
            out_ref[:, c * width : (c + 1) * width] = merged[at : at + size]
    across = owner_ref[...]
    r = lax.broadcasted_iota(jnp.int32, (count, count), 0)
    s = lax.broadcasted_iota(jnp.int32, (count, count), 1)
    owner = jnp.sum(jnp.where(r == s, across, 0), axis=1, keepdims=True)
    earlier = (across == owner) & (s < r)
    rank = jnp.sum(earlier.astype(jnp.int32), axis=1, keepdims=True)
    slot = (owner * cap + rank).astype(F32).astype(BF16)
    for i, out_ref in enumerate(out_refs):
        out_ref[:, 4 * width :] = jnp.broadcast_to(
            slot[i * size : (i + 1) * size], (size, LANES)
        )


def merge(residual, out_bias, merge_gain, merge_index, owners, parts, cap):
    rows, width = residual.shape
    operands = (
        residual,
        out_bias,
        merge_gain,
        merge_index.reshape(1, rows),
        owners.reshape(1, rows // 4),
        parts[0],
        *map(in_vmem, parts[1:]),
    )
    return pl.pallas_call(
        lambda *refs: merge_kernel(*refs, cap=cap),
        out_shape=(jax.ShapeDtypeStruct((rows // 4 // RINGS, 4 * width + LANES), BF16),) * RINGS,
        in_specs=[pl.BlockSpec(memory_space=pltpu.VMEM)] * len(operands),
        out_specs=(pl.BlockSpec(memory_space=pltpu.VMEM),) * RINGS,
        compiler_params=cparams(),
        cost_estimate=cost(2 * rows * rows * width, 4 << 20),
        name="merge",
    )(*operands)


def embed_kernel(*refs, pieces, cap, slots):
    x_refs = refs[: len(pieces)]
    w_hbm, bias_ref, out_ref, x_sc, w_sc, sems = refs[len(pieces) :]
    depth, cols = w_hbm.shape
    block = depth // 4
    copies = []
    for i in range(4):
        at = pl.ds(i * block, block)
        copies.append(pltpu.make_async_copy(w_hbm.at[at], w_sc.at[at], sems.at[i]))
        copies[-1].start()
    for at, x_ref in zip(pieces, x_refs):
        x_sc[at : at + x_ref.shape[0], :] = x_ref[...]
    embedded = jnp.broadcast_to(bias_ref[...].reshape(1, cols), (x_sc.shape[0], cols))
    for i in range(4):
        copies[i].wait()
        at = slice(i * block, (i + 1) * block)
        embedded = embedded + dot(x_sc[:, at], w_sc[at, :])
    embedded = embedded.astype(BF16)
    total = x_sc.shape[0]
    count = total // 4
    slot = x_sc[:, depth : depth + 1].astype(F32).astype(jnp.int32)
    owner = slot // cap
    rank = slot - owner * cap
    group = lax.axis_index("grp") + lax.broadcasted_iota(jnp.int32, (total, 1), 0) // count
    group = jnp.where(group >= 4, group - 4, group)
    target = owner * slots + group * cap + rank
    lane = lax.broadcasted_iota(jnp.int32, (total, out_ref.shape[0]), 1)
    place = (target == lane).astype(F32).T.astype(BF16)
    out_ref[...] = dot(place, embedded).astype(BF16)


def embed(pieces, w_merge, merge_bias, cap, slots, owners):
    arrays = [in_vmem(array) for _, array in pieces]
    rows = sum(array.shape[0] for array in arrays)
    depth, cols = w_merge.shape
    places = tuple(at for at, _ in pieces)
    return pl.pallas_call(
        lambda *refs: embed_kernel(*refs, pieces=places, cap=cap, slots=slots),
        out_shape=jax.ShapeDtypeStruct((owners * slots, cols), BF16),
        in_specs=[pl.BlockSpec(memory_space=pltpu.VMEM)] * len(arrays)
        + [pl.BlockSpec(memory_space=pl.ANY), pl.BlockSpec(memory_space=pltpu.VMEM)],
        out_specs=pl.BlockSpec(memory_space=pltpu.VMEM),
        scratch_shapes=[
            pltpu.VMEM((rows, arrays[0].shape[1]), BF16),
            pltpu.VMEM((depth, cols), BF16),
            pltpu.SemaphoreType.DMA((4,)),
        ],
        compiler_params=cparams(),
        cost_estimate=cost(2 * rows * depth * cols, 10 << 20),
        name="embed",
    )(*arrays, w_merge, merge_bias)


def flip(value, axis):
    return lax.ppermute(value, axis, [(0, 1), (1, 0)])


def turn(value, axis, by):
    size = lax.axis_size(axis)
    return lax.ppermute(value, axis, [(i, (i + by) % size) for i in range(size)])


def ring_gather(value, axis):
    before = turn(value, axis, 1)
    after = turn(value, axis, -1)
    half = value.shape[0] // 2
    return before, after, turn(before[:half], axis, 1), turn(after[half:], axis, -1)


def pack_kernel(in_ref, bias_ref, out_ref, pack_ref, row_sc, sc, sems, *, shares):
    size = sc.shape[0] // 2
    half = size * shares
    tail = row_sc.shape[0]
    core = lax.axis_index("c")
    first = pl.multiple_of(core * half, half)
    if shares > 1:
        chip = lax.axis_index(CHIPS)
        first = pl.multiple_of(first + chip * size, 16)
    copies = []
    for i, ref in enumerate((in_ref, out_ref)):
        source = ref.at[pl.ds(first, size)]
        copies.append(pltpu.make_async_copy(source, sc.at[pl.ds(i * size, size)], sems.at[i]))
        copies[-1].start()
    width = in_ref.shape[1]
    bias = bias_ref[...].astype(F32).reshape(1, 2 * half)
    bias = jnp.where(core == 0, bias[:, :half], bias[:, half:])
    bias = jnp.broadcast_to(bias, (tail, half))
    if shares > 1:
        bias = pltpu.roll(bias, jnp.where(chip == 0, 0, half - chip * size), 1)
    rest = jnp.zeros((tail, width - half), F32)
    row_sc[...] = jnp.concatenate([bias, rest], axis=1).astype(BF16)
    copies.append(
        pltpu.make_async_copy(row_sc, pack_ref.at[pl.ds(2 * size, tail)], sems.at[2])
    )
    copies[-1].start()
    for i in range(2):
        at = pl.ds(i * size, size)
        copies[i].wait()
        copies.append(pltpu.make_async_copy(sc.at[at], pack_ref.at[at], sems.at[3 + i]))
        copies[-1].start()
    for copy in copies[2:]:
        copy.wait()


def pack(w_in, in_bias, w_out, shares, tail):
    units, width = w_in.shape
    size = units // 2 // shares
    any_space = pl.BlockSpec(memory_space=pl.ANY)
    return pl.pallas_call(
        lambda *refs: pack_kernel(*refs, shares=shares),
        out_shape=jax.ShapeDtypeStruct((2 * size + tail, width), BF16),
        in_specs=[any_space, pl.BlockSpec(memory_space=pltpu.VMEM), any_space],
        out_specs=any_space,
        scratch_shapes=[
            pltpu.VMEM((tail, width), BF16),
            pltpu.VMEM((2 * size, width), BF16),
            pltpu.SemaphoreType.DMA((5,)),
        ],
        compiler_params=cparams(),
        cost_estimate=cost(0, 8 * size * width),
        name="pack",
    )(w_in, in_bias, w_out)


def local(
    tokens,
    seg_ids,
    merge_index,
    owners,
    w_qkv,
    w_attn_out,
    w_in,
    in_bias,
    w_out,
    out_bias,
    merge_gain,
    w_merge,
    merge_bias,
):
    far = turn(pack(w_in, in_bias, w_out, lax.axis_size(CHIPS), EXT), "grp", 2)
    near = pack(w_in, in_bias, w_out, 1, PAD)
    far, near = lax.optimization_barrier((far, near))
    row = [far] + [turn(far, ("xh", "xl"), by) for by in (1, 2, 3)]
    one, two = turn(near, "grp", 1), turn(near, "grp", -1)
    heads = qkv(tokens, seg_ids, w_qkv)
    row[1], row[3], heads = lax.optimization_barrier((row[1], row[3], heads))
    mine = lax.all_to_all(heads, ("y", "xh"), 0, 0, tiled=True)
    row, mine = lax.optimization_barrier((jnp.stack(row), mine))
    below, above = turn(row, "y", 1), turn(row, "y", -1)
    queries, kv = mine[:, : HD + EXT], mine[:, HD:]
    kv_c = flip(kv, "c")
    queries, kv_c = lax.optimization_barrier((queries, kv_c))
    away = flip(queries, "xl")
    acc = attend(queries, [kv])
    away, acc = lax.optimization_barrier((away, acc))
    sent = flip(attend(away, [kv, kv_c], send=True), "xl")
    acc = attend(queries, [kv_c], acc)
    below, above, acc = lax.optimization_barrier((below, above, acc))
    far_a, far_b = turn(below[:2], "y", 1), turn(above[2:], "y", -1)
    sent, acc = lax.optimization_barrier((sent, acc))
    done = combine(acc, sent)
    attended = lax.all_to_all(done, ("y", "xh"), 0, 0, tiled=True)
    far_a, far_b, attended = lax.optimization_barrier((far_a, far_b, attended))
    far = [row, below, above, far_a, far_b]
    residual, mlp_in = project(attended, tokens, w_attn_out)
    pair = flip(mlp_in, "c")
    own, other = mlp(mlp_in, pair, [near, one, two], far)
    parts = [own, flip(other, "c")]
    owner_count = lax.axis_size(("y", "xh", "xl", "c"))
    cap = 4
    merged = merge(residual, out_bias, merge_gain, merge_index, owners, parts, cap)
    size = merged[0].shape[0]
    count = size * RINGS
    pieces = []
    for i, part in enumerate(merged):
        before, after, far_a, far_b = ring_gather(part, "grp")
        at = i * size
        pieces += [
            (at, part),
            (count + at, after),
            (2 * count + at, far_a),
            (2 * count + at + size // 2, far_b),
            (3 * count + at, before),
        ]
    slots = 4 * cap
    outgoing = embed(pieces, w_merge, merge_bias, cap, slots, owner_count)
    cols = outgoing.shape[1]
    received = lax.all_to_all(outgoing, ("y", "xh", "xl", "c"), 0, 0, tiled=True)
    received = received.reshape(owner_count, 4, cap, cols)
    return received.transpose(1, 0, 2, 3).reshape(4 * owner_count * cap, cols)


def solution(mesh):
    inner = Mesh(mesh.devices.reshape(4, 4, 2, 2, 2), ("grp", "y", "xh", "xl", "c"))
    every = ("grp", "y", "xh", "xl", "c")
    tok = ("y", "xh", "xl", "c")
    placed = (
        P(every, None),
        P(every),
        P(every),
        P(every, None),
        P(),
        P(),
        P("grp", None),
        P("grp"),
        P("grp", None),
        P(),
        P(),
        P(None, "grp"),
        P("grp"),
    )
    return jax.shard_map(
        local, mesh=inner, in_specs=placed, out_specs=P(tok, "grp"), check_vma=False
    )
```

```python
import math

import jax
import jax.numpy as jnp
from jax import lax
from jax.experimental import pallas as pl
from jax.experimental.pallas import tpu as pltpu
from jax.sharding import Mesh
from jax.sharding import PartitionSpec as P

HEADS = 8
HD = 88
EXT = 8
NORM_EPS = 1e-06
LANES = 128
PAD = 16
RINGS = 2
CHIPS = ("y", "xh", "xl")
F32 = jnp.float32
BF16 = jnp.bfloat16
VMEM_LIMIT = 60 * 1024 * 1024


def cparams(*semantics):
    return pltpu.CompilerParams(
        dimension_semantics=semantics or None, vmem_limit_bytes=VMEM_LIMIT
    )


def in_vmem(value):
    return pltpu.with_memory_space_constraint(value, pltpu.VMEM)


def layer_norm(values):
    centred = values - jnp.mean(values, axis=-1, keepdims=True)
    return centred * lax.rsqrt(jnp.mean(centred * centred, axis=-1, keepdims=True) + NORM_EPS)


def dot(a, b, dims=(((1,), (0,)), ((), ()))):
    return lax.dot_general(a, b, dims, preferred_element_type=F32)


NT = (((1,), (1,)), ((), ()))


def cost(flops, size, transcendentals=0):
    return pl.CostEstimate(flops=flops, bytes_accessed=size, transcendentals=transcendentals)


def qkv_kernel(x_ref, seg_ref, w_hbm, out_ref, w_ref, sems):
    group = HEADS // 2 * HD
    count = w_ref.shape[0] // group
    copies = []
    for number in range(count):
        at = pl.ds(number * group, group)
        copies.append(pltpu.make_async_copy(w_hbm.at[at], w_ref.at[at], sems.at[number]))
        copies[-1].start()
    normed = layer_norm(x_ref[...].astype(F32)).astype(BF16)
    seg = seg_ref[...]
    high = seg // 64
    low = seg - high * 64
    tokens = seg.shape[1]
    row = lax.broadcasted_iota(jnp.int32, (EXT, tokens), 0)
    extra = jnp.where(row == 0, 1, jnp.where(row == 1, high, jnp.where(row == 2, low, 0)))
    extra = extra.astype(F32)
    scale = math.log2(math.e) / math.sqrt(HD)
    for number in range(count):
        copies[number].wait()
        part = dot(w_ref[number * group : (number + 1) * group, :], normed, NT)
        part = part.astype(BF16).astype(F32)
        kind = number // 2
        for i in range(HEADS // 2):
            head = number % 2 * (HEADS // 2) + i
            rows = part[i * HD : (i + 1) * HD]
            if kind == 2:
                out_ref[head, HD : 2 * HD + EXT] = jnp.concatenate([extra, rows], axis=0).astype(
                    BF16
                )
                continue
            norm = lax.rsqrt(jnp.mean(rows * rows, axis=0, keepdims=True) + NORM_EPS)
            if kind == 0:
                out_ref[head, :HD] = (rows * (norm * scale)).astype(BF16)
            else:
                out_ref[head, 2 * HD + EXT :] = (rows * norm).astype(BF16)


def qkv(tokens, seg_ids, w_qkv):
    rows, width = tokens.shape
    return pl.pallas_call(
        qkv_kernel,
        out_shape=jax.ShapeDtypeStruct((HEADS, 3 * HD + EXT, rows), BF16),
        in_specs=[
            pl.BlockSpec(memory_space=pltpu.VMEM),
            pl.BlockSpec(memory_space=pltpu.VMEM),
            pl.BlockSpec(memory_space=pl.ANY),
        ],
        out_specs=pl.BlockSpec(memory_space=pltpu.VMEM),
        scratch_shapes=[
            pltpu.VMEM((w_qkv.shape[1], width), BF16),
            pltpu.SemaphoreType.DMA((6,)),
        ],
        compiler_params=cparams(),
        cost_estimate=cost(2 * rows * width * w_qkv.shape[1], 8 << 20),
        name="qkv",
    )(tokens, seg_ids.reshape(1, rows), w_qkv.T)


def attend_kernel(*refs, sets, first, send, key_block, unroll):
    q_ref = refs[0]
    kv_refs = refs[1 : 1 + sets]
    rest = refs[1 + sets :]
    if not first:
        acc_ref, rest = rest[0], rest[1:]
    out_ref, k_sc, v_sc, seg_sc = rest
    blocks, top, tokens = q_ref.shape
    width = LANES - HD
    for number, kv_ref in enumerate(kv_refs):
        for j in range(blocks):
            start = (number * blocks + j) * tokens
            digits = kv_ref[j, : 2 * EXT].astype(F32)
            seg = digits[1:2] * 64.0 + digits[2:3]
            keys = kv_ref[j, top:].astype(F32)
            both = jnp.concatenate([keys, jnp.broadcast_to(seg, (width, tokens))], axis=0).T
            v_sc[:, start : start + tokens] = kv_ref[j, :top]
            k_sc[start : start + tokens, :] = both.astype(BF16)
            seg_sc[start : start + tokens, :] = jnp.broadcast_to(
                both[:, HD : HD + 1], (tokens, LANES)
            )

    def tile(i):
        at_q = pl.ds(pl.multiple_of(i * tokens, tokens), tokens)
        mine = q_ref[i].astype(F32)
        q = jnp.concatenate([mine[:HD], jnp.zeros((width, tokens), F32)], axis=0).astype(BF16)
        seg = mine[HD + 1 : HD + 2] * 64.0 + mine[HD + 2 : HD + 3]
        total = None
        for start in range(0, sets * blocks * tokens, key_block):
            at = slice(start, start + key_block)
            scores = dot(k_sc[at, :], q)
            of_key = seg_sc[at, :]
            of_key = jnp.concatenate([of_key] * (tokens // LANES), axis=1)
            weights = jnp.where(of_key == seg, jnp.exp2(scores), 0.0).astype(BF16)
            part = dot(v_sc[:, at], weights)
            total = part if total is None else total + part
        if not first:
            total = total + acc_ref[:, at_q]
        if send:
            near = total[:1].astype(BF16).astype(F32)
            rows = [near, total[:1] - near, jnp.zeros((EXT - 2, tokens), F32), total[EXT:]]
            out_ref[i] = jnp.concatenate(rows, axis=0).astype(BF16)
        else:
            out_ref[:, at_q] = total

    def step(i, carry):
        for j in range(unroll):
            tile(i * unroll + j)
        return carry

    lax.fori_loop(0, blocks // unroll, step, 0)


def attend(queries, sets, acc=None, send=False, key_block=512, unroll=4):
    blocks, top, tokens = queries.shape
    total = blocks * tokens
    keys = total * len(sets)
    first = acc is None
    if send:
        shape = jax.ShapeDtypeStruct(queries.shape, BF16)
    else:
        shape = jax.ShapeDtypeStruct((top, total), F32)
    operands = [in_vmem(queries), *map(in_vmem, sets)]
    if not first:
        operands.append(in_vmem(acc))
    return pl.pallas_call(
        lambda *refs: attend_kernel(
            *refs, sets=len(sets), first=first, send=send, key_block=key_block, unroll=unroll
        ),
        out_shape=shape,
        in_specs=[pl.BlockSpec(memory_space=pltpu.VMEM)] * len(operands),
        out_specs=pl.BlockSpec(memory_space=pltpu.VMEM),
        scratch_shapes=[
            pltpu.VMEM((keys, LANES), BF16),
            pltpu.VMEM((top, keys), BF16),
            pltpu.VMEM((keys, LANES), F32),
        ],
        compiler_params=cparams(),
        cost_estimate=cost(4 * total * keys * LANES, 3 << 20, total * keys),
        name="attend",
    )(*operands)


def combine_kernel(acc_ref, sent_ref, out_ref):
    blocks, _, tokens = sent_ref.shape
    for i in range(blocks):
        acc = acc_ref[:, i * tokens : (i + 1) * tokens]
        sent = sent_ref[i].astype(F32)
        weight = acc[:1] + (sent[:1] + sent[1:2])
        out_ref[i] = ((acc[EXT:] + sent[EXT:]) / weight).astype(BF16)


def combine(acc, sent):
    blocks, top, tokens = sent.shape
    return pl.pallas_call(
        combine_kernel,
        out_shape=jax.ShapeDtypeStruct((blocks, top - EXT, tokens), BF16),
        in_specs=[pl.BlockSpec(memory_space=pltpu.VMEM)] * 2,
        out_specs=pl.BlockSpec(memory_space=pltpu.VMEM),
        compiler_params=cparams(),
        cost_estimate=cost(0, 2 << 20),
        name="combine",
    )(in_vmem(acc), in_vmem(sent))


def project_kernel(att_ref, x_ref, w_ref, res_ref, in_ref):
    heads, _, tokens = att_ref.shape
    att = att_ref[...].astype(F32).reshape(heads * HD, tokens).T.astype(BF16)
    residual = (x_ref[...].astype(F32) + dot(att, w_ref[...])).astype(BF16)
    res_ref[...] = residual
    in_ref[...] = layer_norm(residual.astype(F32)).astype(BF16)


def project(attended, tokens, w_attn_out):
    shape = jax.ShapeDtypeStruct(tokens.shape, BF16)
    return pl.pallas_call(
        project_kernel,
        out_shape=(shape, shape),
        in_specs=[pl.BlockSpec(memory_space=pltpu.VMEM)] * 3,
        out_specs=(pl.BlockSpec(memory_space=pltpu.VMEM),) * 2,
        compiler_params=cparams(),
        cost_estimate=cost(2 * tokens.shape[0] * w_attn_out.shape[0] * w_attn_out.shape[1], 4 << 20),
        name="project",
    )(in_vmem(attended), tokens, w_attn_out)


def mlp_kernel(x_ref, pair_ref, *refs, near_count, far_count):
    near_refs, far_refs = refs[:near_count], refs[near_count : near_count + far_count]
    rest = refs[near_count + far_count :]
    own_ref, other_ref, near = rest[:3]
    far, sems = (rest[3], rest[4]) if far_count else (None, rest[3])
    copies = []
    for number, ref in enumerate(near_refs):
        copies.append(pltpu.make_async_copy(ref, near.at[number], sems.at[number]))
    at = 0
    for number, ref in enumerate(far_refs):
        target = far.at[pl.ds(at, ref.shape[0])]
        copies.append(pltpu.make_async_copy(ref, target, sems.at[near_count + number]))
        at += ref.shape[0]
    for copy in copies:
        copy.start()
    units = (near.shape[1] - PAD) // 2
    x = x_ref[...], pair_ref[...]
    total = [None, None]
    for number in range(near_count + (1 if far_count else 0)):
        if number < near_count:
            copies[number].wait()
            into = near[number, :units]
            out_of = near[number, units : 2 * units]
            bias = near[number, 2 * units : 2 * units + 1, :units].astype(F32)
        else:
            for copy in copies[near_count:]:
                copy.wait()
            shards = far.shape[0]
            piece = (far.shape[1] - EXT) // 2
            into = far[:, :piece].reshape(shards * piece, -1)
            out_of = far[:, piece : 2 * piece].reshape(shards * piece, -1)
            bias = jnp.concatenate(
                [far[i, 2 * piece : 2 * piece + 1, :piece].astype(F32) for i in range(shards)],
                axis=1,
            )
        before = [dot(part, into, NT) + bias for part in x]
        for i in range(2):
            pre = before[i]
            hidden = (0.5 * pre * (1.0 + lax.erf(pre * math.sqrt(0.5)))).astype(BF16)
            part = dot(hidden, out_of)
            total[i] = part if total[i] is None else total[i] + part
    own_ref[...] = total[0].astype(BF16)
    other_ref[...] = total[1].astype(BF16)


def mlp(x, pair, near, far=()):
    rows, width = x.shape
    shape = jax.ShapeDtypeStruct((rows, width), BF16)
    vmem = pl.BlockSpec(memory_space=pltpu.VMEM)
    units = (near[0].shape[0] - PAD) // 2
    groups = len(near) + (1 if far else 0)
    scratch = [pltpu.VMEM((len(near),) + near[0].shape, BF16)]
    if far:
        shards = sum(array.shape[0] for array in far)
        scratch.append(pltpu.VMEM((shards,) + far[0].shape[1:], BF16))
    scratch.append(pltpu.SemaphoreType.DMA((len(near) + len(far),)))
    return pl.pallas_call(
        lambda *refs: mlp_kernel(*refs, near_count=len(near), far_count=len(far)),
        out_shape=(shape, shape),
        in_specs=[vmem, vmem] + [pl.BlockSpec(memory_space=pl.ANY)] * (len(near) + len(far)),
        out_specs=(vmem, vmem),
        scratch_shapes=scratch,
        compiler_params=cparams(),
        cost_estimate=cost(8 * rows * groups * units * width, groups * (5 << 20)),
        name="mlp",
    )(x, in_vmem(pair), *near, *far)


def merge_kernel(res_ref, bias_ref, gain_ref, index_ref, owner_ref, *refs, cap):
    parts, out_refs = refs[:-RINGS], refs[-RINGS:]
    rows, width = res_ref.shape
    total = res_ref[...].astype(F32) + bias_ref[...].reshape(1, width)
    for part in parts:
        total = total + part[...].astype(F32)
    normed = (layer_norm(total) * gain_ref[...].reshape(1, width)).astype(BF16)
    count = rows // 4
    r = lax.broadcasted_iota(jnp.int32, (rows, rows), 0)
    s = lax.broadcasted_iota(jnp.int32, (rows, rows), 1)
    named = (index_ref[...] == r).astype(F32).astype(BF16)
    order = (s == 4 * (r % count) + r // count).astype(F32).astype(BF16)
    pick = dot(order, named, NT).astype(BF16)
    merged = dot(pick, normed).astype(BF16)
    size = count // RINGS
    for c in range(4):
        for i, out_ref in enumerate(out_refs):
            at = c * count + i * size
            out_ref[:, c * width : (c + 1) * width] = merged[at : at + size]
    across = owner_ref[...]
    r = lax.broadcasted_iota(jnp.int32, (count, count), 0)
    s = lax.broadcasted_iota(jnp.int32, (count, count), 1)
    owner = jnp.sum(jnp.where(r == s, across, 0), axis=1, keepdims=True)
    earlier = (across == owner) & (s < r)
    rank = jnp.sum(earlier.astype(jnp.int32), axis=1, keepdims=True)
    slot = (owner * cap + rank).astype(F32).astype(BF16)
    for i, out_ref in enumerate(out_refs):
        out_ref[:, 4 * width :] = jnp.broadcast_to(
            slot[i * size : (i + 1) * size], (size, LANES)
        )


def merge(residual, out_bias, merge_gain, merge_index, owners, parts, cap):
    rows, width = residual.shape
    operands = (
        residual,
        out_bias,
        merge_gain,
        merge_index.reshape(1, rows),
        owners.reshape(1, rows // 4),
        parts[0],
        *map(in_vmem, parts[1:]),
    )
    return pl.pallas_call(
        lambda *refs: merge_kernel(*refs, cap=cap),
        out_shape=(jax.ShapeDtypeStruct((rows // 4 // RINGS, 4 * width + LANES), BF16),) * RINGS,
        in_specs=[pl.BlockSpec(memory_space=pltpu.VMEM)] * len(operands),
        out_specs=(pl.BlockSpec(memory_space=pltpu.VMEM),) * RINGS,
        compiler_params=cparams(),
        cost_estimate=cost(2 * rows * rows * width, 4 << 20),
        name="merge",
    )(*operands)


def embed_kernel(*refs, pieces, cap, slots):
    x_refs = refs[: len(pieces)]
    w_hbm, bias_ref, out_ref, x_sc, w_sc, sems = refs[len(pieces) :]
    depth, cols = w_hbm.shape
    block = depth // 4
    copies = []
    for i in range(4):
        at = pl.ds(i * block, block)
        copies.append(pltpu.make_async_copy(w_hbm.at[at], w_sc.at[at], sems.at[i]))
        copies[-1].start()
    for at, x_ref in zip(pieces, x_refs):
        x_sc[at : at + x_ref.shape[0], :] = x_ref[...]
    embedded = jnp.broadcast_to(bias_ref[...].reshape(1, cols), (x_sc.shape[0], cols))
    for i in range(4):
        copies[i].wait()
        at = slice(i * block, (i + 1) * block)
        embedded = embedded + dot(x_sc[:, at], w_sc[at, :])
    embedded = embedded.astype(BF16)
    total = x_sc.shape[0]
    count = total // 4
    slot = x_sc[:, depth : depth + 1].astype(F32).astype(jnp.int32)
    owner = slot // cap
    rank = slot - owner * cap
    group = lax.axis_index("grp") + lax.broadcasted_iota(jnp.int32, (total, 1), 0) // count
    group = jnp.where(group >= 4, group - 4, group)
    target = owner * slots + group * cap + rank
    lane = lax.broadcasted_iota(jnp.int32, (total, out_ref.shape[0]), 1)
    place = (target == lane).astype(F32).T.astype(BF16)
    out_ref[...] = dot(place, embedded).astype(BF16)


def embed(pieces, w_merge, merge_bias, cap, slots, owners):
    arrays = [in_vmem(array) for _, array in pieces]
    rows = sum(array.shape[0] for array in arrays)
    depth, cols = w_merge.shape
    places = tuple(at for at, _ in pieces)
    return pl.pallas_call(
        lambda *refs: embed_kernel(*refs, pieces=places, cap=cap, slots=slots),
        out_shape=jax.ShapeDtypeStruct((owners * slots, cols), BF16),
        in_specs=[pl.BlockSpec(memory_space=pltpu.VMEM)] * len(arrays)
        + [pl.BlockSpec(memory_space=pl.ANY), pl.BlockSpec(memory_space=pltpu.VMEM)],
        out_specs=pl.BlockSpec(memory_space=pltpu.VMEM),
        scratch_shapes=[
            pltpu.VMEM((rows, arrays[0].shape[1]), BF16),
            pltpu.VMEM((depth, cols), BF16),
            pltpu.SemaphoreType.DMA((4,)),
        ],
        compiler_params=cparams(),
        cost_estimate=cost(2 * rows * depth * cols, 10 << 20),
        name="embed",
    )(*arrays, w_merge, merge_bias)


def flip(value, axis):
    return lax.ppermute(value, axis, [(0, 1), (1, 0)])


def turn(value, axis, by):
    size = lax.axis_size(axis)
    return lax.ppermute(value, axis, [(i, (i + by) % size) for i in range(size)])


def ring_gather(value, axis):
    before = turn(value, axis, 1)
    after = turn(value, axis, -1)
    half = value.shape[0] // 2
    return before, after, turn(before[:half], axis, 1), turn(after[half:], axis, -1)


def pack_kernel(in_ref, bias_ref, out_ref, pack_ref, row_sc, sc, sems, *, shares):
    size = sc.shape[0] // 2
    half = size * shares
    tail = row_sc.shape[0]
    core = lax.axis_index("c")
    first = pl.multiple_of(core * half, half)
    if shares > 1:
        chip = lax.axis_index(CHIPS)
        first = pl.multiple_of(first + chip * size, 16)
    copies = []
    for i, ref in enumerate((in_ref, out_ref)):
        source = ref.at[pl.ds(first, size)]
        copies.append(pltpu.make_async_copy(source, sc.at[pl.ds(i * size, size)], sems.at[i]))
        copies[-1].start()
    width = in_ref.shape[1]
    bias = bias_ref[...].astype(F32).reshape(1, 2 * half)
    bias = jnp.where(core == 0, bias[:, :half], bias[:, half:])
    bias = jnp.broadcast_to(bias, (tail, half))
    if shares > 1:
        bias = pltpu.roll(bias, jnp.where(chip == 0, 0, half - chip * size), 1)
    rest = jnp.zeros((tail, width - half), F32)
    row_sc[...] = jnp.concatenate([bias, rest], axis=1).astype(BF16)
    copies.append(
        pltpu.make_async_copy(row_sc, pack_ref.at[pl.ds(2 * size, tail)], sems.at[2])
    )
    copies[-1].start()
    for i in range(2):
        at = pl.ds(i * size, size)
        copies[i].wait()
        copies.append(pltpu.make_async_copy(sc.at[at], pack_ref.at[at], sems.at[3 + i]))
        copies[-1].start()
    for copy in copies[2:]:
        copy.wait()


def pack(w_in, in_bias, w_out, shares, tail):
    units, width = w_in.shape
    size = units // 2 // shares
    any_space = pl.BlockSpec(memory_space=pl.ANY)
    return pl.pallas_call(
        lambda *refs: pack_kernel(*refs, shares=shares),
        out_shape=jax.ShapeDtypeStruct((2 * size + tail, width), BF16),
        in_specs=[any_space, pl.BlockSpec(memory_space=pltpu.VMEM), any_space],
        out_specs=any_space,
        scratch_shapes=[
            pltpu.VMEM((tail, width), BF16),
            pltpu.VMEM((2 * size, width), BF16),
            pltpu.SemaphoreType.DMA((5,)),
        ],
        compiler_params=cparams(),
        cost_estimate=cost(0, 8 * size * width),
        name="pack",
    )(w_in, in_bias, w_out)


def local(
    tokens,
    seg_ids,
    merge_index,
    owners,
    w_qkv,
    w_attn_out,
    w_in,
    in_bias,
    w_out,
    out_bias,
    merge_gain,
    w_merge,
    merge_bias,
):
    far = turn(pack(w_in, in_bias, w_out, lax.axis_size(CHIPS), EXT), "grp", 2)
    near = pack(w_in, in_bias, w_out, 1, PAD)
    far, near = lax.optimization_barrier((far, near))
    row = [far] + [turn(far, ("xh", "xl"), by) for by in (1, 2, 3)]
    one, two = turn(near, "grp", 1), turn(near, "grp", -1)
    heads = qkv(tokens, seg_ids, w_qkv)
    row, heads = lax.optimization_barrier((row, heads))
    mine = lax.all_to_all(heads, ("y", "xh"), 0, 0, tiled=True)
    row, mine = lax.optimization_barrier((jnp.stack(row), mine))
    below, above = turn(row, "y", 1), turn(row, "y", -1)
    queries, kv = mine[:, : HD + EXT], mine[:, HD:]
    kv_c = flip(kv, "c")
    queries, kv_c = lax.optimization_barrier((queries, kv_c))
    away = flip(queries, "xl")
    acc = attend(queries, [kv])
    away, acc = lax.optimization_barrier((away, acc))
    sent = flip(attend(away, [kv, kv_c], send=True, key_block=1024), "xl")
    acc = attend(queries, [kv_c], acc)
    below, above, acc = lax.optimization_barrier((below, above, acc))
    far_a, far_b = turn(below[:2], "y", 1), turn(above[2:], "y", -1)
    sent, acc = lax.optimization_barrier((sent, acc))
    done = combine(acc, sent)
    attended = lax.all_to_all(done, ("y", "xh"), 0, 0, tiled=True)
    far_a, far_b, attended = lax.optimization_barrier((far_a, far_b, attended))
    far = [row, below, above, far_a, far_b]
    residual, mlp_in = project(attended, tokens, w_attn_out)
    pair = flip(mlp_in, "c")
    own, other = mlp(mlp_in, pair, [near, one, two], far)
    parts = [own, flip(other, "c")]
    owner_count = lax.axis_size(("y", "xh", "xl", "c"))
    cap = 4
    merged = merge(residual, out_bias, merge_gain, merge_index, owners, parts, cap)
    size = merged[0].shape[0]
    count = size * RINGS
    pieces = []
    for i, part in enumerate(merged):
        before, after, far_a, far_b = ring_gather(part, "grp")
        at = i * size
        pieces += [
            (at, part),
            (count + at, after),
            (2 * count + at, far_a),
            (2 * count + at + size // 2, far_b),
            (3 * count + at, before),
        ]
    slots = 4 * cap
    outgoing = embed(pieces, w_merge, merge_bias, cap, slots, owner_count)
    cols = outgoing.shape[1]
    received = lax.all_to_all(outgoing, ("y", "xh", "xl", "c"), 0, 0, tiled=True)
    received = received.reshape(owner_count, 4, cap, cols)
    return received.transpose(1, 0, 2, 3).reshape(4 * owner_count * cap, cols)


def solution(mesh):
    inner = Mesh(mesh.devices.reshape(4, 4, 2, 2, 2), ("grp", "y", "xh", "xl", "c"))
    every = ("grp", "y", "xh", "xl", "c")
    tok = ("y", "xh", "xl", "c")
    placed = (
        P(every, None),
        P(every),
        P(every),
        P(every, None),
        P(),
        P(),
        P("grp", None),
        P("grp"),
        P("grp", None),
        P(),
        P(),
        P(None, "grp"),
        P("grp"),
    )
    return jax.shard_map(
        local, mesh=inner, in_specs=placed, out_specs=P(tok, "grp"), check_vma=False
    )
```
